128 devices in a mesh: pipe: 2 (over core), ctx: 64 (over x, z, y).
Axes of the slice: x: 4, y: 4, z: 4, core: 2. Of those that a mesh axis runs over, the one named last changes fastest.
Arguments:
- saved: bfloat16 [2, 8192, 4096], P('pipe', 'ctx'), may hold values from -6 to 6
- grad_out: bfloat16 [8192, 4096], P('ctx'), may hold values from -6 to 6
- route_blocks: int32 [2, 64, 2], P('pipe', 'ctx'), may hold values from 0 to 31, as said below
- route_dest: int32 [2, 64, 2], P('pipe', 'ctx'), may hold values from -1 to 63, as said below
- gain: float32 [2, 4096], P('pipe'), may hold values from 0.5 to 2
- w_router: bfloat16 [2, 4096], P('pipe'), may hold values from -0.09375 to 0.09375
- w_gate: bfloat16 [2, 14336, 4096], P('pipe', 'ctx'), may hold values from -0.09375 to 0.09375
- w_up: bfloat16 [2, 14336, 4096], P('pipe', 'ctx'), may hold values from -0.09375 to 0.09375
- w_down: bfloat16 [2, 14336, 4096], P('pipe', 'ctx'), may hold values from -0.046875 to 0.046875
Outputs:
- grad_inputs: bfloat16 [2, 8192, 4096], P('pipe', 'ctx')
- grad_gate: float32 [2, 14336, 4096], P('pipe', 'ctx')
- grad_up: float32 [2, 14336, 4096], P('pipe', 'ctx')
- grad_down: float32 [2, 14336, 4096], P('pipe', 'ctx')
- grad_gain: float32 [2, 4096], P('pipe')
- grad_router: float32 [2, 4096], P('pipe')
The draws below stay inside these ranges and needn't reach their ends.
Inputs may be any that keep to these rules, and one draw needn't show every extreme that they name: In each row route_blocks[l, o, :] the 2 entries are distinct block numbers of owner o; only slots whose route_dest entry is not -1 are routed. In each row route_dest[l, o, :] the used slots come first: blocks that owner o works on itself (entry o), then blocks handed to the next owner (entry (o + 1) mod 64), then -1. An owner keeps at most 1 block and hands on at most 1; every device works on exactly 1 block of each layer, so 64 * 1 blocks are routed in each layer; in each layer some owner uses all 2 slots, keeping 1 and handing on 1.
All inputs are finite; a program needn't handle non-finite values.
Results may differ from the reference program's by a relative error of at most 0.007.
Values may be sent and summed in bfloat16 or wider, within the bound.
A program may use at most 128 MiB of HBM per device.

```python
import math
import jax
import jax.numpy as jnp
from jax import lax

D = 4096
FF = 14336
BLOCK = 4
WORK = 1
TOK_DEV = 128
LAYERS = 2
BLK_DEV = 32
MOST = 2
TOKENS = 8192
N_CTX = 64


def draw_route_blocks(key, part):
    row_keys = jax.random.split(jax.random.fold_in(key, 11), LAYERS * N_CTX)

    def one_row(row_key):
        return jax.random.permutation(row_key, BLK_DEV)[:MOST]
    picked = jax.vmap(one_row)(row_keys)
    return picked.reshape(LAYERS, N_CTX, MOST).astype(jnp.int32)


def draw_route_dest(key, part):
    base_key = jax.random.fold_in(key, 23)
    keep_counts = jax.random.randint(jax.random.fold_in(base_key, 1), (LAYERS, N_CTX), 0, WORK + 1).astype(jnp.int32)
    heavy_owner = jax.random.randint(jax.random.fold_in(base_key, 2), (LAYERS, 1), 0, N_CTX).astype(jnp.int32)
    owners = jnp.arange(N_CTX, dtype=jnp.int32)[None, :]
    keep_counts = jnp.where(owners == heavy_owner, WORK, keep_counts)
    keep_counts = jnp.where(owners == (heavy_owner + 1) % N_CTX, 0, keep_counts)
    next_keep = jnp.roll(keep_counts, -1, axis=1)
    totals = keep_counts + WORK - next_keep
    slot_index = jnp.arange(MOST, dtype=jnp.int32)[None, None, :]
    owner_ids = jnp.broadcast_to(owners[:, :, None], (LAYERS, N_CTX, MOST))
    handed = jnp.where(slot_index < totals[:, :, None], (owner_ids + 1) % N_CTX, -1)
    targets = jnp.where(slot_index < keep_counts[:, :, None], owner_ids, handed)
    return targets.astype(jnp.int32)


def levels(key, dims, cuts, smallest, high):
    def one(dim, shards_of):
        heights = jax.random.uniform(jax.random.fold_in(jax.random.fold_in(key, 6), dim), (shards_of,), jnp.float32, smallest / len(cuts), high / len(cuts))
        return jnp.repeat(jnp.exp(heights), dims[dim] // shards_of).reshape((-1,) + (1,) * (len(dims) - dim - 1))

    factor_of = one(*cuts[0])
    for cut in cuts[1:]:
        factor_of = factor_of * one(*cut)
    return factor_of


def gaussian(rng, dims, deviation, limit, shards=(), kind=jnp.bfloat16):
    loudness = levels(rng, dims, shards, -0.22, 0.18) if shards else 1.0
    array = jax.random.normal(rng, dims, jnp.float32) * deviation * loudness
    return jnp.minimum(jnp.maximum(array, -limit), limit).astype(kind)


def setup_inputs(seed: int = 0) -> dict:
    key_of = jax.random.split(jax.random.key(seed), 10)
    saved = gaussian(key_of[0], (LAYERS, TOKENS, D), 1.0, 6.0, ((0, 2), (1, 64)))
    grad_out = gaussian(key_of[1], (TOKENS, D), 1.0, 6.0, ((0, 64),))
    route_blocks = draw_route_blocks(jax.random.fold_in(key_of[9], 71), 0)
    route_dest = draw_route_dest(jax.random.fold_in(key_of[9], 71), 0)
    gain = jnp.clip(jnp.exp(math.log(2.0) - 1.3862944 * jax.random.uniform(key_of[4], (LAYERS, D), jnp.float32) ** levels(key_of[4], (LAYERS, D), ((0, 2),), -0.2, 0.2)), 0.5, 2.0)
    w_router = gaussian(key_of[5], (LAYERS, D), D ** -0.5, 0.09375, ((0, 2),))
    w_gate = gaussian(key_of[6], (LAYERS, FF, D), D ** -0.5, 0.09375, ((0, 2), (1, 64)))
    w_up = gaussian(key_of[7], (LAYERS, FF, D), D ** -0.5, 0.09375, ((0, 2), (1, 64)))
    w_down = gaussian(key_of[8], (LAYERS, FF, D), FF ** -0.5, 0.046875, ((0, 2), (1, 64)))
    return {"saved": saved, "grad_out": grad_out, "route_blocks": route_blocks, "route_dest": route_dest, "gain": gain, "w_router": w_router, "w_gate": w_gate, "w_up": w_up, "w_down": w_down}


EPSILON = 1e-05

def silu_parts(gate_pre):
    sigma = jax.nn.sigmoid(gate_pre)
    return (gate_pre * sigma, sigma * (1.0 + gate_pre * (1.0 - sigma)))

def contract_last(left_side, right_side):
    return lax.dot_general(left_side, right_side, (((1,), (1,)), ((), ())), preferred_element_type=jnp.float32)

def contract_first(left_side, right_side):
    return lax.dot_general(left_side, right_side, (((0,), (0,)), ((), ())), preferred_element_type=jnp.float32)

def layer_backward(inputs, upstream, blocks, targets, gain_row, router_row, gate_weight, up_weight, down_weight):
    owner_ids = jnp.arange(N_CTX, dtype=jnp.int32)[:, None]
    starts = owner_ids * TOK_DEV + blocks.astype(jnp.int32) * BLOCK
    chosen = jnp.nonzero((targets >= 0).reshape(-1), size=N_CTX * WORK)[0].astype(jnp.int32)
    first_rows = starts.reshape(-1)[chosen]
    row_ids = (first_rows[:, None] + jnp.arange(BLOCK, dtype=jnp.int32)[None, :]).reshape(-1)
    picked = inputs[row_ids]
    picked_f = picked.astype(jnp.float32)
    inverse = lax.rsqrt(lax.optimization_barrier(jnp.mean(picked_f * picked_f, axis=1, keepdims=True)) + EPSILON)
    normal_hat = picked_f * inverse
    normed = (normal_hat * gain_row).astype(jnp.bfloat16)
    router_prob = jax.nn.sigmoid(jnp.dot(picked, router_row, preferred_element_type=jnp.float32))
    scaled = (router_prob[:, None] * upstream[row_ids].astype(jnp.float32)).astype(jnp.bfloat16)
    gate_pre = contract_last(normed, gate_weight)
    up_value = contract_last(normed, up_weight)
    activated, slope_term = silu_parts(gate_pre)
    hidden = (activated * up_value).astype(jnp.bfloat16)
    hidden_grad = contract_last(scaled, down_weight)
    row_sums = lax.optimization_barrier(jnp.sum(hidden_grad * hidden.astype(jnp.float32), axis=1))
    grad_down = contract_first(hidden, scaled)
    gate_grad = (hidden_grad * up_value * slope_term).astype(jnp.bfloat16)
    up_grad = (hidden_grad * activated).astype(jnp.bfloat16)
    grad_gate = contract_first(gate_grad, normed)
    grad_up = contract_first(up_grad, normed)
    normed_grad = jnp.dot(gate_grad, gate_weight, preferred_element_type=jnp.float32) + jnp.dot(up_grad, up_weight, preferred_element_type=jnp.float32)
    logit_grad = row_sums * (1.0 - router_prob)
    hat_grad = normed_grad * gain_row
    norm_part = inverse * (hat_grad - normal_hat * lax.optimization_barrier(jnp.mean(hat_grad * normal_hat, axis=1, keepdims=True)))
    row_delta = norm_part + logit_grad[:, None] * router_row.astype(jnp.float32)
    input_grad = upstream.astype(jnp.float32).at[row_ids].add(row_delta).astype(jnp.bfloat16)
    grad_gain = lax.optimization_barrier(jnp.sum(normed_grad * normal_hat, axis=0))
    grad_router = lax.optimization_barrier(jnp.sum(logit_grad[:, None] * picked_f, axis=0))
    return (input_grad, grad_gate, grad_up, grad_down, grad_gain, grad_router)

def reference(saved, grad_out, route_blocks, route_dest, gain, w_router, w_gate, w_up, w_down):
    upstream = grad_out
    results = [None] * LAYERS
    for layer_index in range(LAYERS - 1, -1, -1):
        results[layer_index] = layer_backward(saved[layer_index], upstream, route_blocks[layer_index], route_dest[layer_index], gain[layer_index], w_router[layer_index], w_gate[layer_index], w_up[layer_index], w_down[layer_index])
        upstream = results[layer_index][0]
    stacked = [jnp.stack([results[layer_index][position] for layer_index in range(LAYERS)]) for position in range(6)]
    return (stacked[0], stacked[1], stacked[2], stacked[3], stacked[4], stacked[5])
```

```python
import jax
import jax.numpy as jnp
from jax import lax
from jax.experimental import pallas as pl
from jax.experimental.pallas import tpu as pltpu
from jax.sharding import PartitionSpec as P

BLOCK = 4
EPSILON = 1e-05
RING = 4
OFFS = (1, 2, 3)
QUARTER = 1024
EXTRA = 128
WIDTHS = (384, 384, 384)
FEATS = (384, 384, 256)
STARTS = (0, 384, 768)
ROWS = 16
ORDERS = ((0, 1, 2), (1, 2, 0), (2, 0, 1))
F32 = jnp.float32
BF16 = jnp.bfloat16
MESH = pl.DeviceIdType.MESH


def contract_last(left_side, right_side):
    return lax.dot_general(
        left_side, right_side, (((1,), (1,)), ((), ())), preferred_element_type=F32
    )


def contract_first(left_side, right_side):
    return lax.dot_general(
        left_side, right_side, (((0,), (0,)), ((), ())), preferred_element_type=F32
    )


def hi_lo(value):
    hi = value.astype(BF16).astype(F32)
    return hi, value - hi


def step_kernel(
    bn, up_in, hat_in, gain_in, wr_in, sc, wg_hbm, wu_hbm, wd_hbm,
    go0, go1, go2, so0, so1, so2, hid_o, gg_o, ug_o, nb_o, new_o, st_o,
    up_ref, bs, hn, hs, g0, g1, g2, s0, s1, s2, r0, r1, r2,
    rb00, rb01, rb02, a00, a01, a02, rb10, rb11, rb12, a10, a11, a12, rb20, rb21, rb22,
    u, nb, nbsend, srb, acc, wg, wu, wd,
    hand_send, hand_recv, ag_send, ag_recv, rs_send, rs_recv, st_send, st_recv,
    un_send, un_recv, nb_send, nb_recv, local_sem,
):
    pipe = lax.axis_index("pipe")
    me = lax.axis_index("ctx")
    yy = lax.rem(me, RING)
    quartet = lax.div(me, RING)
    zz = lax.rem(quartet, RING)
    xx = lax.div(quartet, RING)
    at = (yy, xx, zz)
    quartets = RING * RING
    next_base = lax.rem(quartet + 1, quartets) * RING
    prev_last = lax.rem(quartet + quartets - 1, quartets) * RING + RING - 1

    def ring_index(dim, off):
        return lax.rem(at[dim] + RING - off, RING)

    def peer(dim, off):
        pos = list(at)
        pos[dim] = ring_index(dim, off)
        return {"pipe": pipe, "ctx": pos[1] * 16 + pos[2] * 4 + pos[0]}

    def same_pipe(ctx):
        return {"pipe": pipe, "ctx": ctx}

    partner = {"pipe": 1 - pipe, "ctx": me}

    def remote(src, dst, send, recv, device):
        return pltpu.make_async_remote_copy(
            src_ref=src, dst_ref=dst, send_sem=send, recv_sem=recv,
            device_id=device, device_id_type=MESH,
        )

    gs, ss, rs = (g0, g1, g2), (s0, s1, s2), (r0, r1, r2)
    rb0, a0 = (rb00, rb01, rb02), (a00, a01, a02)
    rb1, a1 = (rb10, rb11, rb12), (a10, a11, a12)
    rb2 = (rb20, rb21, rb22)

    weight_copies = [
        pltpu.make_async_copy(src, dst, local_sem.at[i])
        for i, (src, dst) in enumerate(((wg_hbm, wg), (wu_hbm, wu), (wd_hbm, wd)))
    ]
    for copy in weight_copies:
        copy.start()

    barrier = pltpu.get_barrier_semaphore()

    def greet(device):
        pl.semaphore_signal(barrier, inc=1, device_id=device, device_id_type=MESH)

    for dim in range(3):
        for off in OFFS:
            greet(peer(dim, off))
    greet(partner)
    greet(same_pipe(prev_last))

    @pl.when(yy == RING - 1)
    def _():
        for j in range(RING):
            greet(same_pipe(next_base + j))

    pl.semaphore_wait(barrier, 11 + RING * lax.div(yy, RING - 1))

    def hand_copies(src, dst, which):
        return [
            remote(
                src.at[ring_index(0, off)], dst.at[yy + 1],
                hand_send.at[which, off], hand_recv.at[which, off], peer(0, off),
            )
            for off in OFFS
        ]

    def hand_over_copy(src, dst, which, j):
        return remote(
            src.at[j], dst.at[0],
            hand_send.at[which, RING + j], hand_recv.at[which, 0], same_pipe(next_base + j),
        )

    def hand_start(src, dst, which):
        for copy in hand_copies(src, dst, which):
            copy.start()

        @pl.when(yy == RING - 1)
        def _():
            for j in range(RING):
                hand_over_copy(src, dst, which, j).start()

        dst[yy + 1] = src[yy]

    def hand_wait(src, dst, which):
        for copy in hand_copies(src, dst, which):
            copy.wait()
        hand_over_copy(src, dst, which, 0).wait_recv()

        @pl.when(yy == RING - 1)
        def _():
            for j in range(RING):
                hand_over_copy(src, dst, which, j).wait_send()

    def make_tile(held, bufs, widths):
        for k in range(3):
            cols = slice(STARTS[k], STARTS[k] + widths[k])
            b = [held[i, :, cols].astype(F32) for i in range(5)]
            low = lax.broadcasted_iota(jnp.int32, b[0].shape, 0) < BLOCK
            turned = [pltpu.roll(b[i], BLOCK, 0) for i in (0, 2, 4)]
            top = b[1] + jnp.where(low, turned[0], turned[1])
            bottom = b[3] + jnp.where(low, turned[1], turned[2])
            bufs[k][yy, xx, zz] = jnp.concatenate([top, bottom], axis=0).astype(BF16)

    def ag_copies(bufs, which, k, stage):
        dim = ORDERS[k][stage]
        index = tuple(
            slice(None) if d in ORDERS[k][:stage] else at[d] for d in range(3)
        )
        return [
            remote(
                bufs[k].at[index], bufs[k].at[index],
                ag_send.at[which, k, stage, off], ag_recv.at[which, k, stage, off],
                peer(dim, off),
            )
            for off in OFFS
        ]

    def ag_start(bufs, which, k, stage):
        for copy in ag_copies(bufs, which, k, stage):
            copy.start()

    def ag_recv_wait(bufs, which, k, stage):
        for copy in ag_copies(bufs, which, k, stage):
            copy.wait_recv()

    def ag_send_wait(bufs, which):
        for k in range(3):
            for stage in range(3):
                for copy in ag_copies(bufs, which, k, stage):
                    copy.wait_send()

    def make_scaled():
        for q in range(RING):
            bs[q] = (sc[1][:, 0:1] * up_ref[q]).astype(BF16)

    @pl.when(pipe == 1)
    def _():
        up_ref[...] = up_in[...]
        make_scaled()

    hand_start(bn, hn, 0)

    @pl.when(pipe == 1)
    def _():
        hand_start(bs, hs, 1)

    hand_wait(bn, hn, 0)
    make_tile(hn, gs, WIDTHS)
    for k in range(3):
        ag_start(gs, 0, k, 0)

    @pl.when(pipe == 1)
    def _():
        hand_wait(bs, hs, 1)
        make_tile(hs, ss, FEATS)
        for k in range(3):
            ag_start(ss, 1, k, 0)

    for stage in (1, 2):
        for k in range(3):
            ag_recv_wait(gs, 0, k, stage - 1)
            ag_start(gs, 0, k, stage)

        @pl.when(pipe == 1)
        def _(stage=stage):
            for k in range(3):
                ag_recv_wait(ss, 1, k, stage - 1)
                ag_start(ss, 1, k, stage)

    for copy in weight_copies:
        copy.wait()

    def rows_of(bufs, k, q):
        return bufs[k][q, :, :, :, : FEATS[k]].reshape(quartets * ROWS, FEATS[k])

    def columns(k, q):
        return slice(q * QUARTER + STARTS[k], q * QUARTER + STARTS[k] + FEATS[k])

    gathered_out = [
        pltpu.make_async_copy(src, dst, local_sem.at[3 + i])
        for i, (src, dst) in enumerate(zip(gs + ss, (go0, go1, go2, so0, so1, so2)))
    ]

    for k in range(3):
        ag_recv_wait(gs, 0, k, 2)
        gathered_out[k].start()
        gate_sum = None
        up_sum = None
        for q in range(RING):
            rows = rows_of(gs, k, q)
            gate_part = contract_last(rows, wg[:, columns(k, q)])
            up_part = contract_last(rows, wu[:, columns(k, q)])
            gate_sum = gate_part if gate_sum is None else gate_sum + gate_part
            up_sum = up_part if up_sum is None else up_sum + up_part
        if k == 0:
            acc[0] = gate_sum
            acc[1] = up_sum
        else:
            acc[0] += gate_sum
            acc[1] += up_sum

    def nb_copy():
        return remote(nbsend, nb, nb_send, nb_recv, partner)

    @pl.when(pipe == 0)
    def _():
        nb_copy().wait_recv()
        low = lax.broadcasted_iota(jnp.int32, (2 * BLOCK, 1), 0) < BLOCK
        mine = sc[4][:, 0:1]
        same = 1.0 - jnp.minimum(jnp.abs(nb[0, :, QUARTER : QUARTER + 1].astype(F32) - mine), 1.0)
        other = pltpu.roll(nb[0, :, QUARTER:].astype(F32), BLOCK, 0)[:, 0:1]
        cross = 1.0 - jnp.minimum(jnp.abs(other - mine), 1.0)
        for q in range(RING):
            rows = nb[q, :, :QUARTER].astype(F32)
            turned = pltpu.roll(rows, BLOCK, 0)
            kept_rows = (1.0 - same - cross) * up_in[q]
            up_ref[q] = same * rows + cross * turned + kept_rows
        make_scaled()
        hand_start(bs, hs, 1)
        hand_wait(bs, hs, 1)
        make_tile(hs, ss, FEATS)
        for k in range(3):
            ag_start(ss, 1, k, 0)
        for stage in (1, 2):
            for k in range(3):
                ag_recv_wait(ss, 1, k, stage - 1)
                ag_start(ss, 1, k, stage)

    for k in range(3):
        ag_recv_wait(ss, 1, k, 2)
        gathered_out[3 + k].start()
        grad_sum = None
        for q in range(RING):
            part = contract_last(rows_of(ss, k, q), wd[:, columns(k, q)])
            grad_sum = part if grad_sum is None else grad_sum + part
        if k == 0:
            acc[2] = grad_sum
        else:
            acc[2] += grad_sum

    gate_pre = acc[0]
    up_value = acc[1]
    hidden_grad = acc[2]
    sigma = jax.nn.sigmoid(gate_pre)
    activated = gate_pre * sigma
    slope = sigma * (1.0 + gate_pre * (1.0 - sigma))
    hidden = (activated * up_value).astype(BF16)
    hid_o[...] = hidden
    row_part = jnp.sum(hidden_grad * hidden.astype(F32), axis=1, keepdims=True)
    gg_o[...] = (hidden_grad * up_value * slope).astype(BF16)
    ug_o[...] = (hidden_grad * activated).astype(BF16)
    extra = g2[0, :, :, :, FEATS[2] :].reshape(quartets * ROWS, EXTRA).astype(F32)
    weight = row_part * jnp.sum(extra, axis=1, keepdims=True)
    row_hi, row_lo = hi_lo(row_part)
    lane = lax.broadcasted_iota(jnp.int32, (quartets * ROWS, EXTRA), 1)
    row_lanes = jnp.where(lane == 0, row_hi, jnp.where(lane == 1, row_lo, 0.0)).astype(BF16)

    def rs_copies(k, stage):
        order = ORDERS[k]
        dim = order[stage]
        src = (rs, a0, a1)[stage][k]
        dst = (rb0, rb1, rb2)[stage][k]
        left = [d for d in range(3) if d not in order[:stage]]
        copies = []
        for off in OFFS:
            index = tuple(ring_index(d, off) if d == dim else slice(None) for d in left)
            copies.append(
                remote(
                    src.at[index], dst.at[off - 1],
                    rs_send.at[k, stage, off], rs_recv.at[k, stage, off], peer(dim, off),
                )
            )
        return copies

    def rs_start(k, stage):
        for copy in rs_copies(k, stage):
            copy.start()

    def rs_sum(k, stage):
        for copy in rs_copies(k, stage):
            copy.wait_recv()
        order = ORDERS[k]
        dim = order[stage]
        src = (rs, a0, a1)[stage][k]
        got = (rb0, rb1, rb2)[stage][k]
        left = [d for d in range(3) if d not in order[:stage]]
        index = tuple(at[d] if d == dim else slice(None) for d in left)
        return (src[index].astype(F32) + got[0].astype(F32)) + (
            got[1].astype(F32) + got[2].astype(F32)
        )

    srb[0, yy] = jnp.zeros((2 * RING, QUARTER + EXTRA), F32)
    gg = gg_o[...]
    ug = ug_o[...]
    for k in range(3):
        for q in range(RING):
            part = jnp.dot(gg, wg[:, columns(k, q)], preferred_element_type=F32) + jnp.dot(
                ug, wu[:, columns(k, q)], preferred_element_type=F32
            )
            shape = (RING, RING, ROWS, FEATS[k])
            rs[k][q, :, :, :, : FEATS[k]] = part.astype(BF16).reshape(shape)
            if k == 2:
                rs[k][q, :, :, :, FEATS[k] :] = row_lanes.reshape(RING, RING, ROWS, EXTRA)
            rows = rows_of(gs, k, q).astype(F32)
            cols = slice(STARTS[k], STARTS[k] + FEATS[k])
            srb[0, yy, 2 * q : 2 * q + 1, cols] = jnp.sum(part * rows, axis=0, keepdims=True)
            srb[0, yy, 2 * q + 1 : 2 * q + 2, cols] = jnp.sum(
                weight * rows, axis=0, keepdims=True
            )
        rs_start(k, 0)

    def st_copies(stage):
        here = srb.at[stage, at[stage]]
        return [
            remote(
                here, here, st_send.at[stage, off], st_recv.at[stage, off], peer(stage, off)
            )
            for off in OFFS
        ]

    def st_sum(stage):
        for copy in st_copies(stage):
            copy.wait()
        return (srb[stage, 0] + srb[stage, 1]) + (srb[stage, 2] + srb[stage, 3])

    for copy in st_copies(0):
        copy.start()
    for stage in (0, 1):
        for k in range(3):
            (a0, a1)[stage][k][...] = rs_sum(k, stage)
            rs_start(k, stage + 1)
        srb[stage + 1, at[stage + 1]] = st_sum(stage)
        for copy in st_copies(stage + 1):
            copy.start()
    for k in range(3):
        u[yy, 0:ROWS, STARTS[k] : STARTS[k] + WIDTHS[k]] = rs_sum(k, 2)

    def back_copies():
        return [
            remote(
                u.at[yy, pl.ds(0, ROWS)], u.at[yy, pl.ds(0, ROWS)],
                un_send.at[off], un_recv.at[off], peer(0, off),
            )
            for off in OFFS
        ]

    def back_over_copy(q):
        return remote(
            u.at[yy, pl.ds(0, 8)], u.at[yy, pl.ds(ROWS, 8)],
            un_send.at[0], un_recv.at[RING + q], same_pipe(prev_last),
        )

    def back_over_wait(q):
        return remote(
            u.at[q, pl.ds(0, 8)], u.at[q, pl.ds(ROWS, 8)],
            un_send.at[0], un_recv.at[RING + q], same_pipe(prev_last),
        )

    for copy in back_copies():
        copy.start()
    back_over_copy(yy).start()
    for copy in back_copies():
        copy.wait_recv()

    @pl.when(yy == RING - 1)
    def _():
        for q in range(RING):
            back_over_wait(q).wait_recv()

    first = pl.multiple_of(lax.div(yy, 2) * 8, 8)
    odd = lax.rem(yy, 2) == 1

    def owned(q, cols):
        a = u[q, pl.ds(first, 8), cols]
        b = u[q, pl.ds(first + 8, 8), cols]
        low = lax.broadcasted_iota(jnp.int32, a.shape, 0) < BLOCK
        turned = jnp.where(low, pltpu.roll(a, BLOCK, 0), pltpu.roll(b, BLOCK, 0))
        return jnp.where(odd, turned, a)

    feats = slice(0, QUARTER)
    total = jnp.zeros((2 * BLOCK, 1), F32)
    for q in range(RING):
        hat_grad = owned(q, feats) * gain_in[q]
        total = total + jnp.sum(hat_grad * hat_in[q], axis=1, keepdims=True)
    mean = total / float(RING * QUARTER)
    row_sum = jnp.sum(owned(0, slice(QUARTER, QUARTER + EXTRA)), axis=1, keepdims=True)
    logit_grad = row_sum * sc[2][:, 0:1]
    inverse = sc[3][:, 0:1]
    for q in range(RING):
        hat_grad = owned(q, feats) * gain_in[q]
        delta = inverse * (hat_grad - hat_in[q] * mean) + logit_grad * wr_in[q]
        fresh = (up_ref[q] + delta).astype(BF16)
        nbsend[q, :, :QUARTER] = fresh
        nbsend[q, :, QUARTER:] = sc[4].astype(BF16)
        new_o[q] = fresh

    @pl.when(pipe == 1)
    def _():
        nb_copy().start()
        nb_o[...] = nbsend[...]

    @pl.when(pipe == 0)
    def _():
        nb_o[...] = nb[...]

    st_o[...] = st_sum(2)

    ag_send_wait(gs, 0)
    ag_send_wait(ss, 1)
    for k in range(3):
        for stage in range(3):
            for copy in rs_copies(k, stage):
                copy.wait_send()
    for copy in back_copies():
        copy.wait_send()
    back_over_copy(yy).wait_send()

    @pl.when(pipe == 1)
    def _():
        nb_copy().wait_send()

    for copy in gathered_out:
        copy.wait()


def communicate(bn, up, hat, gain, wr, sc, wg, wu, wd):
    ff = wg.shape[0]
    rows = RING * RING * ROWS
    width = QUARTER + EXTRA
    vmem = pl.BlockSpec(memory_space=pltpu.VMEM)
    hbm = pl.BlockSpec(memory_space=pl.ANY)
    cube = (RING, RING, RING, ROWS)
    shape = jax.ShapeDtypeStruct
    out_shape = (
        [shape(cube + (w,), BF16) for w in WIDTHS]
        + [shape(cube + (w,), BF16) for w in FEATS]
        + [shape((rows, ff), BF16)] * 3
        + [shape((RING, 8, width), BF16), shape((RING, 8, QUARTER), BF16)]
        + [shape((8, width), F32)]
    )
    dma = pltpu.SemaphoreType.DMA
    scratch = (
        [pltpu.VMEM((RING, 8, QUARTER), F32), pltpu.VMEM((RING, 8, QUARTER), BF16)]
        + [pltpu.VMEM((5, 8, width), BF16), pltpu.VMEM((5, 8, QUARTER), BF16)]
        + [pltpu.VMEM(cube + (w,), BF16) for w in WIDTHS]
        + [pltpu.VMEM(cube + (w,), BF16) for w in FEATS]
        + [pltpu.VMEM(cube + (w,), BF16) for w in WIDTHS]
        + [pltpu.VMEM((3, RING, RING, ROWS, w), BF16) for w in WIDTHS]
        + [pltpu.VMEM((RING, RING, ROWS, w), F32) for w in WIDTHS]
        + [pltpu.VMEM((3, RING, ROWS, w), F32) for w in WIDTHS]
        + [pltpu.VMEM((RING, ROWS, w), F32) for w in WIDTHS]
        + [pltpu.VMEM((3, ROWS, w), F32) for w in WIDTHS]
        + [pltpu.VMEM((RING, ROWS + 8, width), F32)]
        + [pltpu.VMEM((RING, 8, width), BF16)] * 2
        + [pltpu.VMEM((3, RING, 8, width), F32)]
        + [pltpu.VMEM((3, rows, ff), F32)]
        + [pltpu.VMEM(wg.shape, BF16)] * 3
        + [dma((2, 8)), dma((2, 4))]
        + [dma((2, 3, 3, 4)), dma((2, 3, 3, 4))]
        + [dma((3, 3, 4)), dma((3, 3, 4))]
        + [dma((3, 4)), dma((3, 4))]
        + [dma((4,)), dma((8,))]
        + [dma, dma]
        + [dma((9,))]
    )
    return pl.pallas_call(
        step_kernel,
        out_shape=out_shape,
        in_specs=[vmem] * 6 + [hbm] * 3,
        out_specs=[hbm] * 6 + [vmem] * 6,
        scratch_shapes=scratch,
        compiler_params=pltpu.CompilerParams(
            collective_id=0, has_side_effects=True, vmem_limit_bytes=56 * 1024 * 1024
        ),
        name="routed_step",
    )(bn, up, hat, gain, wr, sc, wg, wu, wd)


def weight_kernel(hid, gg, ug, g0, g1, g2, s0, s1, s2, out_gate, out_up, out_down):
    rows = hid.shape[0]
    for k, (g, s) in enumerate(zip((g0, g1, g2), (s0, s1, s2))):
        cols = slice(STARTS[k], STARTS[k] + FEATS[k])
        normed = g[0, :, :, :, : FEATS[k]].reshape(rows, FEATS[k])
        scaled = s[0].reshape(rows, FEATS[k])
        out_gate[:, cols] = contract_first(gg[...], normed)
        out_up[:, cols] = contract_first(ug[...], normed)
        out_down[:, cols] = contract_first(hid[...], scaled)


def weight_grads(hid, gg, ug, gathered, ff, model_dim):
    small = pl.BlockSpec(hid.shape, lambda q: (0, 0))

    def part(width):
        return pl.BlockSpec((1, RING, RING, ROWS, width), lambda q: (q, 0, 0, 0, 0))

    out = pl.BlockSpec((ff, QUARTER), lambda q: (0, q))
    return pl.pallas_call(
        weight_kernel,
        grid=(RING,),
        out_shape=[jax.ShapeDtypeStruct((ff, model_dim), F32)] * 3,
        in_specs=[small] * 3 + [part(w) for w in WIDTHS + FEATS],
        out_specs=[out] * 3,
        compiler_params=pltpu.CompilerParams(vmem_limit_bytes=40 * 1024 * 1024),
        name="weight_grads",
    )(hid, gg, ug, *gathered)


def quarters(rows):
    count = rows.shape[0]
    return rows.reshape(count, RING, QUARTER).transpose(1, 0, 2)


def on_device(saved, grad_out, route_blocks, route_dest, gain, w_router, w_gate, w_up, w_down):
    me = lax.axis_index("ctx")
    tokens = saved[0]
    tok_rows, model_dim = tokens.shape
    block_count = tok_rows // BLOCK
    blocks = route_blocks[0, 0]
    targets = route_dest[0, 0]
    kept = targets[0] == me
    keep_block = jnp.where(kept, blocks[0], blocks[1])
    hand_block = jnp.where(kept, blocks[1], blocks[0])
    handed = jnp.where(kept, targets[1] >= 0, targets[0] >= 0)

    def pick(array):
        by_block = array.reshape(block_count, BLOCK, model_dim)
        return jnp.concatenate(
            [
                lax.dynamic_index_in_dim(by_block, keep_block, 0, keepdims=False),
                lax.dynamic_index_in_dim(by_block, hand_block, 0, keepdims=False),
            ],
            axis=0,
        )

    first = jnp.arange(2 * BLOCK)[:, None] < BLOCK
    mask = jnp.where(first, kept, handed).astype(F32)
    block_id = jnp.where(first, keep_block, hand_block).astype(F32)
    gain_row = gain[0]
    router_row = w_router[0].astype(F32)
    picked = pick(tokens).astype(F32)
    inverse = lax.rsqrt(jnp.mean(picked * picked, axis=1, keepdims=True) + EPSILON)
    hat = picked * inverse
    router = jax.nn.sigmoid(jnp.sum(picked * router_row, axis=1, keepdims=True))
    normed = (hat * gain_row * mask).astype(BF16)
    carried = (1.0 - router) * mask / inverse
    carried_hi = lax.reduce_precision(carried, 8, 7)
    carried_lo = carried - carried_hi
    lane = jnp.arange(EXTRA)[None, :]
    extra = jnp.where(lane == 0, carried_hi, jnp.where(lane == 1, carried_lo, 0.0)).astype(BF16)
    bn = jnp.concatenate(
        [quarters(normed), jnp.broadcast_to(extra[None], (RING,) + extra.shape)], axis=2
    )
    scalars = jnp.stack(
        [inverse, router * mask, (1.0 - router) * mask, inverse * mask, block_id]
    )
    scalars = jnp.broadcast_to(scalars, scalars.shape[:2] + (EXTRA,))
    upstream = quarters(pick(grad_out).astype(F32))
    results = communicate(
        bn,
        upstream,
        quarters(hat),
        quarters(gain_row[None]),
        quarters(router_row[None]),
        scalars,
        w_gate[0],
        w_up[0],
        w_down[0],
    )
    gathered = results[:6]
    hid, gg, ug, nb, fresh, stats = results[6:]
    grads = weight_grads(hid, gg, ug, gathered, w_gate.shape[1], model_dim)

    def whole(rows):
        return rows[:, :, :QUARTER].transpose(1, 0, 2).reshape(2, BLOCK, model_dim)

    above = whole(nb)
    above_ids = nb[0, :: BLOCK, QUARTER].astype(jnp.int32)
    own = whole(fresh)
    ids = jnp.arange(block_count, dtype=jnp.int32)[:, None, None]
    outcome = grad_out.reshape(block_count, BLOCK, model_dim)
    for rows, where in (
        (above[0], above_ids[0]),
        (above[1], above_ids[1]),
        (own[0], keep_block),
        (own[1], hand_block),
    ):
        outcome = jnp.where(ids == where, rows[None], outcome)
    by_row = stats[:, :QUARTER].reshape(RING, 2, QUARTER)
    stat_gain = by_row[:, 0].reshape(model_dim) / gain_row
    stat_router = by_row[:, 1].reshape(model_dim) / gain_row
    return (
        outcome.reshape(tok_rows, model_dim)[None],
        grads[0][None],
        grads[1][None],
        grads[2][None],
        stat_gain[None],
        stat_router[None],
    )


def solution(mesh):
    in_specs = (
        P("pipe", "ctx", None),
        P("ctx", None),
        P("pipe", "ctx", None),
        P("pipe", "ctx", None),
        P("pipe", None),
        P("pipe", None),
        P("pipe", "ctx", None),
        P("pipe", "ctx", None),
        P("pipe", "ctx", None),
    )
    out_specs = (
        P("pipe", "ctx", None),
        P("pipe", "ctx", None),
        P("pipe", "ctx", None),
        P("pipe", "ctx", None),
        P("pipe", None),
        P("pipe", None),
    )
    return jax.shard_map(
        on_device, mesh=mesh, in_specs=in_specs, out_specs=out_specs, check_vma=False
    )
```

```python
import jax
import jax.numpy as jnp
from jax import lax
from jax.experimental import pallas as pl
from jax.experimental.pallas import tpu as pltpu
from jax.sharding import PartitionSpec as P

BLOCK = 4
EPSILON = 1e-05
RING = 4
OFFS = (1, 2, 3)
QUARTER = 1024
EXTRA = 128
WIDTHS = (384, 384, 384)
FEATS = (384, 384, 256)
STARTS = (0, 384, 768)
ROWS = 16
ORDERS = ((0, 1, 2), (1, 2, 0), (2, 0, 1))
F32 = jnp.float32
BF16 = jnp.bfloat16
MESH = pl.DeviceIdType.MESH


def contract_last(left_side, right_side):
    return lax.dot_general(
        left_side, right_side, (((1,), (1,)), ((), ())), preferred_element_type=F32
    )


def contract_first(left_side, right_side):
    return lax.dot_general(
        left_side, right_side, (((0,), (0,)), ((), ())), preferred_element_type=F32
    )


def hi_lo(value):
    hi = value.astype(BF16).astype(F32)
    return hi, value - hi


def step_kernel(
    blocks, targets, saved_hbm, grad_hbm, gain_hbm, router_hbm, wg_hbm, wu_hbm, wd_hbm,
    go0, go1, go2, so0, so1, so2, hid_o, gg_o, ug_o, nb_o, new_o, st_o,
    saved, grad_out, gain, router_row, hat_ref, up_ref, sc, bn,
    bs, hn, hs, g0, g1, g2, s0, s1, s2, r0, r1, r2,
    rb00, rb01, rb02, a00, a01, a02, rb10, rb11, rb12, a10, a11, a12, rb20, rb21, rb22,
    u, nb, srb, acc, wg, wu, wd,
    hand_send, hand_recv, ag_send, ag_recv, rs_send, rs_recv, st_send, st_recv,
    un_send, un_recv, nb_send, nb_recv, local_sem,
):
    pipe = lax.axis_index("pipe")
    me = lax.axis_index("ctx")
    yy = lax.rem(me, RING)
    quartet = lax.div(me, RING)
    zz = lax.rem(quartet, RING)
    xx = lax.div(quartet, RING)
    at = (yy, xx, zz)
    quartets = RING * RING
    next_base = lax.rem(quartet + 1, quartets) * RING
    prev_last = lax.rem(quartet + quartets - 1, quartets) * RING + RING - 1

    def ring_index(dim, off):
        return lax.rem(at[dim] + RING - off, RING)

    def peer(dim, off):
        pos = list(at)
        pos[dim] = ring_index(dim, off)
        return {"pipe": pipe, "ctx": pos[1] * 16 + pos[2] * 4 + pos[0]}

    def same_pipe(ctx):
        return {"pipe": pipe, "ctx": ctx}

    partner = {"pipe": 1 - pipe, "ctx": me}

    def remote(src, dst, send, recv, device):
        return pltpu.make_async_remote_copy(
            src_ref=src, dst_ref=dst, send_sem=send, recv_sem=recv,
            device_id=device, device_id_type=MESH,
        )

    gs, ss, rs = (g0, g1, g2), (s0, s1, s2), (r0, r1, r2)
    rb0, a0 = (rb00, rb01, rb02), (a00, a01, a02)
    rb1, a1 = (rb10, rb11, rb12), (a10, a11, a12)
    rb2 = (rb20, rb21, rb22)

    row_copies = [
        pltpu.make_async_copy(src, dst, local_sem.at[9 + i])
        for i, (src, dst) in enumerate(
            (
                (saved_hbm.at[0], saved),
                (gain_hbm, gain),
                (router_hbm, router_row),
                (grad_hbm, grad_out),
            )
        )
    ]
    weight_copies = [
        pltpu.make_async_copy(src.at[0], dst, local_sem.at[i])
        for i, (src, dst) in enumerate(((wg_hbm, wg), (wu_hbm, wu), (wd_hbm, wd)))
    ]
    for copy in row_copies + weight_copies:
        copy.start()

    barrier = pltpu.get_barrier_semaphore()

    def greet(device):
        pl.semaphore_signal(barrier, inc=1, device_id=device, device_id_type=MESH)

    for dim in range(3):
        for off in OFFS:
            greet(peer(dim, off))
    greet(partner)
    greet(same_pipe(prev_last))

    @pl.when(yy == RING - 1)
    def _():
        for j in range(RING):
            greet(same_pipe(next_base + j))

    kept = targets[0, 0, 0] == me
    keep_block = jnp.where(kept, blocks[0, 0, 0], blocks[0, 0, 1])
    hand_block = jnp.where(kept, blocks[0, 0, 1], blocks[0, 0, 0])
    handed = jnp.where(kept, targets[0, 0, 1], targets[0, 0, 0]) >= 0
    first_rows = lax.broadcasted_iota(jnp.int32, (2 * BLOCK, 1), 0) < BLOCK
    mask = jnp.where(
        first_rows, jnp.where(kept, 1.0, 0.0).astype(F32), jnp.where(handed, 1.0, 0.0).astype(F32)
    )

    block_id = jnp.where(first_rows, keep_block, hand_block)
    row_in_block = lax.rem(lax.broadcasted_iota(jnp.int32, (2 * BLOCK, 1), 0), BLOCK)
    tokens = lax.broadcasted_iota(jnp.int32, (2 * BLOCK, saved.shape[0]), 1)
    chosen = jnp.where(tokens == block_id * BLOCK + row_in_block, 1.0, 0.0).astype(BF16)

    def pick(array, cols):
        return jnp.dot(chosen, array[:, cols], preferred_element_type=F32)

    def quarter(q):
        return slice(q * QUARTER, (q + 1) * QUARTER)

    for copy in row_copies[:3]:
        copy.wait()
    squares = jnp.zeros((2 * BLOCK, 1), F32)
    logits = jnp.zeros((2 * BLOCK, 1), F32)
    for q in range(RING):
        rows = pick(saved, quarter(q))
        hat_ref[q] = rows
        squares += jnp.sum(rows * rows, axis=1, keepdims=True)
        logits += jnp.sum(rows * router_row[:, quarter(q)].astype(F32), axis=1, keepdims=True)
    inverse = lax.rsqrt(squares / float(RING * QUARTER) + EPSILON)
    router = jax.nn.sigmoid(logits)
    rest = (1.0 - router) * mask
    carried_hi, carried_lo = hi_lo(rest / inverse)
    lane = lax.broadcasted_iota(jnp.int32, (2 * BLOCK, EXTRA), 1)
    extra = jnp.where(lane == 0, carried_hi, jnp.where(lane == 1, carried_lo, 0.0)).astype(BF16)
    for q in range(RING):
        hat = hat_ref[q] * inverse
        hat_ref[q] = hat
        bn[q, :, :QUARTER] = (hat * gain[:, quarter(q)] * mask).astype(BF16)
        bn[q, :, QUARTER:] = extra
    for i, value in enumerate((router * mask, rest, inverse * mask, block_id.astype(F32))):
        sc[i] = jnp.broadcast_to(value, (2 * BLOCK, EXTRA))
    row_copies[3].wait()
    for q in range(RING):
        up_ref[q] = pick(grad_out, quarter(q))

    pl.semaphore_wait(barrier, 11 + RING * lax.div(yy, RING - 1))

    def hand_copies(src, dst, which):
        return [
            remote(
                src.at[ring_index(0, off)], dst.at[yy + 1],
                hand_send.at[which, off], hand_recv.at[which, off], peer(0, off),
            )
            for off in OFFS
        ]

    def hand_over_copy(src, dst, which, j):
        return remote(
            src.at[j], dst.at[0],
            hand_send.at[which, RING + j], hand_recv.at[which, 0], same_pipe(next_base + j),
        )

    def hand_start(src, dst, which):
        for copy in hand_copies(src, dst, which):
            copy.start()

        @pl.when(yy == RING - 1)
        def _():
            for j in range(RING):
                hand_over_copy(src, dst, which, j).start()

        dst[yy + 1] = src[yy]

    def hand_wait(src, dst, which):
        for copy in hand_copies(src, dst, which):
            copy.wait()
        hand_over_copy(src, dst, which, 0).wait_recv()

        @pl.when(yy == RING - 1)
        def _():
            for j in range(RING):
                hand_over_copy(src, dst, which, j).wait_send()

    def make_tile(held, bufs, widths):
        for k in range(3):
            cols = slice(STARTS[k], STARTS[k] + widths[k])
            b = [held[i, :, cols].astype(F32) for i in range(5)]
            low = lax.broadcasted_iota(jnp.int32, b[0].shape, 0) < BLOCK
            turned = [pltpu.roll(b[i], BLOCK, 0) for i in (0, 2, 4)]
            top = b[1] + jnp.where(low, turned[0], turned[1])
            bottom = b[3] + jnp.where(low, turned[1], turned[2])
            bufs[k][yy, xx, zz] = jnp.concatenate([top, bottom], axis=0).astype(BF16)

    def ag_copies(bufs, which, k, stage):
        dim = ORDERS[k][stage]
        index = tuple(
            slice(None) if d in ORDERS[k][:stage] else at[d] for d in range(3)
        )
        return [
            remote(
                bufs[k].at[index], bufs[k].at[index],
                ag_send.at[which, k, stage, off], ag_recv.at[which, k, stage, off],
                peer(dim, off),
            )
            for off in OFFS
        ]

    def ag_start(bufs, which, k, stage):
        for copy in ag_copies(bufs, which, k, stage):
            copy.start()

    def ag_recv_wait(bufs, which, k, stage):
        for copy in ag_copies(bufs, which, k, stage):
            copy.wait_recv()

    def ag_send_wait(bufs, which):
        for k in range(3):
            for stage in range(3):
                for copy in ag_copies(bufs, which, k, stage):
                    copy.wait_send()

    def make_scaled():
        for q in range(RING):
            bs[q] = (sc[0][:, 0:1] * up_ref[q]).astype(BF16)

    @pl.when(pipe == 1)
    def _():
        make_scaled()

    hand_start(bn, hn, 0)

    @pl.when(pipe == 1)
    def _():
        hand_start(bs, hs, 1)

    hand_wait(bn, hn, 0)
    make_tile(hn, gs, WIDTHS)
    for k in range(3):
        ag_start(gs, 0, k, 0)

    @pl.when(pipe == 1)
    def _():
        hand_wait(bs, hs, 1)
        make_tile(hs, ss, FEATS)
        for k in range(3):
            ag_start(ss, 1, k, 0)

    for stage in (1, 2):
        for k in range(3):
            ag_recv_wait(gs, 0, k, stage - 1)
            ag_start(gs, 0, k, stage)

        @pl.when(pipe == 1)
        def _(stage=stage):
            for k in range(3):
                ag_recv_wait(ss, 1, k, stage - 1)
                ag_start(ss, 1, k, stage)

    for copy in weight_copies:
        copy.wait()

    def rows_of(bufs, k, q):
        return bufs[k][q, :, :, :, : FEATS[k]].reshape(quartets * ROWS, FEATS[k])

    def columns(k, q):
        return slice(q * QUARTER + STARTS[k], q * QUARTER + STARTS[k] + FEATS[k])

    gathered_out = [
        pltpu.make_async_copy(src, dst, local_sem.at[3 + i])
        for i, (src, dst) in enumerate(zip(gs + ss, (go0, go1, go2, so0, so1, so2)))
    ]

    for k in range(3):
        ag_recv_wait(gs, 0, k, 2)
        gathered_out[k].start()
        gate_sum = None
        up_sum = None
        for q in range(RING):
            rows = rows_of(gs, k, q)
            gate_part = contract_last(rows, wg[:, columns(k, q)])
            up_part = contract_last(rows, wu[:, columns(k, q)])
            gate_sum = gate_part if gate_sum is None else gate_sum + gate_part
            up_sum = up_part if up_sum is None else up_sum + up_part
        if k == 0:
            acc[0] = gate_sum
            acc[1] = up_sum
        else:
            acc[0] += gate_sum
            acc[1] += up_sum

    def nb_copy():
        return remote(new_o, nb, nb_send, nb_recv, partner)

    @pl.when(pipe == 0)
    def _():
        nb_copy().wait_recv()
        low = lax.broadcasted_iota(jnp.int32, (2 * BLOCK, 1), 0) < BLOCK
        mine = sc[3][:, 0:1]
        same = 1.0 - jnp.minimum(jnp.abs(nb[0, :, QUARTER : QUARTER + 1].astype(F32) - mine), 1.0)
        other = pltpu.roll(nb[0, :, QUARTER:].astype(F32), BLOCK, 0)[:, 0:1]
        cross = 1.0 - jnp.minimum(jnp.abs(other - mine), 1.0)
        for q in range(RING):
            rows = nb[q, :, :QUARTER].astype(F32)
            turned = pltpu.roll(rows, BLOCK, 0)
            kept_rows = (1.0 - same - cross) * up_ref[q]
            up_ref[q] = same * rows + cross * turned + kept_rows
        make_scaled()
        hand_start(bs, hs, 1)
        hand_wait(bs, hs, 1)
        make_tile(hs, ss, FEATS)
        for k in range(3):
            ag_start(ss, 1, k, 0)
        for stage in (1, 2):
            for k in range(3):
                ag_recv_wait(ss, 1, k, stage - 1)
                ag_start(ss, 1, k, stage)

    for k in range(3):
        ag_recv_wait(ss, 1, k, 2)
        gathered_out[3 + k].start()
        grad_sum = None
        for q in range(RING):
            part = contract_last(rows_of(ss, k, q), wd[:, columns(k, q)])
            grad_sum = part if grad_sum is None else grad_sum + part
        if k == 0:
            acc[2] = grad_sum
        else:
            acc[2] += grad_sum

    gate_pre = acc[0]
    up_value = acc[1]
    hidden_grad = acc[2]
    sigma = jax.nn.sigmoid(gate_pre)
    activated = gate_pre * sigma
    slope = sigma * (1.0 + gate_pre * (1.0 - sigma))
    hidden = (activated * up_value).astype(BF16)
    hid_o[...] = hidden
    row_part = jnp.sum(hidden_grad * hidden.astype(F32), axis=1, keepdims=True)
    gg_o[...] = (hidden_grad * up_value * slope).astype(BF16)
    ug_o[...] = (hidden_grad * activated).astype(BF16)
    extra = g2[0, :, :, :, FEATS[2] :].reshape(quartets * ROWS, EXTRA).astype(F32)
    weight = row_part * jnp.sum(extra, axis=1, keepdims=True)
    row_hi, row_lo = hi_lo(row_part)
    lane = lax.broadcasted_iota(jnp.int32, (quartets * ROWS, EXTRA), 1)
    row_lanes = jnp.where(lane == 0, row_hi, jnp.where(lane == 1, row_lo, 0.0)).astype(BF16)

    def rs_copies(k, stage):
        order = ORDERS[k]
        dim = order[stage]
        src = (rs, a0, a1)[stage][k]
        dst = (rb0, rb1, rb2)[stage][k]
        left = [d for d in range(3) if d not in order[:stage]]
        copies = []
        for off in OFFS:
            index = tuple(ring_index(d, off) if d == dim else slice(None) for d in left)
            copies.append(
                remote(
                    src.at[index], dst.at[off - 1],
                    rs_send.at[k, stage, off], rs_recv.at[k, stage, off], peer(dim, off),
                )
            )
        return copies

    def rs_start(k, stage):
        for copy in rs_copies(k, stage):
            copy.start()

    def rs_sum(k, stage):
        for copy in rs_copies(k, stage):
            copy.wait_recv()
        order = ORDERS[k]
        dim = order[stage]
        src = (rs, a0, a1)[stage][k]
        got = (rb0, rb1, rb2)[stage][k]
        left = [d for d in range(3) if d not in order[:stage]]
        index = tuple(at[d] if d == dim else slice(None) for d in left)
        return (src[index].astype(F32) + got[0].astype(F32)) + (
            got[1].astype(F32) + got[2].astype(F32)
        )

    srb[0, yy] = jnp.zeros((2 * RING, QUARTER + EXTRA), F32)
    gg = gg_o[...]
    ug = ug_o[...]
    for k in range(3):
        for q in range(RING):
            part = jnp.dot(gg, wg[:, columns(k, q)], preferred_element_type=F32) + jnp.dot(
                ug, wu[:, columns(k, q)], preferred_element_type=F32
            )
            shape = (RING, RING, ROWS, FEATS[k])
            rs[k][q, :, :, :, : FEATS[k]] = part.astype(BF16).reshape(shape)
            if k == 2:
                rs[k][q, :, :, :, FEATS[k] :] = row_lanes.reshape(RING, RING, ROWS, EXTRA)
            rows = rows_of(gs, k, q).astype(F32)
            cols = slice(STARTS[k], STARTS[k] + FEATS[k])
            srb[0, yy, 2 * q : 2 * q + 1, cols] = jnp.sum(part * rows, axis=0, keepdims=True)
            srb[0, yy, 2 * q + 1 : 2 * q + 2, cols] = jnp.sum(
                weight * rows, axis=0, keepdims=True
            )
        rs_start(k, 0)

    def st_copies(stage):
        here = srb.at[stage, at[stage]]
        return [
            remote(
                here, here, st_send.at[stage, off], st_recv.at[stage, off], peer(stage, off)
            )
            for off in OFFS
        ]

    def st_sum(stage):
        for copy in st_copies(stage):
            copy.wait()
        return (srb[stage, 0] + srb[stage, 1]) + (srb[stage, 2] + srb[stage, 3])

    for copy in st_copies(0):
        copy.start()
    for stage in (0, 1):
        for k in range(3):
            (a0, a1)[stage][k][...] = rs_sum(k, stage)
            rs_start(k, stage + 1)
        srb[stage + 1, at[stage + 1]] = st_sum(stage)
        for copy in st_copies(stage + 1):
            copy.start()
    for k in range(3):
        u[yy, 0:ROWS, STARTS[k] : STARTS[k] + WIDTHS[k]] = rs_sum(k, 2)

    def back_copies():
        return [
            remote(
                u.at[yy, pl.ds(0, ROWS)], u.at[yy, pl.ds(0, ROWS)],
                un_send.at[off], un_recv.at[off], peer(0, off),
            )
            for off in OFFS
        ]

    def back_over_copy(q):
        return remote(
            u.at[yy, pl.ds(0, 8)], u.at[yy, pl.ds(ROWS, 8)],
            un_send.at[0], un_recv.at[RING + q], same_pipe(prev_last),
        )

    def back_over_wait(q):
        return remote(
            u.at[q, pl.ds(0, 8)], u.at[q, pl.ds(ROWS, 8)],
            un_send.at[0], un_recv.at[RING + q], same_pipe(prev_last),
        )

    for copy in back_copies():
        copy.start()
    back_over_copy(yy).start()
    for copy in back_copies():
        copy.wait_recv()

    @pl.when(yy == RING - 1)
    def _():
        for q in range(RING):
            back_over_wait(q).wait_recv()

    first = pl.multiple_of(lax.div(yy, 2) * 8, 8)
    odd = lax.rem(yy, 2) == 1

    def owned(q, cols):
        a = u[q, pl.ds(first, 8), cols]
        b = u[q, pl.ds(first + 8, 8), cols]
        low = lax.broadcasted_iota(jnp.int32, a.shape, 0) < BLOCK
        turned = jnp.where(low, pltpu.roll(a, BLOCK, 0), pltpu.roll(b, BLOCK, 0))
        return jnp.where(odd, turned, a)

    feats = slice(0, QUARTER)
    total = jnp.zeros((2 * BLOCK, 1), F32)
    for q in range(RING):
        hat_grad = owned(q, feats) * gain[:, quarter(q)]
        total = total + jnp.sum(hat_grad * hat_ref[q], axis=1, keepdims=True)
    mean = total / float(RING * QUARTER)
    row_sum = jnp.sum(owned(0, slice(QUARTER, QUARTER + EXTRA)), axis=1, keepdims=True)
    logit_grad = row_sum * sc[1][:, 0:1]
    scale = sc[2][:, 0:1]
    for q in range(RING):
        hat_grad = owned(q, feats) * gain[:, quarter(q)]
        delta = scale * (hat_grad - hat_ref[q] * mean) + logit_grad * router_row[
            :, quarter(q)
        ].astype(F32)
        new_o[q, :, :QUARTER] = (up_ref[q] + delta).astype(BF16)
        new_o[q, :, QUARTER:] = sc[3].astype(BF16)

    @pl.when(pipe == 1)
    def _():
        nb_copy().start()
        nb_o[...] = new_o[...]

    @pl.when(pipe == 0)
    def _():
        nb_o[...] = nb[...]

    st_o[...] = st_sum(2)

    ag_send_wait(gs, 0)
    ag_send_wait(ss, 1)
    for k in range(3):
        for stage in range(3):
            for copy in rs_copies(k, stage):
                copy.wait_send()
    for copy in back_copies():
        copy.wait_send()
    back_over_copy(yy).wait_send()

    @pl.when(pipe == 1)
    def _():
        nb_copy().wait_send()

    for copy in gathered_out:
        copy.wait()


def communicate(route_blocks, route_dest, saved, grad_out, gain, w_router, wg, wu, wd):
    ff = wg.shape[1]
    rows = RING * RING * ROWS
    width = QUARTER + EXTRA
    vmem = pl.BlockSpec(memory_space=pltpu.VMEM)
    smem = pl.BlockSpec(memory_space=pltpu.SMEM)
    hbm = pl.BlockSpec(memory_space=pl.ANY)
    cube = (RING, RING, RING, ROWS)
    shape = jax.ShapeDtypeStruct
    out_shape = (
        [shape(cube + (w,), BF16) for w in WIDTHS]
        + [shape(cube + (w,), BF16) for w in FEATS]
        + [shape((rows, ff), BF16)] * 3
        + [shape((RING, 8, width), BF16)] * 2
        + [shape((8, width), F32)]
    )
    dma = pltpu.SemaphoreType.DMA
    scratch = (
        [pltpu.VMEM(grad_out.shape, BF16)] * 2
        + [pltpu.VMEM(gain.shape, F32), pltpu.VMEM(w_router.shape, BF16)]
        + [pltpu.VMEM((RING, 8, QUARTER), F32)] * 2
        + [pltpu.VMEM((4, 8, EXTRA), F32), pltpu.VMEM((RING, 8, width), BF16)]
        + [pltpu.VMEM((RING, 8, QUARTER), BF16)]
        + [pltpu.VMEM((5, 8, width), BF16), pltpu.VMEM((5, 8, QUARTER), BF16)]
        + [pltpu.VMEM(cube + (w,), BF16) for w in WIDTHS]
        + [pltpu.VMEM(cube + (w,), BF16) for w in FEATS]
        + [pltpu.VMEM(cube + (w,), BF16) for w in WIDTHS]
        + [pltpu.VMEM((3, RING, RING, ROWS, w), BF16) for w in WIDTHS]
        + [pltpu.VMEM((RING, RING, ROWS, w), F32) for w in WIDTHS]
        + [pltpu.VMEM((3, RING, ROWS, w), F32) for w in WIDTHS]
        + [pltpu.VMEM((RING, ROWS, w), F32) for w in WIDTHS]
        + [pltpu.VMEM((3, ROWS, w), F32) for w in WIDTHS]
        + [pltpu.VMEM((RING, ROWS + 8, width), F32)]
        + [pltpu.VMEM((RING, 8, width), BF16)]
        + [pltpu.VMEM((3, RING, 8, width), F32)]
        + [pltpu.VMEM((3, rows, ff), F32)]
        + [pltpu.VMEM(wg.shape[1:], BF16)] * 3
        + [dma((2, 8)), dma((2, 4))]
        + [dma((2, 3, 3, 4)), dma((2, 3, 3, 4))]
        + [dma((3, 3, 4)), dma((3, 3, 4))]
        + [dma((3, 4)), dma((3, 4))]
        + [dma((4,)), dma((8,))]
        + [dma, dma]
        + [dma((13,))]
    )
    return pl.pallas_call(
        step_kernel,
        out_shape=out_shape,
        in_specs=[smem] * 2 + [hbm] * 7,
        out_specs=[hbm] * 6 + [vmem] * 6,
        scratch_shapes=scratch,
        compiler_params=pltpu.CompilerParams(
            collective_id=0, has_side_effects=True, vmem_limit_bytes=58 * 1024 * 1024
        ),
        name="routed_step",
    )(route_blocks, route_dest, saved, grad_out, gain, w_router, wg, wu, wd)


def finish_kernel(
    hid, gg, ug, g0, g1, g2, s0, s1, s2, grad_out, nb, fresh, stats, gain,
    out_inputs, out_gate, out_up, out_down, out_gain, out_router,
):
    rows = hid.shape[0]
    for k, (g, s) in enumerate(zip((g0, g1, g2), (s0, s1, s2))):
        cols = slice(STARTS[k], STARTS[k] + FEATS[k])
        normed = g[0, :, :, :, : FEATS[k]].reshape(rows, FEATS[k])
        scaled = s[0].reshape(rows, FEATS[k])
        out_gate[0, :, cols] = contract_first(gg[...], normed)
        out_up[0, :, cols] = contract_first(ug[...], normed)
        out_down[0, :, cols] = contract_first(hid[...], scaled)
    patterns = []
    low = lax.broadcasted_iota(jnp.int32, (2 * BLOCK, QUARTER), 0) < BLOCK
    for ref in (nb, fresh):
        new_rows = ref[0, :, :QUARTER].astype(F32)
        turned = pltpu.roll(new_rows, BLOCK, 0)
        which = ref[0, :, QUARTER:].astype(F32)
        patterns.append((which[0:1, 0:1], jnp.where(low, new_rows, turned)))
        patterns.append((which[BLOCK : BLOCK + 1, 0:1], jnp.where(low, turned, new_rows)))
    half = jnp.where(lax.broadcasted_iota(jnp.int32, (2 * BLOCK, 1), 0) < BLOCK, 0.0, 1.0)
    for i in range(grad_out.shape[0] // 8):
        block = half + float(2 * i)
        value = grad_out[8 * i : 8 * i + 8, :].astype(F32)
        for which, pattern in patterns:
            value = jnp.where(block == which, pattern, value)
        out_inputs[0, 8 * i : 8 * i + 8, :] = value.astype(BF16)
    q = pl.program_id(0)
    out_gain[...] = stats[pl.ds(2 * q, 1), :QUARTER] / gain[...]
    out_router[...] = stats[pl.ds(2 * q + 1, 1), :QUARTER] / gain[...]


def finish(hid, gg, ug, gathered, grad_out, nb, fresh, stats, gain):
    tok_rows, model_dim = grad_out.shape
    ff = hid.shape[1]

    def whole(array):
        return pl.BlockSpec(array.shape, lambda q: (0,) * array.ndim)

    def part(width):
        return pl.BlockSpec((1, RING, RING, ROWS, width), lambda q: (q, 0, 0, 0, 0))

    new_rows = pl.BlockSpec((1,) + nb.shape[1:], lambda q: (q, 0, 0))
    vector = pl.BlockSpec((1, QUARTER), lambda q: (0, q))
    grads = pl.BlockSpec((1, ff, QUARTER), lambda q: (0, 0, q))
    shape = jax.ShapeDtypeStruct
    return pl.pallas_call(
        finish_kernel,
        grid=(RING,),
        out_shape=[shape((1, tok_rows, model_dim), BF16)]
        + [shape((1, ff, model_dim), F32)] * 3
        + [shape((1, model_dim), F32)] * 2,
        in_specs=[whole(hid)] * 3
        + [part(w) for w in WIDTHS + FEATS]
        + [pl.BlockSpec((tok_rows, QUARTER), lambda q: (0, q)), new_rows, new_rows]
        + [whole(stats), vector],
        out_specs=[pl.BlockSpec((1, tok_rows, QUARTER), lambda q: (0, 0, q))]
        + [grads] * 3
        + [vector] * 2,
        compiler_params=pltpu.CompilerParams(vmem_limit_bytes=60 * 1024 * 1024),
        name="finish",
    )(hid, gg, ug, *gathered, grad_out, nb, fresh, stats, gain)


def on_device(saved, grad_out, route_blocks, route_dest, gain, w_router, w_gate, w_up, w_down):
    results = communicate(
        route_blocks, route_dest, saved, grad_out, gain, w_router, w_gate, w_up, w_down
    )
    hid, gg, ug, nb, fresh, stats = results[6:]
    return tuple(finish(hid, gg, ug, results[:6], grad_out, nb, fresh, stats, gain))


def solution(mesh):
    in_specs = (
        P("pipe", "ctx", None),
        P("ctx", None),
        P("pipe", "ctx", None),
        P("pipe", "ctx", None),
        P("pipe", None),
        P("pipe", None),
        P("pipe", "ctx", None),
        P("pipe", "ctx", None),
        P("pipe", "ctx", None),
    )
    out_specs = (
        P("pipe", "ctx", None),
        P("pipe", "ctx", None),
        P("pipe", "ctx", None),
        P("pipe", "ctx", None),
        P("pipe", None),
        P("pipe", None),
    )
    return jax.shard_map(
        on_device, mesh=mesh, in_specs=in_specs, out_specs=out_specs, check_vma=False
    )
```

```python
import jax
import jax.numpy as jnp
from jax import lax
from jax.experimental import pallas as pl
from jax.experimental.pallas import tpu as pltpu
from jax.sharding import PartitionSpec as P

BLOCK = 4
EPSILON = 1e-05
RING = 4
OFFS = (1, 2, 3)
QUARTER = 1024
EXTRA = 128
WIDTHS = (384, 384, 384)
FEATS = (384, 384, 256)
STARTS = (0, 384, 768)
ROWS = 16
ORDERS = ((0, 1, 2), (1, 2, 0), (2, 0, 1))
F32 = jnp.float32
BF16 = jnp.bfloat16
MESH = pl.DeviceIdType.MESH


def contract_last(left_side, right_side):
    return lax.dot_general(
        left_side, right_side, (((1,), (1,)), ((), ())), preferred_element_type=F32
    )


def hi_lo(value):
    hi = value.astype(BF16).astype(F32)
    return hi, value - hi


def step_kernel(
    blocks, targets, saved_hbm, grad_hbm, gain_hbm, router_hbm, wg_hbm, wu_hbm, wd_hbm,
    go0, go1, go2, so0, so1, so2, hid_o, gg_o, ug_o, nb_o, new_o, st_o,
    saved, grad_out, gain, router_row, gain_q, router_q, bn, bu, hn, hu, up_tile, new_tile,
    above, g0, g1, g2, s0, s1, s2, r0, r1, r2,
    rb00, rb01, rb02, a00, a01, a02, rb10, rb11, rb12, a10, a11, a12, rb20, rb21, rb22,
    u, nb, srb, acc, wg, wu, wd,
    hand_send, hand_recv, ag_send, ag_recv, rs_send, rs_recv, st_send, st_recv,
    un_send, un_recv, ab_send, ab_recv, nb_send, nb_recv, local_sem, go_sem,
):
    pipe = lax.axis_index("pipe")
    me = lax.axis_index("ctx")
    yy = lax.rem(me, RING)
    quartet = lax.div(me, RING)
    zz = lax.rem(quartet, RING)
    xx = lax.div(quartet, RING)
    at = (yy, xx, zz)
    quartets = RING * RING
    next_base = lax.rem(quartet + 1, quartets) * RING
    prev_base = lax.rem(quartet + quartets - 1, quartets) * RING
    prev_last = prev_base + RING - 1

    def ring_index(dim, off):
        return lax.rem(at[dim] + RING - off, RING)

    def peer(dim, off):
        pos = list(at)
        pos[dim] = ring_index(dim, off)
        return {"pipe": pipe, "ctx": pos[1] * 16 + pos[2] * 4 + pos[0]}

    def same_pipe(ctx):
        return {"pipe": pipe, "ctx": ctx}

    def other_pipe(ctx):
        return {"pipe": 1 - pipe, "ctx": ctx}

    def remote(src, dst, send, recv, device):
        return pltpu.make_async_remote_copy(
            src_ref=src, dst_ref=dst, send_sem=send, recv_sem=recv,
            device_id=device, device_id_type=MESH,
        )

    gs, ss, rs = (g0, g1, g2), (s0, s1, s2), (r0, r1, r2)
    rb0, a0 = (rb00, rb01, rb02), (a00, a01, a02)
    rb1, a1 = (rb10, rb11, rb12), (a10, a11, a12)
    rb2 = (rb20, rb21, rb22)

    barrier = pltpu.get_barrier_semaphore()

    def greet(device):
        pl.semaphore_signal(barrier, inc=1, device_id=device, device_id_type=MESH)

    row_copies = [
        pltpu.make_async_copy(src, dst, local_sem.at[9 + i])
        for i, (src, dst) in enumerate(
            (
                (saved_hbm.at[0], saved),
                (gain_hbm, gain),
                (router_hbm, router_row),
                (grad_hbm, grad_out),
            )
        )
    ]
    weight_copies = [
        pltpu.make_async_copy(src.at[0], dst, local_sem.at[i])
        for i, (src, dst) in enumerate(((wg_hbm, wg), (wu_hbm, wu), (wd_hbm, wd)))
    ]
    for copy in row_copies:
        copy.start()
    for dim in range(3):
        for off in OFFS:
            greet(peer(dim, off))
    for base in (prev_base, quartet * RING, next_base):
        greet(other_pipe(base + yy))
    greet(same_pipe(prev_last))

    @pl.when(yy == RING - 1)
    def _():
        for j in range(RING):
            greet(same_pipe(next_base + j))

    kept = targets[0, 0, 0] == me
    keep_block = jnp.where(kept, blocks[0, 0, 0], blocks[0, 0, 1])
    hand_block = jnp.where(kept, blocks[0, 0, 1], blocks[0, 0, 0])
    handed = jnp.where(kept, targets[0, 0, 1], targets[0, 0, 0]) >= 0
    first_rows = lax.broadcasted_iota(jnp.int32, (2 * BLOCK, 1), 0) < BLOCK
    mask = jnp.where(
        first_rows, jnp.where(kept, 1.0, 0.0).astype(F32), jnp.where(handed, 1.0, 0.0).astype(F32)
    )
    block_id = jnp.where(first_rows, keep_block, hand_block)
    row_in_block = lax.rem(lax.broadcasted_iota(jnp.int32, (2 * BLOCK, 1), 0), BLOCK)
    tokens = lax.broadcasted_iota(jnp.int32, (2 * BLOCK, saved.shape[0]), 1)
    chosen = jnp.where(tokens == block_id * BLOCK + row_in_block, mask, 0.0).astype(BF16)

    def pick(array, cols):
        return jnp.dot(chosen, array[:, cols], preferred_element_type=F32)

    def quarter(q):
        return slice(q * QUARTER, (q + 1) * QUARTER)

    for copy in row_copies[:3]:
        copy.wait()
    squares = jnp.zeros((2 * BLOCK, 1), F32)
    logits = jnp.zeros((2 * BLOCK, 1), F32)
    picked = []
    for q in range(RING):
        rows = pick(saved, quarter(q))
        picked.append(rows)
        gain_q[q] = gain[:, quarter(q)]
        router_q[q] = router_row[:, quarter(q)].astype(F32)
        squares += jnp.sum(rows * rows, axis=1, keepdims=True)
        logits += jnp.sum(rows * router_q[q], axis=1, keepdims=True)
    inverse = lax.rsqrt(squares / float(RING * QUARTER) + EPSILON)
    router = jax.nn.sigmoid(logits)
    lane = lax.broadcasted_iota(jnp.int32, (2 * BLOCK, EXTRA), 1)
    extra = jnp.zeros((2 * BLOCK, EXTRA), F32)
    for i, value in enumerate(
        hi_lo((1.0 - router) / inverse)
        + hi_lo(inverse)
        + hi_lo(router)
        + (block_id.astype(F32), me.astype(F32))
    ):
        extra = jnp.where(lane == i, value * mask, extra)
    for q in range(RING):
        bn[q, :, :QUARTER] = (picked[q] * inverse * gain_q[q]).astype(BF16)
        bn[q, :, QUARTER:] = extra.astype(BF16)
    row_copies[3].wait()
    for q in range(RING):
        bu[q] = pick(grad_out, quarter(q)).astype(BF16)
    for copy in weight_copies:
        copy.start()

    pl.semaphore_wait(barrier, 13 + RING * lax.div(yy, RING - 1))

    def hand_copies(src, dst, which):
        return [
            remote(
                src.at[ring_index(0, off)], dst.at[yy + 1],
                hand_send.at[which, off], hand_recv.at[which, off], peer(0, off),
            )
            for off in OFFS
        ]

    def hand_over_copy(src, dst, which, j):
        return remote(
            src.at[j], dst.at[0],
            hand_send.at[which, RING + j], hand_recv.at[which, 0], same_pipe(next_base + j),
        )

    def hand_start(src, dst, which):
        for copy in hand_copies(src, dst, which):
            copy.start()

        @pl.when(yy == RING - 1)
        def _():
            for j in range(RING):
                hand_over_copy(src, dst, which, j).start()

        dst[yy + 1] = src[yy]

    def hand_recv_wait(src, dst, which):
        for copy in hand_copies(src, dst, which):
            copy.wait_recv()
        hand_over_copy(src, dst, which, 0).wait_recv()

    def hand_send_wait(src, dst, which):
        for copy in hand_copies(src, dst, which):
            copy.wait_send()

        @pl.when(yy == RING - 1)
        def _():
            for j in range(RING):
                hand_over_copy(src, dst, which, j).wait_send()

    def halves(held, cols):
        b = [held[i, :, cols].astype(F32) for i in range(5)]
        low = lax.broadcasted_iota(jnp.int32, b[0].shape, 0) < BLOCK
        turned = [pltpu.roll(b[i], BLOCK, 0) for i in (0, 2, 4)]
        return (
            b[1] + jnp.where(low, turned[0], turned[1]),
            b[3] + jnp.where(low, turned[1], turned[2]),
        )

    def ag_copies(bufs, which, k, stage):
        dim = ORDERS[k][stage]
        index = tuple(
            slice(None) if d in ORDERS[k][:stage] else at[d] for d in range(3)
        )
        return [
            remote(
                bufs[k].at[index], bufs[k].at[index],
                ag_send.at[which, k, stage, off], ag_recv.at[which, k, stage, off],
                peer(dim, off),
            )
            for off in OFFS
        ]

    def ag_start(bufs, which, k, stage):
        for copy in ag_copies(bufs, which, k, stage):
            copy.start()

    def ag_recv_wait(bufs, which, k, stage):
        for copy in ag_copies(bufs, which, k, stage):
            copy.wait_recv()

    def ag_send_wait(bufs, which):
        for k in range(3):
            for stage in range(3):
                for copy in ag_copies(bufs, which, k, stage):
                    copy.wait_send()

    def group(k):
        return slice(STARTS[k], STARTS[k] + FEATS[k])

    def tile_info():
        info = g2[yy, xx, zz, :, FEATS[2] :].astype(F32)
        return info, info[:, 4:5] + info[:, 5:6]

    def make_scaled():
        _, chance = tile_info()
        for k in range(3):
            rows = jnp.concatenate([up_tile[0, :, group(k)], up_tile[1, :, group(k)]], axis=0)
            ss[k][yy, xx, zz] = (chance * rows).astype(BF16)
            ag_start(ss, 1, k, 0)

    def go_on(bufs, which, stage):
        for k in range(3):
            ag_recv_wait(bufs, which, k, stage - 1)
            ag_start(bufs, which, k, stage)

    hand_start(bn, hn, 0)
    hand_start(bu, hu, 1)
    hand_recv_wait(bn, hn, 0)
    for k in range(3):
        tile = halves(hn, slice(STARTS[k], STARTS[k] + WIDTHS[k]))
        gs[k][yy, xx, zz] = jnp.concatenate(tile, axis=0).astype(BF16)

        @pl.when(pipe == 1)
        def _(k=k):
            ag_start(gs, 0, k, 0)

    hand_recv_wait(bu, hu, 1)
    for k in range(3):
        tile = halves(hu, group(k))
        for h in range(2):
            up_tile[h, :, group(k)] = tile[h]

    @pl.when(pipe == 1)
    def _():
        make_scaled()
        for stage in (1, 2):
            go_on(gs, 0, stage)
            go_on(ss, 1, stage)
        pl.semaphore_signal(
            go_sem, inc=1, device_id=other_pipe(me), device_id_type=MESH
        )

    @pl.when(pipe == 0)
    def _():
        pl.semaphore_wait(go_sem, 1)
        for k in range(3):
            ag_start(gs, 0, k, 0)
        for stage in (1, 2):
            go_on(gs, 0, stage)

    for copy in weight_copies:
        copy.wait()

    def rows_of(bufs, k, q):
        return bufs[k][q, :, :, :, : FEATS[k]].reshape(quartets * ROWS, FEATS[k])

    def columns(k, q):
        return slice(q * QUARTER + STARTS[k], q * QUARTER + STARTS[k] + FEATS[k])

    gathered_out = [
        pltpu.make_async_copy(src, dst, local_sem.at[3 + i])
        for i, (src, dst) in enumerate(zip(gs + ss, (go0, go1, go2, so0, so1, so2)))
    ]

    for k in range(3):
        ag_recv_wait(gs, 0, k, 2)
        gathered_out[k].start()
        gate_sum = None
        up_sum = None
        for q in range(RING):
            rows = rows_of(gs, k, q)
            gate_part = contract_last(rows, wg[:, columns(k, q)])
            up_part = contract_last(rows, wu[:, columns(k, q)])
            gate_sum = gate_part if gate_sum is None else gate_sum + gate_part
            up_sum = up_part if up_sum is None else up_sum + up_part
        if k == 0:
            acc[0] = gate_sum
            acc[1] = up_sum
        else:
            acc[0] += gate_sum
            acc[1] += up_sum

    def above_copies():
        return [
            remote(
                new_tile, above.at[slot], ab_send.at[slot], ab_recv.at[slot],
                other_pipe(base + yy),
            )
            for slot, base in ((2, prev_base), (1, quartet * RING), (0, next_base))
        ]

    @pl.when(pipe == 0)
    def _():
        for copy in above_copies():
            copy.wait_recv()
        info, _ = tile_info()

        def shifted(cols):
            own = [above[1, h, :, cols].astype(F32) for h in range(2)]
            ends = [above[0, 1, :, cols].astype(F32), above[2, 0, :, cols].astype(F32)]
            turned = [pltpu.roll(v, BLOCK, 0) for v in (ends[0], own[0], own[1], ends[1])]
            low = lax.broadcasted_iota(jnp.int32, own[0].shape, 0) < BLOCK
            return [
                (
                    jnp.where(low, turned[h], turned[h + 1]),
                    own[h],
                    jnp.where(low, turned[h + 1], turned[h + 2]),
                )
                for h in range(2)
            ]

        ids = shifted(slice(QUARTER, QUARTER + EXTRA))
        weights = []
        for h in range(2):
            mine = info[8 * h : 8 * h + 8, 6:8]
            weights.append(
                [
                    1.0
                    - jnp.minimum(
                        jnp.abs(one[:, 6:7] - mine[:, 0:1]) + jnp.abs(one[:, 7:8] - mine[:, 1:2]),
                        1.0,
                    )
                    for one in ids[h]
                ]
            )
        for k in range(3):
            for h, rows in enumerate(shifted(group(k))):
                w = weights[h]
                value = (1.0 - w[0] - w[1] - w[2]) * up_tile[h, :, group(k)]
                for part, one in zip(w, rows):
                    value += part * one
                up_tile[h, :, group(k)] = value
        make_scaled()
        for stage in (1, 2):
            go_on(ss, 1, stage)

    for k in range(3):
        ag_recv_wait(ss, 1, k, 2)
        gathered_out[3 + k].start()
        grad_sum = None
        for q in range(RING):
            part = contract_last(rows_of(ss, k, q), wd[:, columns(k, q)])
            grad_sum = part if grad_sum is None else grad_sum + part
        if k == 0:
            acc[2] = grad_sum
        else:
            acc[2] += grad_sum

    gate_pre = acc[0]
    up_value = acc[1]
    hidden_grad = acc[2]
    sigma = jax.nn.sigmoid(gate_pre)
    activated = gate_pre * sigma
    slope = sigma * (1.0 + gate_pre * (1.0 - sigma))
    hidden = (activated * up_value).astype(BF16)
    row_part = jnp.sum(hidden_grad * hidden.astype(F32), axis=1, keepdims=True)
    gg = (hidden_grad * up_value * slope).astype(BF16)
    ug = (hidden_grad * activated).astype(BF16)
    dot_part = jnp.sum(
        gg.astype(F32) * gate_pre + ug.astype(F32) * up_value, axis=1, keepdims=True
    )
    extra = g2[0, :, :, :, FEATS[2] :].reshape(quartets * ROWS, EXTRA).astype(F32)
    weight = row_part * (extra[:, 0:1] + extra[:, 1:2])
    lane = lax.broadcasted_iota(jnp.int32, (quartets * ROWS, EXTRA), 1)
    row_lanes = jnp.zeros((quartets * ROWS, EXTRA), F32)
    for i, value in enumerate(hi_lo(row_part) + hi_lo(dot_part)):
        row_lanes = jnp.where(lane == i, value, row_lanes)
    row_lanes = row_lanes.astype(BF16).reshape(RING, RING, ROWS, EXTRA)

    def rs_copies(k, stage):
        order = ORDERS[k]
        dim = order[stage]
        src = (rs, a0, a1)[stage][k]
        dst = (rb0, rb1, rb2)[stage][k]
        left = [d for d in range(3) if d not in order[:stage]]
        copies = []
        for off in OFFS:
            index = tuple(ring_index(d, off) if d == dim else slice(None) for d in left)
            copies.append(
                remote(
                    src.at[index], dst.at[off - 1],
                    rs_send.at[k, stage, off], rs_recv.at[k, stage, off], peer(dim, off),
                )
            )
        return copies

    def rs_start(k, stage):
        for copy in rs_copies(k, stage):
            copy.start()

    def rs_sum(k, stage):
        for copy in rs_copies(k, stage):
            copy.wait_recv()
        order = ORDERS[k]
        dim = order[stage]
        src = (rs, a0, a1)[stage][k]
        got = (rb0, rb1, rb2)[stage][k]
        left = [d for d in range(3) if d not in order[:stage]]
        index = tuple(at[d] if d == dim else slice(None) for d in left)
        return (src[index].astype(F32) + got[0].astype(F32)) + (
            got[1].astype(F32) + got[2].astype(F32)
        )

    srb[0, yy] = jnp.zeros((2 * RING, QUARTER + EXTRA), F32)
    for k in range(3):
        for q in range(RING):
            part = jnp.dot(gg, wg[:, columns(k, q)], preferred_element_type=F32) + jnp.dot(
                ug, wu[:, columns(k, q)], preferred_element_type=F32
            )
            shape = (RING, RING, ROWS, FEATS[k])
            rs[k][q, :, :, :, : FEATS[k]] = part.astype(BF16).reshape(shape)
            if k == 2:
                rs[k][q, :, :, :, FEATS[k] :] = row_lanes
            rows = rows_of(gs, k, q).astype(F32)
            srb[0, yy, 2 * q : 2 * q + 1, group(k)] = jnp.sum(part * rows, axis=0, keepdims=True)
            srb[0, yy, 2 * q + 1 : 2 * q + 2, group(k)] = jnp.sum(
                weight * rows, axis=0, keepdims=True
            )
        rs_start(k, 0)

    def st_copies(stage):
        here = srb.at[stage, at[stage]]
        return [
            remote(
                here, here, st_send.at[stage, off], st_recv.at[stage, off], peer(stage, off)
            )
            for off in OFFS
        ]

    def st_sum(stage):
        for copy in st_copies(stage):
            copy.wait()
        return (srb[stage, 0] + srb[stage, 1]) + (srb[stage, 2] + srb[stage, 3])

    for copy in st_copies(0):
        copy.start()
    for ref, value in ((hid_o, hidden), (gg_o, gg), (ug_o, ug)):
        ref[...] = value.astype(F32).T.astype(BF16)
    for stage in (0, 1):
        for k in range(3):
            (a0, a1)[stage][k][...] = rs_sum(k, stage)
            rs_start(k, stage + 1)
        srb[stage + 1, at[stage + 1]] = st_sum(stage)
        for copy in st_copies(stage + 1):
            copy.start()

    sums = [rs_sum(k, 2) for k in range(3)]
    info, chance = tile_info()
    spare = sums[2][:, FEATS[2] :]
    logit_grad = (spare[:, 0:1] + spare[:, 1:2]) * (1.0 - chance)
    mean = (spare[:, 2:3] + spare[:, 3:4]) / float(RING * QUARTER)
    scale = info[:, 2:3] + info[:, 3:4]
    for k in range(3):
        gain_row = gain_q[yy, :, group(k)]
        hat = gs[k][yy, xx, zz, :, : FEATS[k]].astype(F32) / gain_row
        delta = scale * (sums[k][:, : FEATS[k]] * gain_row - hat * mean)
        delta = delta + logit_grad * router_q[yy, :, group(k)]
        for h in range(2):
            half = delta[8 * h : 8 * h + 8]
            new_tile[h, :, group(k)] = (up_tile[h, :, group(k)] + half).astype(BF16)
    for h in range(2):
        new_tile[h, :, QUARTER:] = info[8 * h : 8 * h + 8].astype(BF16)

    @pl.when(pipe == 1)
    def _():
        for copy in above_copies():
            copy.start()

    def back_copies():
        return [
            remote(
                new_tile, u.at[yy, pl.ds(0, 2)], un_send.at[off], un_recv.at[off], peer(0, off)
            )
            for off in OFFS
        ]

    def back_over_copy(q):
        return remote(
            new_tile, u.at[q, pl.ds(2, 2)], un_send.at[0], un_recv.at[RING + q],
            same_pipe(prev_last),
        )

    for copy in back_copies():
        copy.start()
    back_over_copy(yy).start()
    u[yy, 0:2] = new_tile[...]
    st_o[...] = st_sum(2)
    for copy in back_copies():
        copy.wait_recv()

    @pl.when(yy == RING - 1)
    def _():
        for q in range(RING):
            back_over_copy(q).wait_recv()

    upper = lax.div(yy, 2)
    odd = lax.rem(yy, 2) == 1

    def owned(q, cols):
        a = u[q, upper, :, cols].astype(F32)
        b = u[q, upper + 1, :, cols].astype(F32)
        low = lax.broadcasted_iota(jnp.int32, a.shape, 0) < BLOCK
        turned = jnp.where(low, pltpu.roll(a, BLOCK, 0), pltpu.roll(b, BLOCK, 0))
        return jnp.where(odd, turned, a)

    ids = owned(0, slice(QUARTER, QUARTER + EXTRA))
    valid = jnp.abs(ids[:, 7:8] - me.astype(F32)) < 0.5
    which = jnp.broadcast_to(jnp.where(valid, ids[:, 6:7], -1.0), (2 * BLOCK, EXTRA))
    for q in range(RING):
        new_o[q, :, :QUARTER] = owned(q, slice(0, QUARTER)).astype(BF16)
        new_o[q, :, QUARTER:] = which.astype(BF16)

    def nb_copy():
        return remote(new_o, nb, nb_send, nb_recv, other_pipe(me))

    @pl.when(pipe == 1)
    def _():
        nb_copy().start()
        nb_o[...] = new_o[...]

    @pl.when(pipe == 0)
    def _():
        nb_copy().wait_recv()
        nb_o[...] = nb[...]

    hand_send_wait(bn, hn, 0)
    hand_send_wait(bu, hu, 1)
    ag_send_wait(gs, 0)
    ag_send_wait(ss, 1)
    for k in range(3):
        for stage in range(3):
            for copy in rs_copies(k, stage):
                copy.wait_send()
    for copy in back_copies():
        copy.wait_send()
    back_over_copy(yy).wait_send()

    @pl.when(pipe == 1)
    def _():
        for copy in above_copies():
            copy.wait_send()
        nb_copy().wait_send()

    for copy in gathered_out:
        copy.wait()


def communicate(route_blocks, route_dest, saved, grad_out, gain, w_router, wg, wu, wd):
    ff = wg.shape[1]
    rows = RING * RING * ROWS
    width = QUARTER + EXTRA
    vmem = pl.BlockSpec(memory_space=pltpu.VMEM)
    smem = pl.BlockSpec(memory_space=pltpu.SMEM)
    hbm = pl.BlockSpec(memory_space=pl.ANY)
    cube = (RING, RING, RING, ROWS)
    shape = jax.ShapeDtypeStruct
    out_shape = (
        [shape(cube + (w,), BF16) for w in WIDTHS]
        + [shape(cube + (w,), BF16) for w in FEATS]
        + [shape((ff, rows), BF16)] * 3
        + [shape((RING, 8, width), BF16)] * 2
        + [shape((8, width), F32)]
    )
    dma = pltpu.SemaphoreType.DMA
    scratch = (
        [pltpu.VMEM(grad_out.shape, BF16)] * 2
        + [pltpu.VMEM(gain.shape, F32), pltpu.VMEM(w_router.shape, BF16)]
        + [pltpu.VMEM((RING, 1, QUARTER), F32)] * 2
        + [pltpu.VMEM((RING, 8, width), BF16), pltpu.VMEM((RING, 8, QUARTER), BF16)]
        + [pltpu.VMEM((5, 8, width), BF16), pltpu.VMEM((5, 8, QUARTER), BF16)]
        + [pltpu.VMEM((2, 8, QUARTER), F32), pltpu.VMEM((2, 8, width), BF16)]
        + [pltpu.VMEM((3, 2, 8, width), BF16)]
        + [pltpu.VMEM(cube + (w,), BF16) for w in WIDTHS]
        + [pltpu.VMEM(cube + (w,), BF16) for w in FEATS]
        + [pltpu.VMEM(cube + (w,), BF16) for w in WIDTHS]
        + [pltpu.VMEM((3, RING, RING, ROWS, w), BF16) for w in WIDTHS]
        + [pltpu.VMEM((RING, RING, ROWS, w), F32) for w in WIDTHS]
        + [pltpu.VMEM((3, RING, ROWS, w), F32) for w in WIDTHS]
        + [pltpu.VMEM((RING, ROWS, w), F32) for w in WIDTHS]
        + [pltpu.VMEM((3, ROWS, w), F32) for w in WIDTHS]
        + [pltpu.VMEM((RING, 4, 8, width), BF16)]
        + [pltpu.VMEM((RING, 8, width), BF16)]
        + [pltpu.VMEM((3, RING, 8, width), F32)]
        + [pltpu.VMEM((3, rows, ff), F32)]
        + [pltpu.VMEM(wg.shape[1:], BF16)] * 3
        + [dma((2, 8)), dma((2, 4))]
        + [dma((2, 3, 3, 4)), dma((2, 3, 3, 4))]
        + [dma((3, 3, 4)), dma((3, 3, 4))]
        + [dma((3, 4)), dma((3, 4))]
        + [dma((4,)), dma((8,))]
        + [dma((3,)), dma((3,))]
        + [dma, dma]
        + [dma((13,)), pltpu.SemaphoreType.REGULAR]
    )
    return pl.pallas_call(
        step_kernel,
        out_shape=out_shape,
        in_specs=[smem] * 2 + [hbm] * 7,
        out_specs=[hbm] * 6 + [vmem] * 6,
        scratch_shapes=scratch,
        compiler_params=pltpu.CompilerParams(
            collective_id=0, has_side_effects=True, vmem_limit_bytes=58 * 1024 * 1024
        ),
        name="routed_step",
    )(route_blocks, route_dest, saved, grad_out, gain, w_router, wg, wu, wd)


def finish_kernel(
    hid, gg, ug, g0, g1, g2, s0, s1, s2, grad_out, nb, fresh, stats, gain,
    out_inputs, out_gate, out_up, out_down, out_gain, out_router,
):
    rows = hid.shape[1]
    for k, (g, s) in enumerate(zip((g0, g1, g2), (s0, s1, s2))):
        cols = slice(STARTS[k], STARTS[k] + FEATS[k])
        normed = g[0, :, :, :, : FEATS[k]].reshape(rows, FEATS[k])
        scaled = s[0].reshape(rows, FEATS[k])
        out_gate[0, :, cols] = jnp.dot(gg[...], normed, preferred_element_type=F32)
        out_up[0, :, cols] = jnp.dot(ug[...], normed, preferred_element_type=F32)
        out_down[0, :, cols] = jnp.dot(hid[...], scaled, preferred_element_type=F32)
    patterns = []
    low = lax.broadcasted_iota(jnp.int32, (2 * BLOCK, QUARTER), 0) < BLOCK
    for ref in (nb, fresh):
        new_rows = ref[0, :, :QUARTER].astype(F32)
        turned = pltpu.roll(new_rows, BLOCK, 0)
        which = ref[0, :, QUARTER:].astype(F32)
        patterns.append((which[0:1, 0:1], jnp.where(low, new_rows, turned)))
        patterns.append((which[BLOCK : BLOCK + 1, 0:1], jnp.where(low, turned, new_rows)))
    half = jnp.where(lax.broadcasted_iota(jnp.int32, (2 * BLOCK, 1), 0) < BLOCK, 0.0, 1.0)
    for i in range(grad_out.shape[0] // 8):
        block = half + float(2 * i)
        value = grad_out[8 * i : 8 * i + 8, :].astype(F32)
        for which, pattern in patterns:
            value = jnp.where(block == which, pattern, value)
        out_inputs[0, 8 * i : 8 * i + 8, :] = value.astype(BF16)
    q = pl.program_id(0)
    out_gain[...] = stats[pl.ds(2 * q, 1), :QUARTER] / gain[...]
    out_router[...] = stats[pl.ds(2 * q + 1, 1), :QUARTER] / gain[...]


def finish(hid, gg, ug, gathered, grad_out, nb, fresh, stats, gain):
    tok_rows, model_dim = grad_out.shape
    ff = hid.shape[0]

    def whole(array):
        return pl.BlockSpec(array.shape, lambda q: (0,) * array.ndim)

    def part(width):
        return pl.BlockSpec((1, RING, RING, ROWS, width), lambda q: (q, 0, 0, 0, 0))

    new_rows = pl.BlockSpec((1,) + nb.shape[1:], lambda q: (q, 0, 0))
    vector = pl.BlockSpec((1, QUARTER), lambda q: (0, q))
    grads = pl.BlockSpec((1, ff, QUARTER), lambda q: (0, 0, q))
    shape = jax.ShapeDtypeStruct
    return pl.pallas_call(
        finish_kernel,
        grid=(RING,),
        out_shape=[shape((1, tok_rows, model_dim), BF16)]
        + [shape((1, ff, model_dim), F32)] * 3
        + [shape((1, model_dim), F32)] * 2,
        in_specs=[whole(hid)] * 3
        + [part(w) for w in WIDTHS + FEATS]
        + [pl.BlockSpec((tok_rows, QUARTER), lambda q: (0, q)), new_rows, new_rows]
        + [whole(stats), vector],
        out_specs=[pl.BlockSpec((1, tok_rows, QUARTER), lambda q: (0, 0, q))]
        + [grads] * 3
        + [vector] * 2,
        compiler_params=pltpu.CompilerParams(vmem_limit_bytes=60 * 1024 * 1024),
        name="finish",
    )(hid, gg, ug, *gathered, grad_out, nb, fresh, stats, gain)


def on_device(saved, grad_out, route_blocks, route_dest, gain, w_router, w_gate, w_up, w_down):
    results = communicate(
        route_blocks, route_dest, saved, grad_out, gain, w_router, w_gate, w_up, w_down
    )
    hid, gg, ug, nb, fresh, stats = results[6:]
    return tuple(finish(hid, gg, ug, results[:6], grad_out, nb, fresh, stats, gain))


def solution(mesh):
    in_specs = (
        P("pipe", "ctx", None),
        P("ctx", None),
        P("pipe", "ctx", None),
        P("pipe", "ctx", None),
        P("pipe", None),
        P("pipe", None),
        P("pipe", "ctx", None),
        P("pipe", "ctx", None),
        P("pipe", "ctx", None),
    )
    out_specs = (
        P("pipe", "ctx", None),
        P("pipe", "ctx", None),
        P("pipe", "ctx", None),
        P("pipe", "ctx", None),
        P("pipe", None),
        P("pipe", None),
    )
    return jax.shard_map(
        on_device, mesh=mesh, in_specs=in_specs, out_specs=out_specs, check_vma=False
    )
```

```python
import jax
import jax.numpy as jnp
from jax import lax
from jax.experimental import pallas as pl
from jax.experimental.pallas import tpu as pltpu
from jax.sharding import PartitionSpec as P

BLOCK = 4
EPSILON = 1e-05
RING = 4
OFFS = (1, 2, 3)
QUARTER = 1024
EXTRA = 128
WIDTHS = (384, 384, 384)
FEATS = (384, 384, 256)
STARTS = (0, 384, 768)
ROWS = 16
ORDERS = ((0, 1, 2), (1, 2, 0), (2, 0, 1))
F32 = jnp.float32
BF16 = jnp.bfloat16
MESH = pl.DeviceIdType.MESH


def contract_last(left_side, right_side):
    return lax.dot_general(
        left_side, right_side, (((1,), (1,)), ((), ())), preferred_element_type=F32
    )


def hi_lo(value):
    hi = value.astype(BF16).astype(F32)
    return hi, value - hi


def step_kernel(
    blocks, targets, saved_hbm, grad_hbm, gain_hbm, router_hbm, wg_hbm, wu_hbm, wd_hbm,
    gate_o, up_o, down_o, nb_o, new_o, st_o,
    saved, grad_out, gain, router_row, gain_q, router_q, bn, bu, hn, hu, up_tile, new_tile,
    above, g0, g1, g2, s0, s1, s2, r0, r1, r2,
    rb00, rb01, rb02, a00, a01, a02, rb10, rb11, rb12, a10, a11, a12, rb20, rb21, rb22,
    u, nb, srb, acc, wg, wu, wd,
    hand_send, hand_recv, ag_send, ag_recv, rs_send, rs_recv, st_send, st_recv,
    un_send, un_recv, ab_send, ab_recv, nb_send, nb_recv, local_sem, go_sem,
):
    pipe = lax.axis_index("pipe")
    me = lax.axis_index("ctx")
    yy = lax.rem(me, RING)
    quartet = lax.div(me, RING)
    zz = lax.rem(quartet, RING)
    xx = lax.div(quartet, RING)
    at = (yy, xx, zz)
    quartets = RING * RING
    next_base = lax.rem(quartet + 1, quartets) * RING
    prev_base = lax.rem(quartet + quartets - 1, quartets) * RING
    prev_last = prev_base + RING - 1

    def ring_index(dim, off):
        return lax.rem(at[dim] + RING - off, RING)

    def peer(dim, off):
        pos = list(at)
        pos[dim] = ring_index(dim, off)
        return {"pipe": pipe, "ctx": pos[1] * 16 + pos[2] * 4 + pos[0]}

    def same_pipe(ctx):
        return {"pipe": pipe, "ctx": ctx}

    def other_pipe(ctx):
        return {"pipe": 1 - pipe, "ctx": ctx}

    def remote(src, dst, send, recv, device):
        return pltpu.make_async_remote_copy(
            src_ref=src, dst_ref=dst, send_sem=send, recv_sem=recv,
            device_id=device, device_id_type=MESH,
        )

    gs, ss, rs = (g0, g1, g2), (s0, s1, s2), (r0, r1, r2)
    rb0, a0 = (rb00, rb01, rb02), (a00, a01, a02)
    rb1, a1 = (rb10, rb11, rb12), (a10, a11, a12)
    rb2 = (rb20, rb21, rb22)

    barrier = pltpu.get_barrier_semaphore()

    def greet(device):
        pl.semaphore_signal(barrier, inc=1, device_id=device, device_id_type=MESH)

    row_copies = [
        pltpu.make_async_copy(src, dst, local_sem.at[9 + i])
        for i, (src, dst) in enumerate(
            (
                (saved_hbm.at[0], saved),
                (gain_hbm, gain),
                (router_hbm, router_row),
                (grad_hbm, grad_out),
            )
        )
    ]
    weight_copies = [
        pltpu.make_async_copy(src.at[0], dst, local_sem.at[i])
        for i, (src, dst) in enumerate(((wg_hbm, wg), (wu_hbm, wu), (wd_hbm, wd)))
    ]
    for copy in row_copies:
        copy.start()
    for dim in range(3):
        for off in OFFS:
            greet(peer(dim, off))
    for base in (prev_base, quartet * RING, next_base):
        greet(other_pipe(base + yy))
    greet(same_pipe(prev_last))

    @pl.when(yy == RING - 1)
    def _():
        for j in range(RING):
            greet(same_pipe(next_base + j))

    kept = targets[0, 0, 0] == me
    keep_block = jnp.where(kept, blocks[0, 0, 0], blocks[0, 0, 1])
    hand_block = jnp.where(kept, blocks[0, 0, 1], blocks[0, 0, 0])
    handed = jnp.where(kept, targets[0, 0, 1], targets[0, 0, 0]) >= 0
    first_rows = lax.broadcasted_iota(jnp.int32, (2 * BLOCK, 1), 0) < BLOCK
    mask = jnp.where(
        first_rows, jnp.where(kept, 1.0, 0.0).astype(F32), jnp.where(handed, 1.0, 0.0).astype(F32)
    )
    block_id = jnp.where(first_rows, keep_block, hand_block)
    row_in_block = lax.rem(lax.broadcasted_iota(jnp.int32, (2 * BLOCK, 1), 0), BLOCK)
    tokens = lax.broadcasted_iota(jnp.int32, (2 * BLOCK, saved.shape[0]), 1)
    chosen = jnp.where(tokens == block_id * BLOCK + row_in_block, mask, 0.0).astype(BF16)

    def pick(array, cols):
        return jnp.dot(chosen, array[:, cols], preferred_element_type=F32)

    def quarter(q):
        return slice(q * QUARTER, (q + 1) * QUARTER)

    for copy in row_copies[:3]:
        copy.wait()
    squares = jnp.zeros((2 * BLOCK, 1), F32)
    logits = jnp.zeros((2 * BLOCK, 1), F32)
    picked = []
    for q in range(RING):
        rows = pick(saved, quarter(q))
        picked.append(rows)
        gain_q[q] = gain[:, quarter(q)]
        router_q[q] = router_row[:, quarter(q)].astype(F32)
        squares += jnp.sum(rows * rows, axis=1, keepdims=True)
        logits += jnp.sum(rows * router_q[q], axis=1, keepdims=True)
    inverse = lax.rsqrt(squares / float(RING * QUARTER) + EPSILON)
    router = jax.nn.sigmoid(logits)
    lane = lax.broadcasted_iota(jnp.int32, (2 * BLOCK, EXTRA), 1)
    extra = jnp.zeros((2 * BLOCK, EXTRA), F32)
    for i, value in enumerate(
        hi_lo((1.0 - router) / inverse)
        + hi_lo(inverse)
        + hi_lo(router)
        + (block_id.astype(F32), me.astype(F32))
    ):
        extra = jnp.where(lane == i, value * mask, extra)
    for q in range(RING):
        bn[q, :, :QUARTER] = (picked[q] * inverse * gain_q[q]).astype(BF16)
        bn[q, :, QUARTER:] = extra.astype(BF16)
    pl.semaphore_wait(barrier, 13 + RING * lax.div(yy, RING - 1))

    def hand_copies(src, dst, which):
        return [
            remote(
                src.at[ring_index(0, off)], dst.at[yy + 1],
                hand_send.at[which, off], hand_recv.at[which, off], peer(0, off),
            )
            for off in OFFS
        ]

    def hand_over_copy(src, dst, which, j):
        return remote(
            src.at[j], dst.at[0],
            hand_send.at[which, RING + j], hand_recv.at[which, 0], same_pipe(next_base + j),
        )

    def hand_start(src, dst, which):
        for copy in hand_copies(src, dst, which):
            copy.start()

        @pl.when(yy == RING - 1)
        def _():
            for j in range(RING):
                hand_over_copy(src, dst, which, j).start()

        dst[yy + 1] = src[yy]

    def hand_recv_wait(src, dst, which):
        for copy in hand_copies(src, dst, which):
            copy.wait_recv()
        hand_over_copy(src, dst, which, 0).wait_recv()

    def hand_send_wait(src, dst, which):
        for copy in hand_copies(src, dst, which):
            copy.wait_send()

        @pl.when(yy == RING - 1)
        def _():
            for j in range(RING):
                hand_over_copy(src, dst, which, j).wait_send()

    def halves(held, cols):
        b = [held[i, :, cols].astype(F32) for i in range(5)]
        low = lax.broadcasted_iota(jnp.int32, b[0].shape, 0) < BLOCK
        turned = [pltpu.roll(b[i], BLOCK, 0) for i in (0, 2, 4)]
        return (
            b[1] + jnp.where(low, turned[0], turned[1]),
            b[3] + jnp.where(low, turned[1], turned[2]),
        )

    def ag_copies(bufs, which, k, stage):
        dim = ORDERS[k][stage]
        index = tuple(
            slice(None) if d in ORDERS[k][:stage] else at[d] for d in range(3)
        )
        return [
            remote(
                bufs[k].at[index], bufs[k].at[index],
                ag_send.at[which, k, stage, off], ag_recv.at[which, k, stage, off],
                peer(dim, off),
            )
            for off in OFFS
        ]

    def ag_start(bufs, which, k, stage):
        for copy in ag_copies(bufs, which, k, stage):
            copy.start()

    def ag_recv_wait(bufs, which, k, stage):
        for copy in ag_copies(bufs, which, k, stage):
            copy.wait_recv()

    def ag_send_wait(bufs, which):
        for k in range(3):
            for stage in range(3):
                for copy in ag_copies(bufs, which, k, stage):
                    copy.wait_send()

    def group(k):
        return slice(STARTS[k], STARTS[k] + FEATS[k])

    def tile_info():
        info = g2[yy, xx, zz, :, FEATS[2] :].astype(F32)
        return info, info[:, 4:5] + info[:, 5:6]

    def make_scaled():
        _, chance = tile_info()
        for k in range(3):
            rows = jnp.concatenate([up_tile[0, :, group(k)], up_tile[1, :, group(k)]], axis=0)
            ss[k][yy, xx, zz] = (chance * rows).astype(BF16)
            ag_start(ss, 1, k, 0)

    def go_on(bufs, which, stage):
        for k in range(3):
            ag_recv_wait(bufs, which, k, stage - 1)
            ag_start(bufs, which, k, stage)

    hand_start(bn, hn, 0)
    row_copies[3].wait()
    for q in range(RING):
        bu[q] = pick(grad_out, quarter(q)).astype(BF16)
    hand_start(bu, hu, 1)
    for copy in weight_copies:
        copy.start()
    hand_recv_wait(bn, hn, 0)
    for k in range(3):
        tile = halves(hn, slice(STARTS[k], STARTS[k] + WIDTHS[k]))
        gs[k][yy, xx, zz] = jnp.concatenate(tile, axis=0).astype(BF16)

        @pl.when(pipe == 1)
        def _(k=k):
            ag_start(gs, 0, k, 0)

    hand_recv_wait(bu, hu, 1)
    for k in range(3):
        tile = halves(hu, group(k))
        for h in range(2):
            up_tile[h, :, group(k)] = tile[h]

    @pl.when(pipe == 1)
    def _():
        make_scaled()
        for stage in (1, 2):
            go_on(gs, 0, stage)
            go_on(ss, 1, stage)
        pl.semaphore_signal(
            go_sem, inc=1, device_id=other_pipe(me), device_id_type=MESH
        )

    @pl.when(pipe == 0)
    def _():
        pl.semaphore_wait(go_sem, 1)
        for k in range(3):
            ag_start(gs, 0, k, 0)
        for stage in (1, 2):
            go_on(gs, 0, stage)

    for copy in weight_copies:
        copy.wait()

    def rows_of(bufs, k, q):
        return bufs[k][q, :, :, :, : FEATS[k]].reshape(quartets * ROWS, FEATS[k])

    def columns(k, q):
        return slice(q * QUARTER + STARTS[k], q * QUARTER + STARTS[k] + FEATS[k])

    for k in range(3):
        ag_recv_wait(gs, 0, k, 2)
        gate_sum = None
        up_sum = None
        for q in range(RING):
            rows = rows_of(gs, k, q)
            gate_part = contract_last(rows, wg[:, columns(k, q)])
            up_part = contract_last(rows, wu[:, columns(k, q)])
            gate_sum = gate_part if gate_sum is None else gate_sum + gate_part
            up_sum = up_part if up_sum is None else up_sum + up_part
        if k == 0:
            acc[0] = gate_sum
            acc[1] = up_sum
        else:
            acc[0] += gate_sum
            acc[1] += up_sum

    def above_copies():
        return [
            remote(
                new_tile, above.at[slot], ab_send.at[slot], ab_recv.at[slot],
                other_pipe(base + yy),
            )
            for slot, base in ((2, prev_base), (1, quartet * RING), (0, next_base))
        ]

    @pl.when(pipe == 0)
    def _():
        for copy in above_copies():
            copy.wait_recv()
        info, _ = tile_info()

        def shifted(cols):
            own = [above[1, h, :, cols].astype(F32) for h in range(2)]
            ends = [above[0, 1, :, cols].astype(F32), above[2, 0, :, cols].astype(F32)]
            turned = [pltpu.roll(v, BLOCK, 0) for v in (ends[0], own[0], own[1], ends[1])]
            low = lax.broadcasted_iota(jnp.int32, own[0].shape, 0) < BLOCK
            return [
                (
                    jnp.where(low, turned[h], turned[h + 1]),
                    own[h],
                    jnp.where(low, turned[h + 1], turned[h + 2]),
                )
                for h in range(2)
            ]

        ids = shifted(slice(QUARTER, QUARTER + EXTRA))
        weights = []
        for h in range(2):
            mine = info[8 * h : 8 * h + 8, 6:8]
            weights.append(
                [
                    1.0
                    - jnp.minimum(
                        jnp.abs(one[:, 6:7] - mine[:, 0:1]) + jnp.abs(one[:, 7:8] - mine[:, 1:2]),
                        1.0,
                    )
                    for one in ids[h]
                ]
            )
        for k in range(3):
            for h, rows in enumerate(shifted(group(k))):
                w = weights[h]
                value = (1.0 - w[0] - w[1] - w[2]) * up_tile[h, :, group(k)]
                for part, one in zip(w, rows):
                    value += part * one
                up_tile[h, :, group(k)] = value
        make_scaled()
        for stage in (1, 2):
            go_on(ss, 1, stage)

    for k in range(3):
        ag_recv_wait(ss, 1, k, 2)
        grad_sum = None
        for q in range(RING):
            part = contract_last(rows_of(ss, k, q), wd[:, columns(k, q)])
            grad_sum = part if grad_sum is None else grad_sum + part
        if k == 0:
            acc[2] = grad_sum
        else:
            acc[2] += grad_sum

    gate_pre = acc[0]
    up_value = acc[1]
    hidden_grad = acc[2]
    sigma = jax.nn.sigmoid(gate_pre)
    activated = gate_pre * sigma
    slope = sigma * (1.0 + gate_pre * (1.0 - sigma))
    hidden = (activated * up_value).astype(BF16)
    row_part = jnp.sum(hidden_grad * hidden.astype(F32), axis=1, keepdims=True)
    gg = (hidden_grad * up_value * slope).astype(BF16)
    ug = (hidden_grad * activated).astype(BF16)
    dot_part = jnp.sum(
        gg.astype(F32) * gate_pre + ug.astype(F32) * up_value, axis=1, keepdims=True
    )
    extra = g2[0, :, :, :, FEATS[2] :].reshape(quartets * ROWS, EXTRA).astype(F32)
    weight = row_part * (extra[:, 0:1] + extra[:, 1:2])
    lane = lax.broadcasted_iota(jnp.int32, (quartets * ROWS, EXTRA), 1)
    row_lanes = jnp.zeros((quartets * ROWS, EXTRA), F32)
    for i, value in enumerate(hi_lo(row_part) + hi_lo(dot_part)):
        row_lanes = jnp.where(lane == i, value, row_lanes)
    row_lanes = row_lanes.astype(BF16).reshape(RING, RING, ROWS, EXTRA)

    def rs_copies(k, stage):
        order = ORDERS[k]
        dim = order[stage]
        src = (rs, a0, a1)[stage][k]
        dst = (rb0, rb1, rb2)[stage][k]
        left = [d for d in range(3) if d not in order[:stage]]
        copies = []
        for off in OFFS:
            index = tuple(ring_index(d, off) if d == dim else slice(None) for d in left)
            copies.append(
                remote(
                    src.at[index], dst.at[off - 1],
                    rs_send.at[k, stage, off], rs_recv.at[k, stage, off], peer(dim, off),
                )
            )
        return copies

    def rs_start(k, stage):
        for copy in rs_copies(k, stage):
            copy.start()

    def rs_sum(k, stage):
        for copy in rs_copies(k, stage):
            copy.wait_recv()
        order = ORDERS[k]
        dim = order[stage]
        src = (rs, a0, a1)[stage][k]
        got = (rb0, rb1, rb2)[stage][k]
        left = [d for d in range(3) if d not in order[:stage]]
        index = tuple(at[d] if d == dim else slice(None) for d in left)
        return (src[index].astype(F32) + got[0].astype(F32)) + (
            got[1].astype(F32) + got[2].astype(F32)
        )

    srb[0, yy] = jnp.zeros((2 * RING, QUARTER + EXTRA), F32)
    for k in range(3):
        for q in range(RING):
            part = jnp.dot(gg, wg[:, columns(k, q)], preferred_element_type=F32) + jnp.dot(
                ug, wu[:, columns(k, q)], preferred_element_type=F32
            )
            shape = (RING, RING, ROWS, FEATS[k])
            rs[k][q, :, :, :, : FEATS[k]] = part.astype(BF16).reshape(shape)
            if k == 2:
                rs[k][q, :, :, :, FEATS[k] :] = row_lanes
            rows = rows_of(gs, k, q).astype(F32)
            srb[0, yy, 2 * q : 2 * q + 1, group(k)] = jnp.sum(part * rows, axis=0, keepdims=True)
            srb[0, yy, 2 * q + 1 : 2 * q + 2, group(k)] = jnp.sum(
                weight * rows, axis=0, keepdims=True
            )
        rs_start(k, 0)

    def st_copies(stage):
        here = srb.at[stage, at[stage]]
        return [
            remote(
                here, here, st_send.at[stage, off], st_recv.at[stage, off], peer(stage, off)
            )
            for off in OFFS
        ]

    def st_sum(stage):
        for copy in st_copies(stage):
            copy.wait()
        return (srb[stage, 0] + srb[stage, 1]) + (srb[stage, 2] + srb[stage, 3])

    for copy in st_copies(0):
        copy.start()
    turned = [value.astype(F32).T.astype(BF16) for value in (gg, ug, hidden)]
    for q in range(RING):
        for k in range(3):
            normed = rows_of(gs, k, q)
            gate_o[:, columns(k, q)] = jnp.dot(turned[0], normed, preferred_element_type=F32)
            up_o[:, columns(k, q)] = jnp.dot(turned[1], normed, preferred_element_type=F32)
            down_o[:, columns(k, q)] = jnp.dot(
                turned[2], rows_of(ss, k, q), preferred_element_type=F32
            )
    for stage in (0, 1):
        for k in range(3):
            (a0, a1)[stage][k][...] = rs_sum(k, stage).astype(BF16)
            rs_start(k, stage + 1)
        srb[stage + 1, at[stage + 1]] = st_sum(stage)
        for copy in st_copies(stage + 1):
            copy.start()

    sums = [rs_sum(k, 2) for k in range(3)]
    info, chance = tile_info()
    spare = sums[2][:, FEATS[2] :]
    logit_grad = (spare[:, 0:1] + spare[:, 1:2]) * (1.0 - chance)
    mean = (spare[:, 2:3] + spare[:, 3:4]) / float(RING * QUARTER)
    scale = info[:, 2:3] + info[:, 3:4]
    for k in range(3):
        gain_row = gain_q[yy, :, group(k)]
        hat = gs[k][yy, xx, zz, :, : FEATS[k]].astype(F32) / gain_row
        delta = scale * (sums[k][:, : FEATS[k]] * gain_row - hat * mean)
        delta = delta + logit_grad * router_q[yy, :, group(k)]
        for h in range(2):
            half = delta[8 * h : 8 * h + 8]
            new_tile[h, :, group(k)] = (up_tile[h, :, group(k)] + half).astype(BF16)
    for h in range(2):
        new_tile[h, :, QUARTER:] = info[8 * h : 8 * h + 8].astype(BF16)

    @pl.when(pipe == 1)
    def _():
        for copy in above_copies():
            copy.start()

    def back_copies():
        return [
            remote(
                new_tile, u.at[yy, pl.ds(0, 2)], un_send.at[off], un_recv.at[off], peer(0, off)
            )
            for off in OFFS
        ]

    def back_over_copy(q):
        return remote(
            new_tile, u.at[q, pl.ds(2, 2)], un_send.at[0], un_recv.at[RING + q],
            same_pipe(prev_last),
        )

    for copy in back_copies():
        copy.start()
    back_over_copy(yy).start()
    u[yy, 0:2] = new_tile[...]
    st_o[...] = st_sum(2)
    for copy in back_copies():
        copy.wait_recv()

    @pl.when(yy == RING - 1)
    def _():
        for q in range(RING):
            back_over_copy(q).wait_recv()

    upper = lax.div(yy, 2)
    odd = lax.rem(yy, 2) == 1

    def owned(q, cols):
        a = u[q, upper, :, cols].astype(F32)
        b = u[q, upper + 1, :, cols].astype(F32)
        low = lax.broadcasted_iota(jnp.int32, a.shape, 0) < BLOCK
        turned = jnp.where(low, pltpu.roll(a, BLOCK, 0), pltpu.roll(b, BLOCK, 0))
        return jnp.where(odd, turned, a)

    ids = owned(0, slice(QUARTER, QUARTER + EXTRA))
    valid = jnp.abs(ids[:, 7:8] - me.astype(F32)) < 0.5
    which = jnp.broadcast_to(jnp.where(valid, ids[:, 6:7], -1.0), (2 * BLOCK, EXTRA))
    for q in range(RING):
        new_o[q, :, :QUARTER] = owned(q, slice(0, QUARTER)).astype(BF16)
        new_o[q, :, QUARTER:] = which.astype(BF16)

    def nb_copy():
        return remote(new_o, nb, nb_send, nb_recv, other_pipe(me))

    @pl.when(pipe == 1)
    def _():
        nb_copy().start()
        nb_o[...] = new_o[...]

    @pl.when(pipe == 0)
    def _():
        nb_copy().wait_recv()
        nb_o[...] = nb[...]

    hand_send_wait(bn, hn, 0)
    hand_send_wait(bu, hu, 1)
    ag_send_wait(gs, 0)
    ag_send_wait(ss, 1)
    for k in range(3):
        for stage in range(3):
            for copy in rs_copies(k, stage):
                copy.wait_send()
    for copy in back_copies():
        copy.wait_send()
    back_over_copy(yy).wait_send()

    @pl.when(pipe == 1)
    def _():
        for copy in above_copies():
            copy.wait_send()
        nb_copy().wait_send()


def communicate(route_blocks, route_dest, saved, grad_out, gain, w_router, wg, wu, wd):
    ff = wg.shape[1]
    rows = RING * RING * ROWS
    width = QUARTER + EXTRA
    vmem = pl.BlockSpec(memory_space=pltpu.VMEM)
    smem = pl.BlockSpec(memory_space=pltpu.SMEM)
    hbm = pl.BlockSpec(memory_space=pl.ANY)
    cube = (RING, RING, RING, ROWS)
    out_shape = (
        [pltpu.VMEM((ff, grad_out.shape[1]), F32)] * 3
        + [pltpu.VMEM((RING, 8, width), BF16)] * 2
        + [pltpu.VMEM((8, width), F32)]
    )
    dma = pltpu.SemaphoreType.DMA
    scratch = (
        [pltpu.VMEM(grad_out.shape, BF16)] * 2
        + [pltpu.VMEM(gain.shape, F32), pltpu.VMEM(w_router.shape, BF16)]
        + [pltpu.VMEM((RING, 1, QUARTER), F32)] * 2
        + [pltpu.VMEM((RING, 8, width), BF16), pltpu.VMEM((RING, 8, QUARTER), BF16)]
        + [pltpu.VMEM((5, 8, width), BF16), pltpu.VMEM((5, 8, QUARTER), BF16)]
        + [pltpu.VMEM((2, 8, QUARTER), F32), pltpu.VMEM((2, 8, width), BF16)]
        + [pltpu.VMEM((3, 2, 8, width), BF16)]
        + [pltpu.VMEM(cube + (w,), BF16) for w in WIDTHS]
        + [pltpu.VMEM(cube + (w,), BF16) for w in FEATS]
        + [pltpu.VMEM(cube + (w,), BF16) for w in WIDTHS]
        + [pltpu.VMEM((3, RING, RING, ROWS, w), BF16) for w in WIDTHS]
        + [pltpu.VMEM((RING, RING, ROWS, w), BF16) for w in WIDTHS]
        + [pltpu.VMEM((3, RING, ROWS, w), BF16) for w in WIDTHS]
        + [pltpu.VMEM((RING, ROWS, w), BF16) for w in WIDTHS]
        + [pltpu.VMEM((3, ROWS, w), BF16) for w in WIDTHS]
        + [pltpu.VMEM((RING, 4, 8, width), BF16)]
        + [pltpu.VMEM((RING, 8, width), BF16)]
        + [pltpu.VMEM((3, RING, 8, width), F32)]
        + [pltpu.VMEM((3, rows, ff), F32)]
        + [pltpu.VMEM(wg.shape[1:], BF16)] * 3
        + [dma((2, 8)), dma((2, 4))]
        + [dma((2, 3, 3, 4)), dma((2, 3, 3, 4))]
        + [dma((3, 3, 4)), dma((3, 3, 4))]
        + [dma((3, 4)), dma((3, 4))]
        + [dma((4,)), dma((8,))]
        + [dma((3,)), dma((3,))]
        + [dma, dma]
        + [dma((13,)), pltpu.SemaphoreType.REGULAR]
    )
    return pl.pallas_call(
        step_kernel,
        out_shape=out_shape,
        in_specs=[smem] * 2 + [hbm] * 7,
        out_specs=[vmem] * 6,
        scratch_shapes=scratch,
        compiler_params=pltpu.CompilerParams(
            collective_id=0, has_side_effects=True, vmem_limit_bytes=50 * 1024 * 1024
        ),
        name="routed_step",
    )(route_blocks, route_dest, saved, grad_out, gain, w_router, wg, wu, wd)


def finish_kernel(
    gate, up, down, grad_hbm, nb, fresh, stats, gain,
    out_inputs, out_gate, out_up, out_down, out_gain, out_router,
    grad_out, outcome, sem,
):
    load = pltpu.make_async_copy(grad_hbm, grad_out, sem.at[0])
    load.start()
    copies = [
        pltpu.make_async_copy(src, dst.at[0], sem.at[1 + i])
        for i, (src, dst) in enumerate(((gate, out_gate), (up, out_up), (down, out_down)))
    ]
    for copy in copies:
        copy.start()
    for q in range(RING):
        cols = slice(q * QUARTER, (q + 1) * QUARTER)
        out_gain[:, cols] = stats[2 * q : 2 * q + 1, :QUARTER] / gain[:, cols]
        out_router[:, cols] = stats[2 * q + 1 : 2 * q + 2, :QUARTER] / gain[:, cols]
    low = lax.broadcasted_iota(jnp.int32, (2 * BLOCK, QUARTER), 0) < BLOCK
    half = jnp.where(lax.broadcasted_iota(jnp.int32, (2 * BLOCK, 1), 0) < BLOCK, 0.0, 1.0)
    load.wait()
    for q in range(RING):
        cols = slice(q * QUARTER, (q + 1) * QUARTER)
        patterns = []
        for ref in (nb, fresh):
            new_rows = ref[q, :, :QUARTER].astype(F32)
            turned = pltpu.roll(new_rows, BLOCK, 0)
            which = ref[q, :, QUARTER:].astype(F32)
            patterns.append((which[0:1, 0:1], jnp.where(low, new_rows, turned)))
            patterns.append((which[BLOCK : BLOCK + 1, 0:1], jnp.where(low, turned, new_rows)))
        for i in range(grad_out.shape[0] // 8):
            block = half + float(2 * i)
            value = grad_out[8 * i : 8 * i + 8, cols].astype(F32)
            for which, pattern in patterns:
                value = jnp.where(block == which, pattern, value)
            outcome[8 * i : 8 * i + 8, cols] = value.astype(BF16)
    store = pltpu.make_async_copy(outcome, out_inputs.at[0], sem.at[4])
    store.start()
    for copy in copies + [store]:
        copy.wait()


def finish(gate, up, down, grad_out, nb, fresh, stats, gain):
    tok_rows, model_dim = grad_out.shape
    ff = gate.shape[0]
    shape = jax.ShapeDtypeStruct
    vmem = pl.BlockSpec(memory_space=pltpu.VMEM)
    hbm = pl.BlockSpec(memory_space=pl.ANY)
    return pl.pallas_call(
        finish_kernel,
        out_shape=[shape((1, tok_rows, model_dim), BF16)]
        + [shape((1, ff, model_dim), F32)] * 3
        + [shape((1, model_dim), F32)] * 2,
        in_specs=[vmem] * 3 + [hbm] + [vmem] * 4,
        out_specs=[hbm] * 4 + [vmem] * 2,
        scratch_shapes=[pltpu.VMEM(grad_out.shape, BF16)] * 2
        + [pltpu.SemaphoreType.DMA((5,))],
        compiler_params=pltpu.CompilerParams(vmem_limit_bytes=8 * 1024 * 1024),
        name="finish",
    )(gate, up, down, grad_out, nb, fresh, stats, gain)


def on_device(saved, grad_out, route_blocks, route_dest, gain, w_router, w_gate, w_up, w_down):
    gate, up, down, nb, fresh, stats = communicate(
        route_blocks, route_dest, saved, grad_out, gain, w_router, w_gate, w_up, w_down
    )
    return tuple(finish(gate, up, down, grad_out, nb, fresh, stats, gain))


def solution(mesh):
    in_specs = (
        P("pipe", "ctx", None),
        P("ctx", None),
        P("pipe", "ctx", None),
        P("pipe", "ctx", None),
        P("pipe", None),
        P("pipe", None),
        P("pipe", "ctx", None),
        P("pipe", "ctx", None),
        P("pipe", "ctx", None),
    )
    out_specs = (
        P("pipe", "ctx", None),
        P("pipe", "ctx", None),
        P("pipe", "ctx", None),
        P("pipe", "ctx", None),
        P("pipe", None),
        P("pipe", None),
    )
    return jax.shard_map(
        on_device, mesh=mesh, in_specs=in_specs, out_specs=out_specs, check_vma=False
    )
```

```python
import jax
import jax.numpy as jnp
from jax import lax
from jax.experimental import pallas as pl
from jax.experimental.pallas import tpu as pltpu
from jax.sharding import PartitionSpec as P

BLOCK = 4
EPSILON = 1e-05
RING = 4
OFFS = (1, 2, 3)
QUARTER = 1024
EXTRA = 128
WIDTHS = (384, 384, 384)
FEATS = (384, 384, 256)
STARTS = (0, 384, 768)
ROWS = 16
ALONG = (0, 1, 2)
PLANES = ((1, 2), (0, 2), (0, 1))
STEPS = tuple((i, j) for i in range(RING) for j in range(RING) if (i, j) != (0, 0))
F32 = jnp.float32
BF16 = jnp.bfloat16
MESH = pl.DeviceIdType.MESH


def contract_last(left_side, right_side):
    return lax.dot_general(
        left_side, right_side, (((1,), (1,)), ((), ())), preferred_element_type=F32
    )


def hi_lo(value):
    hi = value.astype(BF16).astype(F32)
    return hi, value - hi


def step_kernel(
    blocks, targets, saved_hbm, grad_hbm, gain_hbm, router_hbm, wg_hbm, wu_hbm, wd_hbm,
    gate_o, up_o, down_o, nb_o, new_o, st_o,
    saved, grad_out, gain, router_row, gain_q, router_q, bn, bu, hn, hu, up_tile, new_tile,
    above, g0, g1, g2, s0, s1, s2, r0, r1, r2,
    rb00, rb01, rb02, a00, a01, a02, rb10, rb11, rb12,
    u, nb, srb, acc, wg, wu, wd,
    hand_send, hand_recv, ag_send, ag_recv, rs_send, rs_recv, st_send, st_recv,
    un_send, un_recv, ab_send, ab_recv, nb_send, nb_recv, local_sem, go_sem,
):
    pipe = lax.axis_index("pipe")
    me = lax.axis_index("ctx")
    yy = lax.rem(me, RING)
    quartet = lax.div(me, RING)
    zz = lax.rem(quartet, RING)
    xx = lax.div(quartet, RING)
    at = (yy, xx, zz)
    quartets = RING * RING
    next_base = lax.rem(quartet + 1, quartets) * RING
    prev_base = lax.rem(quartet + quartets - 1, quartets) * RING
    prev_last = prev_base + RING - 1

    def ring_index(dim, off):
        return lax.rem(at[dim] + RING - off, RING)

    def peer(dim, off):
        pos = list(at)
        pos[dim] = ring_index(dim, off)
        return {"pipe": pipe, "ctx": pos[1] * 16 + pos[2] * 4 + pos[0]}

    def plane_peer(k, step):
        pos = list(at)
        for dim, off in zip(PLANES[k], step):
            pos[dim] = ring_index(dim, off)
        return {"pipe": pipe, "ctx": pos[1] * 16 + pos[2] * 4 + pos[0]}

    def same_pipe(ctx):
        return {"pipe": pipe, "ctx": ctx}

    def other_pipe(ctx):
        return {"pipe": 1 - pipe, "ctx": ctx}

    def remote(src, dst, send, recv, device):
        return pltpu.make_async_remote_copy(
            src_ref=src, dst_ref=dst, send_sem=send, recv_sem=recv,
            device_id=device, device_id_type=MESH,
        )

    gs, ss, rs = (g0, g1, g2), (s0, s1, s2), (r0, r1, r2)
    rb0, rb1, a0 = (rb00, rb01, rb02), (rb10, rb11, rb12), (a00, a01, a02)
    sb0 = (rb00, rb01, rb02.at[:, :, :, :, : FEATS[2]])
    sb1 = (rb10, rb11, rb12.at[:, :, : FEATS[2]])

    barrier = pltpu.get_barrier_semaphore()

    def greet(device):
        pl.semaphore_signal(barrier, inc=1, device_id=device, device_id_type=MESH)

    row_copies = [
        pltpu.make_async_copy(src, dst, local_sem.at[9 + i])
        for i, (src, dst) in enumerate(
            (
                (saved_hbm.at[0], saved),
                (gain_hbm, gain),
                (router_hbm, router_row),
                (grad_hbm, grad_out),
            )
        )
    ]
    weight_copies = [
        pltpu.make_async_copy(src.at[0], dst, local_sem.at[i])
        for i, (src, dst) in enumerate(((wg_hbm, wg), (wu_hbm, wu), (wd_hbm, wd)))
    ]
    for copy in row_copies:
        copy.start()
    for dim in range(3):
        for off in OFFS:
            greet(peer(dim, off))
        for step in STEPS:
            if step[0] and step[1]:
                greet(plane_peer(dim, step))
    for base in (prev_base, quartet * RING, next_base):
        greet(other_pipe(base + yy))
    greet(same_pipe(prev_last))

    @pl.when(yy == RING - 1)
    def _():
        for j in range(RING):
            greet(same_pipe(next_base + j))

    kept = targets[0, 0, 0] == me
    keep_block = jnp.where(kept, blocks[0, 0, 0], blocks[0, 0, 1])
    hand_block = jnp.where(kept, blocks[0, 0, 1], blocks[0, 0, 0])
    handed = jnp.where(kept, targets[0, 0, 1], targets[0, 0, 0]) >= 0
    first_rows = lax.broadcasted_iota(jnp.int32, (2 * BLOCK, 1), 0) < BLOCK
    mask = jnp.where(
        first_rows, jnp.where(kept, 1.0, 0.0).astype(F32), jnp.where(handed, 1.0, 0.0).astype(F32)
    )
    block_id = jnp.where(first_rows, keep_block, hand_block)
    row_in_block = lax.rem(lax.broadcasted_iota(jnp.int32, (2 * BLOCK, 1), 0), BLOCK)
    tokens = lax.broadcasted_iota(jnp.int32, (2 * BLOCK, saved.shape[0]), 1)
    chosen = jnp.where(tokens == block_id * BLOCK + row_in_block, mask, 0.0).astype(BF16)

    def pick(array, cols):
        return jnp.dot(chosen, array[:, cols], preferred_element_type=F32)

    def quarter(q):
        return slice(q * QUARTER, (q + 1) * QUARTER)

    for copy in row_copies[:3]:
        copy.wait()
    squares = jnp.zeros((2 * BLOCK, 1), F32)
    logits = jnp.zeros((2 * BLOCK, 1), F32)
    picked = []
    for q in range(RING):
        rows = pick(saved, quarter(q))
        picked.append(rows)
        gain_q[q] = gain[:, quarter(q)]
        router_q[q] = router_row[:, quarter(q)].astype(F32)
        squares += jnp.sum(rows * rows, axis=1, keepdims=True)
        logits += jnp.sum(rows * router_q[q], axis=1, keepdims=True)
    inverse = lax.rsqrt(squares / float(RING * QUARTER) + EPSILON)
    router = jax.nn.sigmoid(logits)
    lane = lax.broadcasted_iota(jnp.int32, (2 * BLOCK, EXTRA), 1)
    extra = jnp.zeros((2 * BLOCK, EXTRA), F32)
    for i, value in enumerate(
        hi_lo((1.0 - router) / inverse)
        + hi_lo(inverse)
        + hi_lo(router)
        + (block_id.astype(F32), me.astype(F32))
    ):
        extra = jnp.where(lane == i, value * mask, extra)
    for q in range(RING):
        bn[q, :, :QUARTER] = (picked[q] * inverse * gain_q[q]).astype(BF16)
        bn[q, :, QUARTER:] = extra.astype(BF16)
    pl.semaphore_wait(barrier, 40 + RING * lax.div(yy, RING - 1))

    def hand_copies(src, dst, which):
        return [
            remote(
                src.at[ring_index(0, off)], dst.at[yy + 1],
                hand_send.at[which, off], hand_recv.at[which, off], peer(0, off),
            )
            for off in OFFS
        ]

    def hand_over_copy(src, dst, which, j):
        return remote(
            src.at[j], dst.at[0],
            hand_send.at[which, RING + j], hand_recv.at[which, 0], same_pipe(next_base + j),
        )

    def hand_start(src, dst, which):
        for copy in hand_copies(src, dst, which):
            copy.start()

        @pl.when(yy == RING - 1)
        def _():
            for j in range(RING):
                hand_over_copy(src, dst, which, j).start()

        dst[yy + 1] = src[yy]

    def hand_recv_wait(src, dst, which):
        for copy in hand_copies(src, dst, which):
            copy.wait_recv()
        hand_over_copy(src, dst, which, 0).wait_recv()

    def hand_send_wait(src, dst, which):
        for copy in hand_copies(src, dst, which):
            copy.wait_send()

        @pl.when(yy == RING - 1)
        def _():
            for j in range(RING):
                hand_over_copy(src, dst, which, j).wait_send()

    def halves(held, cols):
        b = [held[i, :, cols].astype(F32) for i in range(5)]
        low = lax.broadcasted_iota(jnp.int32, b[0].shape, 0) < BLOCK
        turned = [pltpu.roll(b[i], BLOCK, 0) for i in (0, 2, 4)]
        return (
            b[1] + jnp.where(low, turned[0], turned[1]),
            b[3] + jnp.where(low, turned[1], turned[2]),
        )

    def ag_copies(bufs, which, k, stage):
        if stage == 0:
            tile = bufs[k].at[yy, xx, zz]
            return [
                remote(
                    tile, tile, ag_send.at[which, k, 0], ag_recv.at[which, k, 0],
                    plane_peer(k, step),
                )
                for step in STEPS
            ]
        index = tuple(at[d] if d == ALONG[k] else slice(None) for d in range(3))
        tiles = bufs[k].at[index]
        return [
            remote(
                tiles, tiles, ag_send.at[which, k, 1], ag_recv.at[which, k, 1],
                peer(ALONG[k], off),
            )
            for off in OFFS
        ]

    def ag_start(bufs, which, k, stage):
        for copy in ag_copies(bufs, which, k, stage):
            copy.start()

    def ag_all(bufs, which, k, stage):
        if stage == 0:
            ref = (rb1, sb1)[which][k]
        else:
            ref = (rb0, sb0)[which][k]
        return remote(
            ref, ref, ag_send.at[which, k, stage], ag_recv.at[which, k, stage],
            peer(ALONG[k], 1),
        )

    def ag_recv_wait(bufs, which, k, stage):
        ag_all(bufs, which, k, stage).wait_recv()

    def ag_send_wait(bufs, which):
        for k in range(3):
            for stage in range(2):
                ag_all(bufs, which, k, stage).wait_send()

    def group(k):
        return slice(STARTS[k], STARTS[k] + FEATS[k])

    def tile_info():
        info = g2[yy, xx, zz, :, FEATS[2] :].astype(F32)
        return info, info[:, 4:5] + info[:, 5:6]

    def make_scaled():
        _, chance = tile_info()
        for k in range(3):
            rows = jnp.concatenate([up_tile[0, :, group(k)], up_tile[1, :, group(k)]], axis=0)
            ss[k][yy, xx, zz] = (chance * rows).astype(BF16)
            ag_start(ss, 1, k, 0)

    def go_on(bufs, which):
        for k in range(3):
            ag_recv_wait(bufs, which, k, 0)
            ag_start(bufs, which, k, 1)

    hand_start(bn, hn, 0)
    row_copies[3].wait()
    for q in range(RING):
        bu[q] = pick(grad_out, quarter(q)).astype(BF16)
    hand_start(bu, hu, 1)
    for copy in weight_copies:
        copy.start()
    hand_recv_wait(bn, hn, 0)
    for k in range(3):
        tile = halves(hn, slice(STARTS[k], STARTS[k] + WIDTHS[k]))
        gs[k][yy, xx, zz] = jnp.concatenate(tile, axis=0).astype(BF16)

        @pl.when(pipe == 1)
        def _(k=k):
            ag_start(gs, 0, k, 0)

    hand_recv_wait(bu, hu, 1)
    for k in range(3):
        tile = halves(hu, group(k))
        for h in range(2):
            up_tile[h, :, group(k)] = tile[h]

    @pl.when(pipe == 1)
    def _():
        make_scaled()
        go_on(gs, 0)
        go_on(ss, 1)
        pl.semaphore_signal(
            go_sem, inc=1, device_id=other_pipe(me), device_id_type=MESH
        )

    @pl.when(pipe == 0)
    def _():
        pl.semaphore_wait(go_sem, 1)
        for k in range(3):
            ag_start(gs, 0, k, 0)
        go_on(gs, 0)

    for copy in weight_copies:
        copy.wait()

    def rows_of(bufs, k, q):
        return bufs[k][q, :, :, :, : FEATS[k]].reshape(quartets * ROWS, FEATS[k])

    def columns(k, q):
        return slice(q * QUARTER + STARTS[k], q * QUARTER + STARTS[k] + FEATS[k])

    for k in range(3):
        ag_recv_wait(gs, 0, k, 1)
        gate_sum = None
        up_sum = None
        for q in range(RING):
            rows = rows_of(gs, k, q)
            gate_part = contract_last(rows, wg[:, columns(k, q)])
            up_part = contract_last(rows, wu[:, columns(k, q)])
            gate_sum = gate_part if gate_sum is None else gate_sum + gate_part
            up_sum = up_part if up_sum is None else up_sum + up_part
        if k == 0:
            acc[0] = gate_sum
            acc[1] = up_sum
        else:
            acc[0] += gate_sum
            acc[1] += up_sum

    gate_pre = acc[0]
    sigma = jax.nn.sigmoid(gate_pre)
    activated = gate_pre * sigma
    acc[3] = activated
    acc[4] = acc[1] * sigma * (1.0 + gate_pre * (1.0 - sigma))

    def above_copies():
        return [
            remote(
                new_tile, above.at[slot], ab_send.at[slot], ab_recv.at[slot],
                other_pipe(base + yy),
            )
            for slot, base in ((2, prev_base), (1, quartet * RING), (0, next_base))
        ]

    @pl.when(pipe == 0)
    def _():
        for copy in above_copies():
            copy.wait_recv()
        info, _ = tile_info()

        def shifted(cols):
            own = [above[1, h, :, cols].astype(F32) for h in range(2)]
            ends = [above[0, 1, :, cols].astype(F32), above[2, 0, :, cols].astype(F32)]
            turned = [pltpu.roll(v, BLOCK, 0) for v in (ends[0], own[0], own[1], ends[1])]
            low = lax.broadcasted_iota(jnp.int32, own[0].shape, 0) < BLOCK
            return [
                (
                    jnp.where(low, turned[h], turned[h + 1]),
                    own[h],
                    jnp.where(low, turned[h + 1], turned[h + 2]),
                )
                for h in range(2)
            ]

        ids = shifted(slice(QUARTER, QUARTER + EXTRA))
        weights = []
        for h in range(2):
            mine = info[8 * h : 8 * h + 8, 6:8]
            weights.append(
                [
                    1.0
                    - jnp.minimum(
                        jnp.abs(one[:, 6:7] - mine[:, 0:1]) + jnp.abs(one[:, 7:8] - mine[:, 1:2]),
                        1.0,
                    )
                    for one in ids[h]
                ]
            )
        for k in range(3):
            for h, rows in enumerate(shifted(group(k))):
                w = weights[h]
                value = (1.0 - w[0] - w[1] - w[2]) * up_tile[h, :, group(k)]
                for part, one in zip(w, rows):
                    value += part * one
                up_tile[h, :, group(k)] = value
        make_scaled()
        go_on(ss, 1)

    for k in range(3):
        ag_recv_wait(ss, 1, k, 1)
        grad_sum = None
        for q in range(RING):
            part = contract_last(rows_of(ss, k, q), wd[:, columns(k, q)])
            grad_sum = part if grad_sum is None else grad_sum + part
        if k == 0:
            acc[2] = grad_sum
        else:
            acc[2] += grad_sum

    gate_pre = acc[0]
    up_value = acc[1]
    hidden_grad = acc[2]
    activated = acc[3]
    hidden = (activated * up_value).astype(BF16)
    row_part = jnp.sum(hidden_grad * hidden.astype(F32), axis=1, keepdims=True)
    gg = (hidden_grad * acc[4]).astype(BF16)
    ug = (hidden_grad * activated).astype(BF16)
    dot_part = jnp.sum(
        gg.astype(F32) * gate_pre + ug.astype(F32) * up_value, axis=1, keepdims=True
    )
    extra = g2[0, :, :, :, FEATS[2] :].reshape(quartets * ROWS, EXTRA).astype(F32)
    lane = lax.broadcasted_iota(jnp.int32, (quartets * ROWS, EXTRA), 1)
    row_lanes = jnp.zeros((quartets * ROWS, EXTRA), F32)
    for i, value in enumerate(hi_lo(row_part) + hi_lo(dot_part)):
        row_lanes = jnp.where(lane == i, value, row_lanes)
    row_lanes = row_lanes.astype(BF16).reshape(RING, RING, ROWS, EXTRA)

    def rs_copies(k, stage):
        if stage == 0:
            copies = []
            for off in OFFS:
                index = tuple(
                    ring_index(d, off) if d == ALONG[k] else slice(None) for d in range(3)
                )
                copies.append(
                    remote(
                        rs[k].at[index], rb0[k].at[off - 1], rs_send.at[k, 0], rs_recv.at[k, 0],
                        peer(ALONG[k], off),
                    )
                )
            return copies
        return [
            remote(
                a0[k].at[tuple(ring_index(d, off) for d, off in zip(PLANES[k], step))],
                rb1[k].at[i], rs_send.at[k, 1], rs_recv.at[k, 1], plane_peer(k, step),
            )
            for i, step in enumerate(STEPS)
        ]

    def rs_start(k, stage):
        for copy in rs_copies(k, stage):
            copy.start()

    def rs_all(k, stage):
        ref = (rb0, rb1)[stage][k]
        return remote(
            ref, ref, rs_send.at[k, stage], rs_recv.at[k, stage], peer(ALONG[k], 1)
        )

    def rs_sum(k, stage):
        rs_all(k, stage).wait_recv()
        if stage == 0:
            index = tuple(at[d] if d == ALONG[k] else slice(None) for d in range(3))
            parts = [rs[k][index]] + [rb0[k][i] for i in range(3)]
        else:
            own = a0[k][tuple(at[d] for d in PLANES[k])]
            parts = [own] + [rb1[k][i] for i in range(len(STEPS))]
        parts = [part.astype(F32) for part in parts]
        while len(parts) > 1:
            parts = [parts[i] + parts[i + 1] for i in range(0, len(parts), 2)]
        return parts[0]

    srb[0, yy] = jnp.zeros((2 * RING, QUARTER + EXTRA), F32)
    for k in range(3):
        for q in range(RING):
            part = jnp.dot(gg, wg[:, columns(k, q)], preferred_element_type=F32) + jnp.dot(
                ug, wu[:, columns(k, q)], preferred_element_type=F32
            )
            shape = (RING, RING, ROWS, FEATS[k])
            rs[k][q, :, :, :, : FEATS[k]] = part.astype(BF16).reshape(shape)
            if k == 2:
                rs[k][q, :, :, :, FEATS[k] :] = row_lanes
        rs_start(k, 0)

    def st_copies(stage):
        here = srb.at[stage, at[stage]]
        return [
            remote(
                here, here, st_send.at[stage, off], st_recv.at[stage, off], peer(stage, off)
            )
            for off in OFFS
        ]

    def st_sum(stage):
        for copy in st_copies(stage):
            copy.wait()
        return (srb[stage, 0] + srb[stage, 1]) + (srb[stage, 2] + srb[stage, 3])

    turned = [value.astype(F32).T.astype(BF16) for value in (gg, ug, hidden)]
    weight_hi, weight_lo = hi_lo(row_part * (extra[:, 0:1] + extra[:, 1:2]))
    lane = lax.broadcasted_iota(jnp.int32, (quartets * ROWS, EXTRA), 1)
    weights = jnp.where(lane == 0, weight_hi, jnp.where(lane == 1, weight_lo, 0.0))
    weights = weights.T[0:16].astype(BF16)
    for q in range(RING):
        for k in range(3):
            normed = rows_of(gs, k, q)
            gate_o[:, columns(k, q)] = jnp.dot(turned[0], normed, preferred_element_type=F32)
            up_o[:, columns(k, q)] = jnp.dot(turned[1], normed, preferred_element_type=F32)
            down_o[:, columns(k, q)] = jnp.dot(
                turned[2], rows_of(ss, k, q), preferred_element_type=F32
            )
            srb[0, yy, 2 * q : 2 * q + 1, group(k)] = jnp.sum(
                gate_o[:, columns(k, q)] * wg[:, columns(k, q)].astype(F32)
                + up_o[:, columns(k, q)] * wu[:, columns(k, q)].astype(F32),
                axis=0,
                keepdims=True,
            )
            router_sums = jnp.dot(weights, normed, preferred_element_type=F32)
            srb[0, yy, 2 * q + 1 : 2 * q + 2, group(k)] = router_sums[0:1] + router_sums[1:2]
    for copy in st_copies(0):
        copy.start()
    hand_send_wait(bn, hn, 0)
    hand_send_wait(bu, hu, 1)
    ag_send_wait(gs, 0)
    ag_send_wait(ss, 1)
    for k in range(3):
        a0[k][...] = rs_sum(k, 0).astype(BF16)
        rs_start(k, 1)
    srb[1, xx] = st_sum(0)
    for copy in st_copies(1):
        copy.start()

    sums = [rs_sum(k, 1) for k in range(3)]
    srb[2, zz] = st_sum(1)
    for copy in st_copies(2):
        copy.start()
    info, chance = tile_info()
    spare = sums[2][:, FEATS[2] :]
    logit_grad = (spare[:, 0:1] + spare[:, 1:2]) * (1.0 - chance)
    mean = (spare[:, 2:3] + spare[:, 3:4]) / float(RING * QUARTER)
    scale = info[:, 2:3] + info[:, 3:4]
    for k in range(3):
        gain_row = gain_q[yy, :, group(k)]
        hat = gs[k][yy, xx, zz, :, : FEATS[k]].astype(F32) / gain_row
        delta = scale * (sums[k][:, : FEATS[k]] * gain_row - hat * mean)
        delta = delta + logit_grad * router_q[yy, :, group(k)]
        for h in range(2):
            half = delta[8 * h : 8 * h + 8]
            new_tile[h, :, group(k)] = (up_tile[h, :, group(k)] + half).astype(BF16)
    for h in range(2):
        new_tile[h, :, QUARTER:] = info[8 * h : 8 * h + 8].astype(BF16)

    @pl.when(pipe == 1)
    def _():
        for copy in above_copies():
            copy.start()

    def back_copies():
        return [
            remote(
                new_tile, u.at[yy, pl.ds(0, 2)], un_send.at[off], un_recv.at[off], peer(0, off)
            )
            for off in OFFS
        ]

    def back_over_copy(q):
        return remote(
            new_tile, u.at[q, pl.ds(2, 2)], un_send.at[0], un_recv.at[RING + q],
            same_pipe(prev_last),
        )

    for copy in back_copies():
        copy.start()
    back_over_copy(yy).start()
    u[yy, 0:2] = new_tile[...]
    st_o[...] = st_sum(2)
    for k in range(3):
        for stage in range(2):
            rs_all(k, stage).wait_send()
    for copy in back_copies():
        copy.wait_recv()

    @pl.when(yy == RING - 1)
    def _():
        for q in range(RING):
            back_over_copy(q).wait_recv()

    upper = lax.div(yy, 2)
    odd = lax.rem(yy, 2) == 1

    def owned(q, cols):
        a = u[q, upper, :, cols].astype(F32)
        b = u[q, upper + 1, :, cols].astype(F32)
        low = lax.broadcasted_iota(jnp.int32, a.shape, 0) < BLOCK
        turned = jnp.where(low, pltpu.roll(a, BLOCK, 0), pltpu.roll(b, BLOCK, 0))
        return jnp.where(odd, turned, a)

    ids = owned(0, slice(QUARTER, QUARTER + EXTRA))
    valid = jnp.abs(ids[:, 7:8] - me.astype(F32)) < 0.5
    which = jnp.broadcast_to(jnp.where(valid, ids[:, 6:7], -1.0), (2 * BLOCK, EXTRA))
    for q in range(RING):
        new_o[q, :, :QUARTER] = owned(q, slice(0, QUARTER)).astype(BF16)
        new_o[q, :, QUARTER:] = which.astype(BF16)

    def nb_copy():
        return remote(new_o, nb, nb_send, nb_recv, other_pipe(me))

    @pl.when(pipe == 1)
    def _():
        nb_copy().start()
        nb_o[...] = new_o[...]

    @pl.when(pipe == 0)
    def _():
        nb_copy().wait_recv()
        nb_o[...] = nb[...]

    for copy in back_copies():
        copy.wait_send()
    back_over_copy(yy).wait_send()

    @pl.when(pipe == 1)
    def _():
        for copy in above_copies():
            copy.wait_send()
        nb_copy().wait_send()


def communicate(route_blocks, route_dest, saved, grad_out, gain, w_router, wg, wu, wd):
    ff = wg.shape[1]
    rows = RING * RING * ROWS
    width = QUARTER + EXTRA
    vmem = pl.BlockSpec(memory_space=pltpu.VMEM)
    smem = pl.BlockSpec(memory_space=pltpu.SMEM)
    hbm = pl.BlockSpec(memory_space=pl.ANY)
    cube = (RING, RING, RING, ROWS)
    out_shape = (
        [pltpu.VMEM((ff, grad_out.shape[1]), F32)] * 3
        + [pltpu.VMEM((RING, 8, width), BF16)] * 2
        + [pltpu.VMEM((8, width), F32)]
    )
    dma = pltpu.SemaphoreType.DMA
    scratch = (
        [pltpu.VMEM(grad_out.shape, BF16)] * 2
        + [pltpu.VMEM(gain.shape, F32), pltpu.VMEM(w_router.shape, BF16)]
        + [pltpu.VMEM((RING, 1, QUARTER), F32)] * 2
        + [pltpu.VMEM((RING, 8, width), BF16), pltpu.VMEM((RING, 8, QUARTER), BF16)]
        + [pltpu.VMEM((5, 8, width), BF16), pltpu.VMEM((5, 8, QUARTER), BF16)]
        + [pltpu.VMEM((2, 8, QUARTER), F32), pltpu.VMEM((2, 8, width), BF16)]
        + [pltpu.VMEM((3, 2, 8, width), BF16)]
        + [pltpu.VMEM(cube + (w,), BF16) for w in WIDTHS]
        + [pltpu.VMEM(cube + (w,), BF16) for w in FEATS]
        + [pltpu.VMEM(cube + (w,), BF16) for w in WIDTHS]
        + [pltpu.VMEM((3, RING, RING, ROWS, w), BF16) for w in WIDTHS]
        + [pltpu.VMEM((RING, RING, ROWS, w), BF16) for w in WIDTHS]
        + [pltpu.VMEM((len(STEPS), ROWS, w), BF16) for w in WIDTHS]
        + [pltpu.VMEM((RING, 4, 8, width), BF16)]
        + [pltpu.VMEM((RING, 8, width), BF16)]
        + [pltpu.VMEM((3, RING, 8, width), F32)]
        + [pltpu.VMEM((5, rows, ff), F32)]
        + [pltpu.VMEM(wg.shape[1:], BF16)] * 3
        + [dma((2, 8)), dma((2, 4))]
        + [dma((2, 3, 2)), dma((2, 3, 2))]
        + [dma((3, 2)), dma((3, 2))]
        + [dma((3, 4)), dma((3, 4))]
        + [dma((4,)), dma((8,))]
        + [dma((3,)), dma((3,))]
        + [dma, dma]
        + [dma((13,)), pltpu.SemaphoreType.REGULAR]
    )
    return pl.pallas_call(
        step_kernel,
        out_shape=out_shape,
        in_specs=[smem] * 2 + [hbm] * 7,
        out_specs=[vmem] * 6,
        scratch_shapes=scratch,
        compiler_params=pltpu.CompilerParams(
            collective_id=0, has_side_effects=True, vmem_limit_bytes=50 * 1024 * 1024
        ),
        name="routed_step",
    )(route_blocks, route_dest, saved, grad_out, gain, w_router, wg, wu, wd)


def finish_kernel(
    gate, up, down, grad_hbm, nb, fresh, stats, gain,
    out_inputs, out_gate, out_up, out_down, out_gain, out_router,
    grad_out, outcome, sem,
):
    load = pltpu.make_async_copy(grad_hbm, grad_out, sem.at[0])
    load.start()
    copies = [
        pltpu.make_async_copy(src, dst.at[0], sem.at[1 + i])
        for i, (src, dst) in enumerate(((gate, out_gate), (up, out_up), (down, out_down)))
    ]
    for copy in copies:
        copy.start()
    for q in range(RING):
        cols = slice(q * QUARTER, (q + 1) * QUARTER)
        out_gain[:, cols] = stats[2 * q : 2 * q + 1, :QUARTER] / gain[:, cols]
        out_router[:, cols] = stats[2 * q + 1 : 2 * q + 2, :QUARTER] / gain[:, cols]
    low = lax.broadcasted_iota(jnp.int32, (2 * BLOCK, QUARTER), 0) < BLOCK
    half = jnp.where(lax.broadcasted_iota(jnp.int32, (2 * BLOCK, 1), 0) < BLOCK, 0.0, 1.0)
    load.wait()
    for q in range(RING):
        cols = slice(q * QUARTER, (q + 1) * QUARTER)
        patterns = []
        for ref in (nb, fresh):
            new_rows = ref[q, :, :QUARTER].astype(F32)
            turned = pltpu.roll(new_rows, BLOCK, 0)
            which = ref[q, :, QUARTER:].astype(F32)
            patterns.append((which[0:1, 0:1], jnp.where(low, new_rows, turned)))
            patterns.append((which[BLOCK : BLOCK + 1, 0:1], jnp.where(low, turned, new_rows)))
        for i in range(grad_out.shape[0] // 8):
            block = half + float(2 * i)
            value = grad_out[8 * i : 8 * i + 8, cols].astype(F32)
            for which, pattern in patterns:
                value = jnp.where(block == which, pattern, value)
            outcome[8 * i : 8 * i + 8, cols] = value.astype(BF16)
    store = pltpu.make_async_copy(outcome, out_inputs.at[0], sem.at[4])
    store.start()
    for copy in copies + [store]:
        copy.wait()


def finish(gate, up, down, grad_out, nb, fresh, stats, gain):
    tok_rows, model_dim = grad_out.shape
    ff = gate.shape[0]
    shape = jax.ShapeDtypeStruct
    vmem = pl.BlockSpec(memory_space=pltpu.VMEM)
    hbm = pl.BlockSpec(memory_space=pl.ANY)
    return pl.pallas_call(
        finish_kernel,
        out_shape=[shape((1, tok_rows, model_dim), BF16)]
        + [shape((1, ff, model_dim), F32)] * 3
        + [shape((1, model_dim), F32)] * 2,
        in_specs=[vmem] * 3 + [hbm] + [vmem] * 4,
        out_specs=[hbm] * 4 + [vmem] * 2,
        scratch_shapes=[pltpu.VMEM(grad_out.shape, BF16)] * 2
        + [pltpu.SemaphoreType.DMA((5,))],
        compiler_params=pltpu.CompilerParams(vmem_limit_bytes=8 * 1024 * 1024),
        name="finish",
    )(gate, up, down, grad_out, nb, fresh, stats, gain)


def on_device(saved, grad_out, route_blocks, route_dest, gain, w_router, w_gate, w_up, w_down):
    gate, up, down, nb, fresh, stats = communicate(
        route_blocks, route_dest, saved, grad_out, gain, w_router, w_gate, w_up, w_down
    )
    return tuple(finish(gate, up, down, grad_out, nb, fresh, stats, gain))


def solution(mesh):
    in_specs = (
        P("pipe", "ctx", None),
        P("ctx", None),
        P("pipe", "ctx", None),
        P("pipe", "ctx", None),
        P("pipe", None),
        P("pipe", None),
        P("pipe", "ctx", None),
        P("pipe", "ctx", None),
        P("pipe", "ctx", None),
    )
    out_specs = (
        P("pipe", "ctx", None),
        P("pipe", "ctx", None),
        P("pipe", "ctx", None),
        P("pipe", "ctx", None),
        P("pipe", None),
        P("pipe", None),
    )
    return jax.shard_map(
        on_device, mesh=mesh, in_specs=in_specs, out_specs=out_specs, check_vma=False
    )
```

```python
import jax
import jax.numpy as jnp
from jax import lax
from jax.experimental import pallas as pl
from jax.experimental.pallas import tpu as pltpu
from jax.sharding import PartitionSpec as P

BLOCK = 4
EPSILON = 1e-05
RING = 4
OFFS = (1, 2, 3)
QUARTER = 1024
EXTRA = 128
WIDTHS = (384, 384, 384)
FEATS = (384, 384, 256)
STARTS = (0, 384, 768)
ROWS = 16
PARTS = 4
ALONG = (0, 1, 2)
PLANES = ((1, 2), (0, 2), (0, 1))
STEPS = tuple((i, j) for i in range(RING) for j in range(RING) if (i, j) != (0, 0))
F32 = jnp.float32
BF16 = jnp.bfloat16
MESH = pl.DeviceIdType.MESH


def contract_last(left_side, right_side):
    return lax.dot_general(
        left_side, right_side, (((1,), (1,)), ((), ())), preferred_element_type=F32
    )


def hi_lo(value):
    hi = value.astype(BF16).astype(F32)
    return hi, value - hi


def step_kernel(
    blocks_hbm, targets_hbm, saved_hbm, grad_hbm, gain_hbm, router_hbm, wg_hbm, wu_hbm, wd_hbm,
    gate_o, up_o, down_o, nb_o, new_o, st_o,
    blocks, targets, saved, grad_out, gain, router_row, gain_q, router_q, bn, bu, hn, hu, up_tile, new_tile,
    above, g0, g1, g2, s0, s1, s2, r0, r1, r2,
    rb00, rb01, rb02, a00, a01, a02, rb10, rb11, rb12,
    u, nb, srb, acc, wg, wu, wd,
    hand_send, hand_recv, ag_send, ag_recv, rs_send, rs_recv, st_send, st_recv,
    un_send, un_recv, ab_send, ab_recv, nb_send, nb_recv, local_sem, go_sem,
):
    pipe = lax.axis_index("pipe")
    me = lax.axis_index("ctx")
    yy = lax.rem(me, RING)
    quartet = lax.div(me, RING)
    zz = lax.rem(quartet, RING)
    xx = lax.div(quartet, RING)
    at = (yy, xx, zz)
    quartets = RING * RING
    next_base = lax.rem(quartet + 1, quartets) * RING
    prev_base = lax.rem(quartet + quartets - 1, quartets) * RING
    prev_last = prev_base + RING - 1

    ring = [[one] + [lax.rem(one + RING - off, RING) for off in OFFS] for one in at]
    share = [[one * stride for one in row] for row, stride in zip(ring, (1, 16, 4))]

    def ring_index(dim, off):
        return ring[dim][off]

    def peer(dim, off):
        parts = [row[0] for row in share]
        parts[dim] = share[dim][off]
        return {"pipe": pipe, "ctx": parts[0] + parts[1] + parts[2]}

    def plane_peer(k, step):
        parts = [row[0] for row in share]
        for dim, off in zip(PLANES[k], step):
            parts[dim] = share[dim][off]
        return {"pipe": pipe, "ctx": parts[0] + parts[1] + parts[2]}

    def same_pipe(ctx):
        return {"pipe": pipe, "ctx": ctx}

    def other_pipe(ctx):
        return {"pipe": 1 - pipe, "ctx": ctx}

    def remote(src, dst, send, recv, device):
        return pltpu.make_async_remote_copy(
            src_ref=src, dst_ref=dst, send_sem=send, recv_sem=recv,
            device_id=device, device_id_type=MESH,
        )

    gs, ss, rs = (g0, g1, g2), (s0, s1, s2), (r0, r1, r2)
    rb0, rb1, a0 = (rb00, rb01, rb02), (rb10, rb11, rb12), (a00, a01, a02)
    sb0 = (rb00, rb01, rb02.at[:, :, :, :, : FEATS[2]])
    sb1 = (rb10, rb11, rb12.at[:, :, : FEATS[2]])

    barrier = pltpu.get_barrier_semaphore()

    def greet(device):
        pl.semaphore_signal(barrier, inc=1, device_id=device, device_id_type=MESH)

    row_copies = [
        pltpu.make_async_copy(src, dst, local_sem.at[3 + i])
        for i, (src, dst) in enumerate(
            (
                (blocks_hbm, blocks),
                (targets_hbm, targets),
                (gain_hbm, gain),
                (router_hbm, router_row),
                (grad_hbm, grad_out),
            )
        )
    ]
    weight_copies = [
        pltpu.make_async_copy(src.at[0], dst, local_sem.at[i])
        for i, (src, dst) in enumerate(((wg_hbm, wg), (wu_hbm, wu), (wd_hbm, wd)))
    ]
    saved_copies = [
        pltpu.make_async_copy(
            saved_hbm.at[0, :, pl.ds(q * QUARTER, QUARTER)],
            saved.at[:, pl.ds(q * QUARTER, QUARTER)],
            local_sem.at[8 + q],
        )
        for q in range(RING)
    ]
    for copy in row_copies[:2] + saved_copies + row_copies[2:]:
        copy.start()
    for dim in range(3):
        for off in OFFS:
            greet(peer(dim, off))
        for step in STEPS:
            if step[0] and step[1]:
                greet(plane_peer(dim, step))
    for base in (prev_base, quartet * RING, next_base):
        greet(other_pipe(base + yy))
    greet(same_pipe(prev_last))

    @pl.when(yy == RING - 1)
    def _():
        for j in range(RING):
            greet(same_pipe(next_base + j))

    for copy in row_copies[:2]:
        copy.wait()
    kept = targets[0, 0, 0] == me
    keep_block = jnp.where(kept, blocks[0, 0, 0], blocks[0, 0, 1])
    hand_block = jnp.where(kept, blocks[0, 0, 1], blocks[0, 0, 0])
    handed = jnp.where(kept, targets[0, 0, 1], targets[0, 0, 0]) >= 0
    first_rows = lax.broadcasted_iota(jnp.int32, (2 * BLOCK, 1), 0) < BLOCK
    mask = jnp.where(
        first_rows, jnp.where(kept, 1.0, 0.0).astype(F32), jnp.where(handed, 1.0, 0.0).astype(F32)
    )
    block_id = jnp.where(first_rows, keep_block, hand_block)
    row_in_block = lax.rem(lax.broadcasted_iota(jnp.int32, (2 * BLOCK, 1), 0), BLOCK)
    tokens = lax.broadcasted_iota(jnp.int32, (2 * BLOCK, saved.shape[0]), 1)
    chosen = jnp.where(tokens == block_id * BLOCK + row_in_block, mask, 0.0).astype(BF16)

    def pick(array, cols):
        return jnp.dot(chosen, array[:, cols], preferred_element_type=F32)

    def quarter(q):
        return slice(q * QUARTER, (q + 1) * QUARTER)

    for copy in row_copies[2:4]:
        copy.wait()
    squares = jnp.zeros((2 * BLOCK, 1), F32)
    logits = jnp.zeros((2 * BLOCK, 1), F32)
    picked = []
    for q in range(RING):
        saved_copies[q].wait()
        rows = pick(saved, quarter(q))
        picked.append(rows)
        gain_q[q] = gain[:, quarter(q)]
        router_q[q] = router_row[:, quarter(q)].astype(F32)
        squares += jnp.sum(rows * rows, axis=1, keepdims=True)
        logits += jnp.sum(rows * router_q[q], axis=1, keepdims=True)
    inverse = lax.rsqrt(squares / float(RING * QUARTER) + EPSILON)
    router = jax.nn.sigmoid(logits)
    lane = lax.broadcasted_iota(jnp.int32, (2 * BLOCK, EXTRA), 1)
    extra = jnp.zeros((2 * BLOCK, EXTRA), F32)
    for i, value in enumerate(
        hi_lo((1.0 - router) / inverse)
        + hi_lo(inverse)
        + hi_lo(router)
        + (block_id.astype(F32), me.astype(F32))
    ):
        extra = jnp.where(lane == i, value * mask, extra)
    for q in range(RING):
        bn[q, :, :QUARTER] = (picked[q] * inverse * gain_q[q]).astype(BF16)
        bn[q, :, QUARTER:] = extra.astype(BF16)
    pl.semaphore_wait(barrier, 40 + RING * lax.div(yy, RING - 1))

    def hand_copies(src, dst, which):
        return [
            remote(
                src.at[ring_index(0, off)], dst.at[yy + 1],
                hand_send.at[which, off], hand_recv.at[which, off], peer(0, off),
            )
            for off in OFFS
        ]

    def hand_over_copy(src, dst, which, j):
        return remote(
            src.at[j], dst.at[0],
            hand_send.at[which, RING + j], hand_recv.at[which, 0], same_pipe(next_base + j),
        )

    def hand_start(src, dst, which):
        for copy in hand_copies(src, dst, which):
            copy.start()

        @pl.when(yy == RING - 1)
        def _():
            for j in range(RING):
                hand_over_copy(src, dst, which, j).start()

        dst[yy + 1] = src[yy]

    def hand_recv_wait(src, dst, which):
        for copy in hand_copies(src, dst, which):
            copy.wait_recv()
        hand_over_copy(src, dst, which, 0).wait_recv()

    def hand_send_wait(src, dst, which):
        for copy in hand_copies(src, dst, which):
            copy.wait_send()

        @pl.when(yy == RING - 1)
        def _():
            for j in range(RING):
                hand_over_copy(src, dst, which, j).wait_send()

    def halves(held, cols):
        b = [held[i, :, cols].astype(F32) for i in range(5)]
        low = lax.broadcasted_iota(jnp.int32, b[0].shape, 0) < BLOCK
        turned = [pltpu.roll(b[i], BLOCK, 0) for i in (0, 2, 4)]
        return (
            b[1] + jnp.where(low, turned[0], turned[1]),
            b[3] + jnp.where(low, turned[1], turned[2]),
        )

    def ag_copies(bufs, which, k, stage):
        if stage == 0:
            tile = bufs[k].at[yy, xx, zz]
            return [
                remote(
                    tile, tile, ag_send.at[which, k, 0], ag_recv.at[which, k, 0],
                    plane_peer(k, step),
                )
                for step in STEPS
            ]
        index = tuple(at[d] if d == ALONG[k] else slice(None) for d in range(3))
        tiles = bufs[k].at[index]
        return [
            remote(
                tiles, tiles, ag_send.at[which, k, 1], ag_recv.at[which, k, 1],
                peer(ALONG[k], off),
            )
            for off in OFFS
        ]

    def ag_start(bufs, which, k, stage):
        for copy in ag_copies(bufs, which, k, stage):
            copy.start()

    def ag_all(bufs, which, k, stage):
        if stage == 0:
            ref = (rb1, sb1)[which][k]
        else:
            ref = (rb0, sb0)[which][k]
        return remote(
            ref, ref, ag_send.at[which, k, stage], ag_recv.at[which, k, stage],
            peer(ALONG[k], 1),
        )

    def ag_recv_wait(bufs, which, k, stage):
        ag_all(bufs, which, k, stage).wait_recv()

    def ag_send_wait(bufs, which):
        for k in range(3):
            for stage in range(2):
                ag_all(bufs, which, k, stage).wait_send()

    def group(k):
        return slice(STARTS[k], STARTS[k] + FEATS[k])

    def tile_info():
        info = g2[yy, xx, zz, :, FEATS[2] :].astype(F32)
        return info, info[:, 4:5] + info[:, 5:6]

    def make_scaled():
        _, chance = tile_info()
        for k in range(3):
            rows = jnp.concatenate([up_tile[0, :, group(k)], up_tile[1, :, group(k)]], axis=0)
            ss[k][yy, xx, zz] = (chance * rows).astype(BF16)
            ag_start(ss, 1, k, 0)

    def go_on(bufs, which):
        for k in range(3):
            ag_recv_wait(bufs, which, k, 0)
            ag_start(bufs, which, k, 1)

    hand_start(bn, hn, 0)
    row_copies[4].wait()
    for q in range(RING):
        bu[q] = pick(grad_out, quarter(q)).astype(BF16)
    hand_start(bu, hu, 1)
    for copy in weight_copies:
        copy.start()
    hand_recv_wait(bn, hn, 0)
    for k in range(3):
        tile = halves(hn, slice(STARTS[k], STARTS[k] + WIDTHS[k]))
        gs[k][yy, xx, zz] = jnp.concatenate(tile, axis=0).astype(BF16)

        @pl.when(pipe == 1)
        def _(k=k):
            ag_start(gs, 0, k, 0)

    hand_recv_wait(bu, hu, 1)
    for k in range(3):
        tile = halves(hu, group(k))
        for h in range(2):
            up_tile[h, :, group(k)] = tile[h]

    @pl.when(pipe == 1)
    def _():
        make_scaled()
        go_on(gs, 0)
        go_on(ss, 1)
        pl.semaphore_signal(
            go_sem, inc=1, device_id=other_pipe(me), device_id_type=MESH
        )

    @pl.when(pipe == 0)
    def _():
        pl.semaphore_wait(go_sem, 1)
        for k in range(3):
            ag_start(gs, 0, k, 0)
        go_on(gs, 0)

    for copy in weight_copies:
        copy.wait()

    def rows_of(bufs, k, q):
        return bufs[k][q, :, :, :, : FEATS[k]].reshape(quartets * ROWS, FEATS[k])

    def columns(k, q):
        return slice(q * QUARTER + STARTS[k], q * QUARTER + STARTS[k] + FEATS[k])

    for k in range(3):
        ag_recv_wait(gs, 0, k, 1)
        gate_sum = None
        up_sum = None
        for q in range(RING):
            rows = rows_of(gs, k, q)
            gate_part = contract_last(rows, wg[:, columns(k, q)])
            up_part = contract_last(rows, wu[:, columns(k, q)])
            gate_sum = gate_part if gate_sum is None else gate_sum + gate_part
            up_sum = up_part if up_sum is None else up_sum + up_part
        if k == 0:
            acc[0] = gate_sum
            acc[1] = up_sum
        else:
            acc[0] += gate_sum
            acc[1] += up_sum

    gate_pre = acc[0]
    sigma = jax.nn.sigmoid(gate_pre)
    activated = gate_pre * sigma
    acc[3] = activated
    acc[4] = acc[1] * sigma * (1.0 + gate_pre * (1.0 - sigma))

    def above_copies():
        whole = remote(
            new_tile, above.at[1], ab_send.at[1], ab_recv.at[1], other_pipe(me)
        )
        return [whole] + [
            remote(
                new_tile.at[h], above.at[slot, h], ab_send.at[slot], ab_recv.at[slot],
                other_pipe(base + yy),
            )
            for slot, h, base in ((2, 0, prev_base), (0, 1, next_base))
        ]

    @pl.when(pipe == 0)
    def _():
        for copy in above_copies():
            copy.wait_recv()
        info, _ = tile_info()

        def shifted(cols):
            own = [above[1, h, :, cols].astype(F32) for h in range(2)]
            ends = [above[0, 1, :, cols].astype(F32), above[2, 0, :, cols].astype(F32)]
            turned = [pltpu.roll(v, BLOCK, 0) for v in (ends[0], own[0], own[1], ends[1])]
            low = lax.broadcasted_iota(jnp.int32, own[0].shape, 0) < BLOCK
            return [
                (
                    jnp.where(low, turned[h], turned[h + 1]),
                    own[h],
                    jnp.where(low, turned[h + 1], turned[h + 2]),
                )
                for h in range(2)
            ]

        ids = shifted(slice(QUARTER, QUARTER + EXTRA))
        weights = []
        for h in range(2):
            mine = info[8 * h : 8 * h + 8, 6:8]
            weights.append(
                [
                    1.0
                    - jnp.minimum(
                        jnp.abs(one[:, 6:7] - mine[:, 0:1]) + jnp.abs(one[:, 7:8] - mine[:, 1:2]),
                        1.0,
                    )
                    for one in ids[h]
                ]
            )
        for k in range(3):
            for h, rows in enumerate(shifted(group(k))):
                w = weights[h]
                value = (1.0 - w[0] - w[1] - w[2]) * up_tile[h, :, group(k)]
                for part, one in zip(w, rows):
                    value += part * one
                up_tile[h, :, group(k)] = value
        make_scaled()
        go_on(ss, 1)

    for k in range(3):
        ag_recv_wait(ss, 1, k, 1)
        grad_sum = None
        for q in range(RING):
            part = contract_last(rows_of(ss, k, q), wd[:, columns(k, q)])
            grad_sum = part if grad_sum is None else grad_sum + part
        if k == 0:
            acc[2] = grad_sum
        else:
            acc[2] += grad_sum

    gate_pre = acc[0]
    up_value = acc[1]
    hidden_grad = acc[2]
    activated = acc[3]
    hidden = (activated * up_value).astype(BF16)
    row_part = jnp.sum(hidden_grad * hidden.astype(F32), axis=1, keepdims=True)
    gg = (hidden_grad * acc[4]).astype(BF16)
    ug = (hidden_grad * activated).astype(BF16)
    dot_part = jnp.sum(
        gg.astype(F32) * gate_pre + ug.astype(F32) * up_value, axis=1, keepdims=True
    )
    extra = g2[0, :, :, :, FEATS[2] :].reshape(quartets * ROWS, EXTRA).astype(F32)
    lane = lax.broadcasted_iota(jnp.int32, (quartets * ROWS, EXTRA), 1)
    row_lanes = jnp.zeros((quartets * ROWS, EXTRA), F32)
    for i, value in enumerate(hi_lo(row_part) + hi_lo(dot_part)):
        row_lanes = jnp.where(lane == i, value, row_lanes)
    row_lanes = row_lanes.astype(BF16).reshape(RING, RING, ROWS, EXTRA)

    def rs_copies(k, stage):
        if stage == 0:
            copies = []
            for off in OFFS:
                index = tuple(
                    ring_index(d, off) if d == ALONG[k] else slice(None) for d in range(3)
                )
                copies.append(
                    remote(
                        rs[k].at[index], rb0[k].at[off - 1], rs_send.at[k, 0], rs_recv.at[k, 0],
                        peer(ALONG[k], off),
                    )
                )
            return copies
        return [
            remote(
                a0[k].at[tuple(ring_index(d, off) for d, off in zip(PLANES[k], step))],
                rb1[k].at[i], rs_send.at[k, 1], rs_recv.at[k, 1], plane_peer(k, step),
            )
            for i, step in enumerate(STEPS)
        ]

    def rs_start(k, stage):
        for copy in rs_copies(k, stage):
            copy.start()

    def rs_all(k, stage):
        ref = (rb0, rb1)[stage][k]
        return remote(
            ref, ref, rs_send.at[k, stage], rs_recv.at[k, stage], peer(ALONG[k], 1)
        )

    def rs_sum(k, stage):
        rs_all(k, stage).wait_recv()
        if stage == 0:
            index = tuple(at[d] if d == ALONG[k] else slice(None) for d in range(3))
            parts = [rs[k][index]] + [rb0[k][i] for i in range(3)]
        else:
            own = a0[k][tuple(at[d] for d in PLANES[k])]
            parts = [own] + [rb1[k][i] for i in range(len(STEPS))]
        parts = [part.astype(F32) for part in parts]
        while len(parts) > 1:
            parts = [parts[i] + parts[i + 1] for i in range(0, len(parts), 2)]
        return parts[0]

    srb[0, yy] = jnp.zeros((2 * RING, QUARTER + EXTRA), F32)
    for k in range(3):
        for q in range(RING):
            part = jnp.dot(gg, wg[:, columns(k, q)], preferred_element_type=F32) + jnp.dot(
                ug, wu[:, columns(k, q)], preferred_element_type=F32
            )
            shape = (RING, RING, ROWS, FEATS[k])
            rs[k][q, :, :, :, : FEATS[k]] = part.astype(BF16).reshape(shape)
            if k == 2:
                rs[k][q, :, :, :, FEATS[k] :] = row_lanes
        rs_start(k, 0)

    def st_copies(stage):
        here = srb.at[stage, at[stage]]
        return [
            remote(
                here, here, st_send.at[stage, off], st_recv.at[stage, off], peer(stage, off)
            )
            for off in OFFS
        ]

    def st_sum(stage):
        for copy in st_copies(stage):
            copy.wait()
        return (srb[stage, 0] + srb[stage, 1]) + (srb[stage, 2] + srb[stage, 3])

    turned = [value.astype(F32).T.astype(BF16) for value in (gg, ug, hidden)]
    weight_hi, weight_lo = hi_lo(row_part * (extra[:, 0:1] + extra[:, 1:2]))
    lane = lax.broadcasted_iota(jnp.int32, (quartets * ROWS, EXTRA), 1)
    weights = jnp.where(lane == 0, weight_hi, jnp.where(lane == 1, weight_lo, 0.0))
    weights = weights.T[0:16].astype(BF16)
    for q in range(RING):
        for k in range(3):
            normed = rows_of(gs, k, q)
            gate_o[:, columns(k, q)] = jnp.dot(turned[0], normed, preferred_element_type=F32)
            up_o[:, columns(k, q)] = jnp.dot(turned[1], normed, preferred_element_type=F32)
            down_o[:, columns(k, q)] = jnp.dot(
                turned[2], rows_of(ss, k, q), preferred_element_type=F32
            )
            srb[0, yy, 2 * q : 2 * q + 1, group(k)] = jnp.sum(
                gate_o[:, columns(k, q)] * wg[:, columns(k, q)].astype(F32)
                + up_o[:, columns(k, q)] * wu[:, columns(k, q)].astype(F32),
                axis=0,
                keepdims=True,
            )
            router_sums = jnp.dot(weights, normed, preferred_element_type=F32)
            srb[0, yy, 2 * q + 1 : 2 * q + 2, group(k)] = router_sums[0:1] + router_sums[1:2]
    for copy in st_copies(0):
        copy.start()
    hand_send_wait(bn, hn, 0)
    hand_send_wait(bu, hu, 1)
    ag_send_wait(gs, 0)
    ag_send_wait(ss, 1)
    for k in range(3):
        a0[k][...] = rs_sum(k, 0).astype(BF16)
        rs_start(k, 1)
    srb[1, xx] = st_sum(0)
    for copy in st_copies(1):
        copy.start()

    sums = [rs_sum(k, 1) for k in range(3)]
    info, chance = tile_info()
    spare = sums[2][:, FEATS[2] :]
    logit_grad = (spare[:, 0:1] + spare[:, 1:2]) * (1.0 - chance)
    mean = (spare[:, 2:3] + spare[:, 3:4]) / float(RING * QUARTER)
    scale = info[:, 2:3] + info[:, 3:4]
    for k in range(3):
        gain_row = gain_q[yy, :, group(k)]
        hat = gs[k][yy, xx, zz, :, : FEATS[k]].astype(F32) / gain_row
        delta = scale * (sums[k][:, : FEATS[k]] * gain_row - hat * mean)
        delta = delta + logit_grad * router_q[yy, :, group(k)]
        for h in range(2):
            half = delta[8 * h : 8 * h + 8]
            new_tile[h, :, group(k)] = (up_tile[h, :, group(k)] + half).astype(BF16)
    for h in range(2):
        new_tile[h, :, QUARTER:] = info[8 * h : 8 * h + 8].astype(BF16)

    @pl.when(pipe == 1)
    def _():
        for copy in above_copies():
            copy.start()

    def back_copies():
        return [
            remote(
                new_tile, u.at[yy, pl.ds(0, 2)], un_send.at[off], un_recv.at[off], peer(0, off)
            )
            for off in OFFS
        ]

    def back_over_copy(q):
        return remote(
            new_tile.at[0], u.at[q, 2], un_send.at[0], un_recv.at[RING + q],
            same_pipe(prev_last),
        )

    for copy in back_copies():
        copy.start()
    back_over_copy(yy).start()
    srb[2, zz] = st_sum(1)
    for copy in st_copies(2):
        copy.start()
    u[yy, 0:2] = new_tile[...]
    for k in range(3):
        for stage in range(2):
            rs_all(k, stage).wait_send()
    for copy in back_copies():
        copy.wait_recv()

    @pl.when(yy == RING - 1)
    def _():
        for q in range(RING):
            back_over_copy(q).wait_recv()

    upper = lax.div(yy, 2)
    odd = lax.rem(yy, 2) == 1

    def owned(q, cols):
        a = u[q, upper, :, cols].astype(F32)
        b = u[q, upper + 1, :, cols].astype(F32)
        low = lax.broadcasted_iota(jnp.int32, a.shape, 0) < BLOCK
        turned = jnp.where(low, pltpu.roll(a, BLOCK, 0), pltpu.roll(b, BLOCK, 0))
        return jnp.where(odd, turned, a)

    ids = owned(0, slice(QUARTER, QUARTER + EXTRA))
    valid = jnp.abs(ids[:, 7:8] - me.astype(F32)) < 0.5
    which = jnp.broadcast_to(jnp.where(valid, ids[:, 6:7], -1.0), (2 * BLOCK, EXTRA))
    for q in range(RING):
        new_o[q, :, :QUARTER] = owned(q, slice(0, QUARTER)).astype(BF16)
        new_o[q, :, QUARTER:] = which.astype(BF16)

    st_o[...] = st_sum(2)

    def nb_copy():
        return remote(new_o, nb, nb_send, nb_recv, other_pipe(me))

    @pl.when(pipe == 1)
    def _():
        nb_copy().start()
        nb_o[...] = new_o[...]

    @pl.when(pipe == 0)
    def _():
        nb_copy().wait_recv()
        nb_o[...] = nb[...]

    for copy in back_copies():
        copy.wait_send()
    back_over_copy(yy).wait_send()

    @pl.when(pipe == 1)
    def _():
        for copy in above_copies():
            copy.wait_send()
        nb_copy().wait_send()


def communicate(route_blocks, route_dest, saved, grad_out, gain, w_router, wg, wu, wd):
    ff = wg.shape[1]
    rows = RING * RING * ROWS
    width = QUARTER + EXTRA
    vmem = pl.BlockSpec(memory_space=pltpu.VMEM)
    hbm = pl.BlockSpec(memory_space=pl.ANY)
    cube = (RING, RING, RING, ROWS)
    out_shape = (
        [pltpu.VMEM((ff, grad_out.shape[1]), F32)] * 3
        + [pltpu.VMEM((RING, 8, width), BF16)] * 2
        + [pltpu.VMEM((8, width), F32)]
    )
    dma = pltpu.SemaphoreType.DMA
    scratch = (
        [pltpu.SMEM(route_blocks.shape, jnp.int32)] * 2
        + [pltpu.VMEM(grad_out.shape, BF16)] * 2
        + [pltpu.VMEM(gain.shape, F32), pltpu.VMEM(w_router.shape, BF16)]
        + [pltpu.VMEM((RING, 1, QUARTER), F32)] * 2
        + [pltpu.VMEM((RING, 8, width), BF16), pltpu.VMEM((RING, 8, QUARTER), BF16)]
        + [pltpu.VMEM((5, 8, width), BF16), pltpu.VMEM((5, 8, QUARTER), BF16)]
        + [pltpu.VMEM((2, 8, QUARTER), F32), pltpu.VMEM((2, 8, width), BF16)]
        + [pltpu.VMEM((3, 2, 8, width), BF16)]
        + [pltpu.VMEM(cube + (w,), BF16) for w in WIDTHS]
        + [pltpu.VMEM(cube + (w,), BF16) for w in FEATS]
        + [pltpu.VMEM(cube + (w,), BF16) for w in WIDTHS]
        + [pltpu.VMEM((3, RING, RING, ROWS, w), BF16) for w in WIDTHS]
        + [pltpu.VMEM((RING, RING, ROWS, w), BF16) for w in WIDTHS]
        + [pltpu.VMEM((len(STEPS), ROWS, w), BF16) for w in WIDTHS]
        + [pltpu.VMEM((RING, 3, 8, width), BF16)]
        + [pltpu.VMEM((RING, 8, width), BF16)]
        + [pltpu.VMEM((3, RING, 8, width), F32)]
        + [pltpu.VMEM((5, rows, ff), F32)]
        + [pltpu.VMEM(wg.shape[1:], BF16)] * 3
        + [dma((2, 8)), dma((2, 4))]
        + [dma((2, 3, 2)), dma((2, 3, 2))]
        + [dma((3, 2)), dma((3, 2))]
        + [dma((3, 4)), dma((3, 4))]
        + [dma((4,)), dma((8,))]
        + [dma((3,)), dma((3,))]
        + [dma, dma]
        + [dma((13,)), pltpu.SemaphoreType.REGULAR]
    )
    return pl.pallas_call(
        step_kernel,
        out_shape=out_shape,
        in_specs=[hbm] * 9,
        out_specs=[vmem] * 6,
        scratch_shapes=scratch,
        compiler_params=pltpu.CompilerParams(
            collective_id=0, has_side_effects=True, vmem_limit_bytes=50 * 1024 * 1024
        ),
        name="routed_step",
    )(route_blocks, route_dest, saved, grad_out, gain, w_router, wg, wu, wd)


def finish_kernel(
    gate, up, down, grad_hbm, nb, fresh, stats, gain,
    out_inputs, out_gate, out_up, out_down, out_gain, out_router,
    grad_out, outcome, sem,
):
    load = pltpu.make_async_copy(grad_hbm, grad_out, sem.at[0])
    load.start()
    part = gate.shape[0] // PARTS
    copies = [
        pltpu.make_async_copy(
            src.at[pl.ds(j * part, part)], dst.at[0, pl.ds(j * part, part)],
            sem.at[2 + i * PARTS + j],
        )
        for i, (src, dst) in enumerate(((gate, out_gate), (up, out_up), (down, out_down)))
        for j in range(PARTS)
    ]
    for copy in copies:
        copy.start()
    for q in range(RING):
        cols = slice(q * QUARTER, (q + 1) * QUARTER)
        out_gain[:, cols] = stats[2 * q : 2 * q + 1, :QUARTER] / gain[:, cols]
        out_router[:, cols] = stats[2 * q + 1 : 2 * q + 2, :QUARTER] / gain[:, cols]
    low = lax.broadcasted_iota(jnp.int32, (2 * BLOCK, QUARTER), 0) < BLOCK
    half = jnp.where(lax.broadcasted_iota(jnp.int32, (2 * BLOCK, 1), 0) < BLOCK, 0.0, 1.0)
    load.wait()
    for q in range(RING):
        cols = slice(q * QUARTER, (q + 1) * QUARTER)
        patterns = []
        for ref in (nb, fresh):
            new_rows = ref[q, :, :QUARTER].astype(F32)
            turned = pltpu.roll(new_rows, BLOCK, 0)
            which = ref[q, :, QUARTER:].astype(F32)
            patterns.append((which[0:1, 0:1], jnp.where(low, new_rows, turned)))
            patterns.append((which[BLOCK : BLOCK + 1, 0:1], jnp.where(low, turned, new_rows)))
        for i in range(grad_out.shape[0] // 8):
            block = half + float(2 * i)
            value = grad_out[8 * i : 8 * i + 8, cols].astype(F32)
            for which, pattern in patterns:
                value = jnp.where(block == which, pattern, value)
            outcome[8 * i : 8 * i + 8, cols] = value.astype(BF16)
    store = pltpu.make_async_copy(outcome, out_inputs.at[0], sem.at[1])
    store.start()
    for copy in copies + [store]:
        copy.wait()


def finish(gate, up, down, grad_out, nb, fresh, stats, gain):
    tok_rows, model_dim = grad_out.shape
    ff = gate.shape[0]
    shape = jax.ShapeDtypeStruct
    vmem = pl.BlockSpec(memory_space=pltpu.VMEM)
    hbm = pl.BlockSpec(memory_space=pl.ANY)
    return pl.pallas_call(
        finish_kernel,
        out_shape=[shape((1, tok_rows, model_dim), BF16)]
        + [shape((1, ff, model_dim), F32)] * 3
        + [shape((1, model_dim), F32)] * 2,
        in_specs=[vmem] * 3 + [hbm] + [vmem] * 4,
        out_specs=[hbm] * 4 + [vmem] * 2,
        scratch_shapes=[pltpu.VMEM(grad_out.shape, BF16)] * 2
        + [pltpu.SemaphoreType.DMA((2 + 3 * PARTS,))],
        compiler_params=pltpu.CompilerParams(vmem_limit_bytes=8 * 1024 * 1024),
        name="finish",
    )(gate, up, down, grad_out, nb, fresh, stats, gain)


def on_device(saved, grad_out, route_blocks, route_dest, gain, w_router, w_gate, w_up, w_down):
    gate, up, down, nb, fresh, stats = communicate(
        route_blocks, route_dest, saved, grad_out, gain, w_router, w_gate, w_up, w_down
    )
    return tuple(finish(gate, up, down, grad_out, nb, fresh, stats, gain))


def solution(mesh):
    in_specs = (
        P("pipe", "ctx", None),
        P("ctx", None),
        P("pipe", "ctx", None),
        P("pipe", "ctx", None),
        P("pipe", None),
        P("pipe", None),
        P("pipe", "ctx", None),
        P("pipe", "ctx", None),
        P("pipe", "ctx", None),
    )
    out_specs = (
        P("pipe", "ctx", None),
        P("pipe", "ctx", None),
        P("pipe", "ctx", None),
        P("pipe", "ctx", None),
        P("pipe", None),
        P("pipe", None),
    )
    return jax.shard_map(
        on_device, mesh=mesh, in_specs=in_specs, out_specs=out_specs, check_vma=False
    )
```

```python
import jax
import jax.numpy as jnp
from jax import lax
from jax.experimental import pallas as pl
from jax.experimental.pallas import tpu as pltpu
from jax.sharding import PartitionSpec as P

BLOCK = 4
EPSILON = 1e-05
RING = 4
OFFS = (1, 2, 3)
QUARTER = 1024
EXTRA = 128
WIDTHS = (384, 384, 384)
FEATS = (384, 384, 256)
STARTS = (0, 384, 768)
ROWS = 16
PARTS = 4
ALONG = (0, 1, 2)
PLANES = ((1, 2), (0, 2), (0, 1))
STEPS = tuple((i, j) for i in range(RING) for j in range(RING) if (i, j) != (0, 0))
F32 = jnp.float32
BF16 = jnp.bfloat16
MESH = pl.DeviceIdType.MESH


def contract_last(left_side, right_side):
    return lax.dot_general(
        left_side, right_side, (((1,), (1,)), ((), ())), preferred_element_type=F32
    )


def hi_lo(value):
    hi = value.astype(BF16).astype(F32)
    return hi, value - hi


def step_kernel(
    blocks_hbm, targets_hbm, saved_hbm, grad_hbm, gain_hbm, router_hbm, wg_hbm, wu_hbm, wd_hbm,
    gate_o, up_o, down_o, nb_o, new_o, st_o,
    blocks, targets, saved, grad_out, gain, router_row, gain_q, router_q, bn, bu, hn, hu, up_tile, new_tile,
    above, g0, g1, g2, s0, s1, s2, r0, r1, r2,
    rb00, rb01, rb02, a00, a01, a02, rb10, rb11, rb12,
    u, nb, srb, acc, wg, wu, wd,
    hand_send, hand_recv, ag_send, ag_recv, rs_send, rs_recv, st_send, st_recv,
    un_send, un_recv, ab_send, ab_recv, nb_send, nb_recv, local_sem, go_sem,
):
    pipe = lax.axis_index("pipe")
    me = lax.axis_index("ctx")
    yy = lax.rem(me, RING)
    quartet = lax.div(me, RING)
    zz = lax.rem(quartet, RING)
    xx = lax.div(quartet, RING)
    at = (yy, xx, zz)
    quartets = RING * RING
    next_base = lax.rem(quartet + 1, quartets) * RING
    prev_base = lax.rem(quartet + quartets - 1, quartets) * RING
    prev_last = prev_base + RING - 1

    ring = [[one] + [lax.rem(one + RING - off, RING) for off in OFFS] for one in at]
    share = [[one * stride for one in row] for row, stride in zip(ring, (1, 16, 4))]

    def ring_index(dim, off):
        return ring[dim][off]

    def peer(dim, off):
        parts = [row[0] for row in share]
        parts[dim] = share[dim][off]
        return {"pipe": pipe, "ctx": parts[0] + parts[1] + parts[2]}

    def plane_peer(k, step):
        parts = [row[0] for row in share]
        for dim, off in zip(PLANES[k], step):
            parts[dim] = share[dim][off]
        return {"pipe": pipe, "ctx": parts[0] + parts[1] + parts[2]}

    def same_pipe(ctx):
        return {"pipe": pipe, "ctx": ctx}

    def other_pipe(ctx):
        return {"pipe": 1 - pipe, "ctx": ctx}

    def remote(src, dst, send, recv, device):
        return pltpu.make_async_remote_copy(
            src_ref=src, dst_ref=dst, send_sem=send, recv_sem=recv,
            device_id=device, device_id_type=MESH,
        )

    gs, ss, rs = (g0, g1, g2), (s0, s1, s2), (r0, r1, r2)
    rb0, rb1, a0 = (rb00, rb01, rb02), (rb10, rb11, rb12), (a00, a01, a02)
    sb0 = (rb00, rb01, rb02.at[:, :, :, :, : FEATS[2]])
    sb1 = (rb10, rb11, rb12.at[:, :, : FEATS[2]])

    barrier = pltpu.get_barrier_semaphore()

    def greet(device):
        pl.semaphore_signal(barrier, inc=1, device_id=device, device_id_type=MESH)

    row_copies = [
        pltpu.make_async_copy(src, dst, local_sem.at[3 + i])
        for i, (src, dst) in enumerate(
            (
                (blocks_hbm, blocks),
                (targets_hbm, targets),
                (gain_hbm, gain),
                (router_hbm, router_row),
                (grad_hbm, grad_out),
            )
        )
    ]
    weight_copies = [
        pltpu.make_async_copy(src.at[0], dst, local_sem.at[i])
        for i, (src, dst) in enumerate(((wg_hbm, wg), (wu_hbm, wu), (wd_hbm, wd)))
    ]
    saved_copies = [
        pltpu.make_async_copy(
            saved_hbm.at[0, :, pl.ds(q * QUARTER, QUARTER)],
            saved.at[:, pl.ds(q * QUARTER, QUARTER)],
            local_sem.at[8 + q],
        )
        for q in range(RING)
    ]
    for copy in row_copies[:2] + saved_copies + row_copies[2:]:
        copy.start()
    for dim in range(3):
        for off in OFFS:
            greet(peer(dim, off))
        for step in STEPS:
            if step[0] and step[1]:
                greet(plane_peer(dim, step))
    for base in (prev_base, quartet * RING, next_base):
        greet(other_pipe(base + yy))
    greet(same_pipe(prev_last))

    @pl.when(yy == RING - 1)
    def _():
        for j in range(RING):
            greet(same_pipe(next_base + j))

    for copy in row_copies[:2]:
        copy.wait()
    kept = targets[0, 0, 0] == me
    keep_block = jnp.where(kept, blocks[0, 0, 0], blocks[0, 0, 1])
    hand_block = jnp.where(kept, blocks[0, 0, 1], blocks[0, 0, 0])
    handed = jnp.where(kept, targets[0, 0, 1], targets[0, 0, 0]) >= 0
    first_rows = lax.broadcasted_iota(jnp.int32, (2 * BLOCK, 1), 0) < BLOCK
    mask = jnp.where(
        first_rows, jnp.where(kept, 1.0, 0.0).astype(F32), jnp.where(handed, 1.0, 0.0).astype(F32)
    )
    block_id = jnp.where(first_rows, keep_block, hand_block)
    row_in_block = lax.rem(lax.broadcasted_iota(jnp.int32, (2 * BLOCK, 1), 0), BLOCK)
    tokens = lax.broadcasted_iota(jnp.int32, (2 * BLOCK, saved.shape[0]), 1)
    chosen = jnp.where(tokens == block_id * BLOCK + row_in_block, mask, 0.0).astype(BF16)

    def pick(array, cols):
        return jnp.dot(chosen, array[:, cols], preferred_element_type=F32)

    def quarter(q):
        return slice(q * QUARTER, (q + 1) * QUARTER)

    for copy in row_copies[2:4]:
        copy.wait()
    squares = jnp.zeros((2 * BLOCK, 1), F32)
    logits = jnp.zeros((2 * BLOCK, 1), F32)
    picked = []
    for q in range(RING):
        saved_copies[q].wait()
        rows = pick(saved, quarter(q))
        picked.append(rows)
        gain_q[q] = gain[:, quarter(q)]
        router_q[q] = router_row[:, quarter(q)].astype(F32)
        squares += jnp.sum(rows * rows, axis=1, keepdims=True)
        logits += jnp.sum(rows * router_q[q], axis=1, keepdims=True)
    inverse = lax.rsqrt(squares / float(RING * QUARTER) + EPSILON)
    router = jax.nn.sigmoid(logits)
    lane = lax.broadcasted_iota(jnp.int32, (2 * BLOCK, EXTRA), 1)
    extra = jnp.zeros((2 * BLOCK, EXTRA), F32)
    for i, value in enumerate(
        hi_lo((1.0 - router) / inverse)
        + hi_lo(inverse)
        + hi_lo(router)
        + (block_id.astype(F32), me.astype(F32))
    ):
        extra = jnp.where(lane == i, value * mask, extra)
    for q in range(RING):
        bn[q, :, :QUARTER] = (picked[q] * inverse * gain_q[q]).astype(BF16)
        bn[q, :, QUARTER:] = extra.astype(BF16)
    pl.semaphore_wait(barrier, 40 + RING * lax.div(yy, RING - 1))

    def hand_copies(src, dst, which):
        return [
            remote(
                src.at[ring_index(0, off)], dst.at[yy + 1],
                hand_send.at[which, off], hand_recv.at[which, off], peer(0, off),
            )
            for off in OFFS
        ]

    def hand_over_copy(src, dst, which, j):
        return remote(
            src.at[j], dst.at[0],
            hand_send.at[which, RING + j], hand_recv.at[which, 0], same_pipe(next_base + j),
        )

    def hand_start(src, dst, which):
        for copy in hand_copies(src, dst, which):
            copy.start()

        @pl.when(yy == RING - 1)
        def _():
            for j in range(RING):
                hand_over_copy(src, dst, which, j).start()

        dst[yy + 1] = src[yy]

    def hand_recv_wait(src, dst, which):
        for copy in hand_copies(src, dst, which):
            copy.wait_recv()
        hand_over_copy(src, dst, which, 0).wait_recv()

    def hand_send_wait(src, dst, which):
        for copy in hand_copies(src, dst, which):
            copy.wait_send()

        @pl.when(yy == RING - 1)
        def _():
            for j in range(RING):
                hand_over_copy(src, dst, which, j).wait_send()

    def halves(held, cols):
        b = [held[i, :, cols].astype(F32) for i in range(5)]
        low = lax.broadcasted_iota(jnp.int32, b[0].shape, 0) < BLOCK
        turned = [pltpu.roll(b[i], BLOCK, 0) for i in (0, 2, 4)]
        return (
            b[1] + jnp.where(low, turned[0], turned[1]),
            b[3] + jnp.where(low, turned[1], turned[2]),
        )

    def ag_copies(bufs, which, k, stage):
        if stage == 0:
            tile = bufs[k].at[yy, xx, zz]
            return [
                remote(
                    tile, tile, ag_send.at[which, k, 0], ag_recv.at[which, k, 0],
                    plane_peer(k, step),
                )
                for step in STEPS
            ]
        index = tuple(at[d] if d == ALONG[k] else slice(None) for d in range(3))
        tiles = bufs[k].at[index]
        return [
            remote(
                tiles, tiles, ag_send.at[which, k, 1], ag_recv.at[which, k, 1],
                peer(ALONG[k], off),
            )
            for off in OFFS
        ]

    def ag_start(bufs, which, k, stage):
        for copy in ag_copies(bufs, which, k, stage):
            copy.start()

    def ag_all(bufs, which, k, stage):
        if stage == 0:
            ref = (rb1, sb1)[which][k]
        else:
            ref = (rb0, sb0)[which][k]
        return remote(
            ref, ref, ag_send.at[which, k, stage], ag_recv.at[which, k, stage],
            peer(ALONG[k], 1),
        )

    def ag_recv_wait(bufs, which, k, stage):
        ag_all(bufs, which, k, stage).wait_recv()

    def ag_send_wait(bufs, which):
        for k in range(3):
            for stage in range(2):
                ag_all(bufs, which, k, stage).wait_send()

    def group(k):
        return slice(STARTS[k], STARTS[k] + FEATS[k])

    def tile_info():
        info = g2[yy, xx, zz, :, FEATS[2] :].astype(F32)
        return info, info[:, 4:5] + info[:, 5:6]

    def make_scaled():
        _, chance = tile_info()
        for k in range(3):
            rows = jnp.concatenate([up_tile[0, :, group(k)], up_tile[1, :, group(k)]], axis=0)
            ss[k][yy, xx, zz] = (chance * rows).astype(BF16)
            ag_start(ss, 1, k, 0)

    def go_on(bufs, which):
        for k in range(3):
            ag_recv_wait(bufs, which, k, 0)
            ag_start(bufs, which, k, 1)

    hand_start(bn, hn, 0)
    row_copies[4].wait()
    for q in range(RING):
        bu[q] = pick(grad_out, quarter(q)).astype(BF16)
    hand_start(bu, hu, 1)
    for copy in weight_copies:
        copy.start()
    hand_recv_wait(bn, hn, 0)
    for k in range(3):
        tile = halves(hn, slice(STARTS[k], STARTS[k] + WIDTHS[k]))
        gs[k][yy, xx, zz] = jnp.concatenate(tile, axis=0).astype(BF16)

        @pl.when(pipe == 1)
        def _(k=k):
            ag_start(gs, 0, k, 0)

    hand_recv_wait(bu, hu, 1)
    for k in range(3):
        tile = halves(hu, group(k))
        for h in range(2):
            up_tile[h, :, group(k)] = tile[h]

    @pl.when(pipe == 1)
    def _():
        make_scaled()
        go_on(gs, 0)
        go_on(ss, 1)
        pl.semaphore_signal(
            go_sem, inc=1, device_id=other_pipe(me), device_id_type=MESH
        )

    @pl.when(pipe == 0)
    def _():
        pl.semaphore_wait(go_sem, 1)
        for k in range(3):
            ag_start(gs, 0, k, 0)
        go_on(gs, 0)

    for copy in weight_copies:
        copy.wait()

    def rows_of(bufs, k, q):
        return bufs[k][q, :, :, :, : FEATS[k]].reshape(quartets * ROWS, FEATS[k])

    def columns(k, q):
        return slice(q * QUARTER + STARTS[k], q * QUARTER + STARTS[k] + FEATS[k])

    for k in range(3):
        ag_recv_wait(gs, 0, k, 1)
        gate_sum = None
        up_sum = None
        for q in range(RING):
            rows = rows_of(gs, k, q)
            gate_part = contract_last(rows, wg[:, columns(k, q)])
            up_part = contract_last(rows, wu[:, columns(k, q)])
            gate_sum = gate_part if gate_sum is None else gate_sum + gate_part
            up_sum = up_part if up_sum is None else up_sum + up_part
        if k == 0:
            acc[0] = gate_sum
            acc[1] = up_sum
        else:
            acc[0] += gate_sum
            acc[1] += up_sum

    gate_pre = acc[0]
    sigma = jax.nn.sigmoid(gate_pre)
    activated = gate_pre * sigma
    acc[3] = activated
    acc[4] = acc[1] * sigma * (1.0 + gate_pre * (1.0 - sigma))

    def above_copies():
        whole = remote(
            new_tile, above.at[1], ab_send.at[1], ab_recv.at[1], other_pipe(me)
        )
        return [whole] + [
            remote(
                new_tile.at[h], above.at[slot, h], ab_send.at[slot], ab_recv.at[slot],
                other_pipe(base + yy),
            )
            for slot, h, base in ((2, 0, prev_base), (0, 1, next_base))
        ]

    @pl.when(pipe == 0)
    def _():
        for copy in above_copies():
            copy.wait_recv()
        info, _ = tile_info()

        def shifted(cols):
            own = [above[1, h, :, cols].astype(F32) for h in range(2)]
            ends = [above[0, 1, :, cols].astype(F32), above[2, 0, :, cols].astype(F32)]
            turned = [pltpu.roll(v, BLOCK, 0) for v in (ends[0], own[0], own[1], ends[1])]
            low = lax.broadcasted_iota(jnp.int32, own[0].shape, 0) < BLOCK
            return [
                (
                    jnp.where(low, turned[h], turned[h + 1]),
                    own[h],
                    jnp.where(low, turned[h + 1], turned[h + 2]),
                )
                for h in range(2)
            ]

        ids = shifted(slice(QUARTER, QUARTER + EXTRA))
        weights = []
        for h in range(2):
            mine = info[8 * h : 8 * h + 8, 6:8]
            weights.append(
                [
                    1.0
                    - jnp.minimum(
                        jnp.abs(one[:, 6:7] - mine[:, 0:1]) + jnp.abs(one[:, 7:8] - mine[:, 1:2]),
                        1.0,
                    )
                    for one in ids[h]
                ]
            )
        for k in range(3):
            for h, rows in enumerate(shifted(group(k))):
                w = weights[h]
                value = (1.0 - w[0] - w[1] - w[2]) * up_tile[h, :, group(k)]
                for part, one in zip(w, rows):
                    value += part * one
                up_tile[h, :, group(k)] = value
        make_scaled()
        go_on(ss, 1)

    for k in (2, 0, 1):
        ag_recv_wait(ss, 1, k, 1)
        grad_sum = None
        for q in range(RING):
            part = contract_last(rows_of(ss, k, q), wd[:, columns(k, q)])
            grad_sum = part if grad_sum is None else grad_sum + part
        if k == 2:
            acc[2] = grad_sum
        else:
            acc[2] += grad_sum

    gate_pre = acc[0]
    up_value = acc[1]
    hidden_grad = acc[2]
    activated = acc[3]
    hidden = (activated * up_value).astype(BF16)
    gg = (hidden_grad * acc[4]).astype(BF16)
    ug = (hidden_grad * activated).astype(BF16)
    def rs_copies(k, stage):
        if stage == 0:
            copies = []
            for off in OFFS:
                index = tuple(
                    ring_index(d, off) if d == ALONG[k] else slice(None) for d in range(3)
                )
                copies.append(
                    remote(
                        rs[k].at[index], rb0[k].at[off - 1], rs_send.at[k, 0], rs_recv.at[k, 0],
                        peer(ALONG[k], off),
                    )
                )
            return copies
        return [
            remote(
                a0[k].at[tuple(ring_index(d, off) for d, off in zip(PLANES[k], step))],
                rb1[k].at[i], rs_send.at[k, 1], rs_recv.at[k, 1], plane_peer(k, step),
            )
            for i, step in enumerate(STEPS)
        ]

    def rs_start(k, stage):
        for copy in rs_copies(k, stage):
            copy.start()

    def rs_all(k, stage):
        ref = (rb0, rb1)[stage][k]
        return remote(
            ref, ref, rs_send.at[k, stage], rs_recv.at[k, stage], peer(ALONG[k], 1)
        )

    def rs_sum(k, stage):
        rs_all(k, stage).wait_recv()
        if stage == 0:
            index = tuple(at[d] if d == ALONG[k] else slice(None) for d in range(3))
            parts = [rs[k][index]] + [rb0[k][i] for i in range(3)]
        else:
            own = a0[k][tuple(at[d] for d in PLANES[k])]
            parts = [own] + [rb1[k][i] for i in range(len(STEPS))]
        parts = [part.astype(F32) for part in parts]
        while len(parts) > 1:
            parts = [parts[i] + parts[i + 1] for i in range(0, len(parts), 2)]
        return parts[0]

    srb[0, yy] = jnp.zeros((2 * RING, QUARTER + EXTRA), F32)
    for k in range(3):
        if k == 2:
            row_part = jnp.sum(hidden_grad * hidden.astype(F32), axis=1, keepdims=True)
            dot_part = jnp.sum(
                gg.astype(F32) * gate_pre + ug.astype(F32) * up_value, axis=1, keepdims=True
            )
            extra = g2[0, :, :, :, FEATS[2] :].reshape(quartets * ROWS, EXTRA).astype(F32)
            lane = lax.broadcasted_iota(jnp.int32, (quartets * ROWS, EXTRA), 1)
            row_lanes = jnp.zeros((quartets * ROWS, EXTRA), F32)
            for i, value in enumerate(hi_lo(row_part) + hi_lo(dot_part)):
                row_lanes = jnp.where(lane == i, value, row_lanes)
            row_lanes = row_lanes.astype(BF16).reshape(RING, RING, ROWS, EXTRA)
        for q in range(RING):
            part = jnp.dot(gg, wg[:, columns(k, q)], preferred_element_type=F32) + jnp.dot(
                ug, wu[:, columns(k, q)], preferred_element_type=F32
            )
            shape = (RING, RING, ROWS, FEATS[k])
            rs[k][q, :, :, :, : FEATS[k]] = part.astype(BF16).reshape(shape)
            if k == 2:
                rs[k][q, :, :, :, FEATS[k] :] = row_lanes
        rs_start(k, 0)

    def st_copies(stage):
        here = srb.at[stage, at[stage]]
        return [
            remote(
                here, here, st_send.at[stage, off], st_recv.at[stage, off], peer(stage, off)
            )
            for off in OFFS
        ]

    def st_sum(stage):
        for copy in st_copies(stage):
            copy.wait()
        return (srb[stage, 0] + srb[stage, 1]) + (srb[stage, 2] + srb[stage, 3])

    turned = [value.astype(F32).T.astype(BF16) for value in (gg, ug, hidden)]
    weight_hi, weight_lo = hi_lo(row_part * (extra[:, 0:1] + extra[:, 1:2]))
    lane = lax.broadcasted_iota(jnp.int32, (quartets * ROWS, EXTRA), 1)
    weights = jnp.where(lane == 0, weight_hi, jnp.where(lane == 1, weight_lo, 0.0))
    weights = weights.T[0:16].astype(BF16)
    for q in range(RING):
        for k in range(3):
            normed = rows_of(gs, k, q)
            gate_o[:, columns(k, q)] = jnp.dot(turned[0], normed, preferred_element_type=F32)
            up_o[:, columns(k, q)] = jnp.dot(turned[1], normed, preferred_element_type=F32)
            down_o[:, columns(k, q)] = jnp.dot(
                turned[2], rows_of(ss, k, q), preferred_element_type=F32
            )
            srb[0, yy, 2 * q : 2 * q + 1, group(k)] = jnp.sum(
                gate_o[:, columns(k, q)] * wg[:, columns(k, q)].astype(F32)
                + up_o[:, columns(k, q)] * wu[:, columns(k, q)].astype(F32),
                axis=0,
                keepdims=True,
            )
            router_sums = jnp.dot(weights, normed, preferred_element_type=F32)
            srb[0, yy, 2 * q + 1 : 2 * q + 2, group(k)] = router_sums[0:1] + router_sums[1:2]
    for copy in st_copies(0):
        copy.start()
    hand_send_wait(bn, hn, 0)
    hand_send_wait(bu, hu, 1)
    ag_send_wait(gs, 0)
    ag_send_wait(ss, 1)
    for k in range(3):
        a0[k][...] = rs_sum(k, 0).astype(BF16)
        rs_start(k, 1)
    srb[1, xx] = st_sum(0)
    for copy in st_copies(1):
        copy.start()

    sums = [rs_sum(k, 1) for k in range(3)]
    info, chance = tile_info()
    spare = sums[2][:, FEATS[2] :]
    logit_grad = (spare[:, 0:1] + spare[:, 1:2]) * (1.0 - chance)
    mean = (spare[:, 2:3] + spare[:, 3:4]) / float(RING * QUARTER)
    scale = info[:, 2:3] + info[:, 3:4]
    for k in range(3):
        gain_row = gain_q[yy, :, group(k)]
        hat = gs[k][yy, xx, zz, :, : FEATS[k]].astype(F32) / gain_row
        delta = scale * (sums[k][:, : FEATS[k]] * gain_row - hat * mean)
        delta = delta + logit_grad * router_q[yy, :, group(k)]
        for h in range(2):
            half = delta[8 * h : 8 * h + 8]
            new_tile[h, :, group(k)] = (up_tile[h, :, group(k)] + half).astype(BF16)
    for h in range(2):
        new_tile[h, :, QUARTER:] = info[8 * h : 8 * h + 8].astype(BF16)

    @pl.when(pipe == 1)
    def _():
        for copy in above_copies():
            copy.start()

    def back_copies():
        return [
            remote(
                new_tile, u.at[yy, pl.ds(0, 2)], un_send.at[off], un_recv.at[off], peer(0, off)
            )
            for off in OFFS
        ]

    def back_over_copy(q):
        return remote(
            new_tile.at[0], u.at[q, 2], un_send.at[0], un_recv.at[RING + q],
            same_pipe(prev_last),
        )

    for copy in back_copies():
        copy.start()
    back_over_copy(yy).start()
    srb[2, zz] = st_sum(1)
    for copy in st_copies(2):
        copy.start()
    u[yy, 0:2] = new_tile[...]
    for k in range(3):
        for stage in range(2):
            rs_all(k, stage).wait_send()
    for copy in back_copies():
        copy.wait_recv()

    @pl.when(yy == RING - 1)
    def _():
        for q in range(RING):
            back_over_copy(q).wait_recv()

    upper = lax.div(yy, 2)
    odd = lax.rem(yy, 2) == 1

    def owned(q, cols):
        a = u[q, upper, :, cols].astype(F32)
        b = u[q, upper + 1, :, cols].astype(F32)
        low = lax.broadcasted_iota(jnp.int32, a.shape, 0) < BLOCK
        turned = jnp.where(low, pltpu.roll(a, BLOCK, 0), pltpu.roll(b, BLOCK, 0))
        return jnp.where(odd, turned, a)

    ids = owned(0, slice(QUARTER, QUARTER + EXTRA))
    valid = jnp.abs(ids[:, 7:8] - me.astype(F32)) < 0.5
    which = jnp.broadcast_to(jnp.where(valid, ids[:, 6:7], -1.0), (2 * BLOCK, EXTRA))
    for q in range(RING):
        new_o[q, :, :QUARTER] = owned(q, slice(0, QUARTER)).astype(BF16)
        new_o[q, :, QUARTER:] = which.astype(BF16)

    st_o[...] = st_sum(2)

    def nb_copy():
        return remote(new_o, nb, nb_send, nb_recv, other_pipe(me))

    @pl.when(pipe == 1)
    def _():
        nb_copy().start()
        nb_o[...] = new_o[...]

    @pl.when(pipe == 0)
    def _():
        nb_copy().wait_recv()
        nb_o[...] = nb[...]

    for copy in back_copies():
        copy.wait_send()
    back_over_copy(yy).wait_send()

    @pl.when(pipe == 1)
    def _():
        for copy in above_copies():
            copy.wait_send()
        nb_copy().wait_send()


def communicate(route_blocks, route_dest, saved, grad_out, gain, w_router, wg, wu, wd):
    ff = wg.shape[1]
    rows = RING * RING * ROWS
    width = QUARTER + EXTRA
    vmem = pl.BlockSpec(memory_space=pltpu.VMEM)
    hbm = pl.BlockSpec(memory_space=pl.ANY)
    cube = (RING, RING, RING, ROWS)
    out_shape = (
        [pltpu.VMEM((ff, grad_out.shape[1]), F32)] * 3
        + [pltpu.VMEM((RING, 8, width), BF16)] * 2
        + [pltpu.VMEM((8, width), F32)]
    )
    dma = pltpu.SemaphoreType.DMA
    scratch = (
        [pltpu.SMEM(route_blocks.shape, jnp.int32)] * 2
        + [pltpu.VMEM(grad_out.shape, BF16)] * 2
        + [pltpu.VMEM(gain.shape, F32), pltpu.VMEM(w_router.shape, BF16)]
        + [pltpu.VMEM((RING, 1, QUARTER), F32)] * 2
        + [pltpu.VMEM((RING, 8, width), BF16), pltpu.VMEM((RING, 8, QUARTER), BF16)]
        + [pltpu.VMEM((5, 8, width), BF16), pltpu.VMEM((5, 8, QUARTER), BF16)]
        + [pltpu.VMEM((2, 8, QUARTER), F32), pltpu.VMEM((2, 8, width), BF16)]
        + [pltpu.VMEM((3, 2, 8, width), BF16)]
        + [pltpu.VMEM(cube + (w,), BF16) for w in WIDTHS]
        + [pltpu.VMEM(cube + (w,), BF16) for w in FEATS]
        + [pltpu.VMEM(cube + (w,), BF16) for w in WIDTHS]
        + [pltpu.VMEM((3, RING, RING, ROWS, w), BF16) for w in WIDTHS]
        + [pltpu.VMEM((RING, RING, ROWS, w), BF16) for w in WIDTHS]
        + [pltpu.VMEM((len(STEPS), ROWS, w), BF16) for w in WIDTHS]
        + [pltpu.VMEM((RING, 3, 8, width), BF16)]
        + [pltpu.VMEM((RING, 8, width), BF16)]
        + [pltpu.VMEM((3, RING, 8, width), F32)]
        + [pltpu.VMEM((5, rows, ff), F32)]
        + [pltpu.VMEM(wg.shape[1:], BF16)] * 3
        + [dma((2, 8)), dma((2, 4))]
        + [dma((2, 3, 2)), dma((2, 3, 2))]
        + [dma((3, 2)), dma((3, 2))]
        + [dma((3, 4)), dma((3, 4))]
        + [dma((4,)), dma((8,))]
        + [dma((3,)), dma((3,))]
        + [dma, dma]
        + [dma((13,)), pltpu.SemaphoreType.REGULAR]
    )
    return pl.pallas_call(
        step_kernel,
        out_shape=out_shape,
        in_specs=[hbm] * 9,
        out_specs=[vmem] * 6,
        scratch_shapes=scratch,
        compiler_params=pltpu.CompilerParams(
            collective_id=0, has_side_effects=True, vmem_limit_bytes=50 * 1024 * 1024
        ),
        name="routed_step",
    )(route_blocks, route_dest, saved, grad_out, gain, w_router, wg, wu, wd)


def finish_kernel(
    gate, up, down, grad_hbm, nb, fresh, stats, gain,
    out_inputs, out_gate, out_up, out_down, out_gain, out_router,
    grad_out, outcome, sem,
):
    load = pltpu.make_async_copy(grad_hbm, grad_out, sem.at[0])
    load.start()
    part = gate.shape[0] // PARTS
    copies = [
        pltpu.make_async_copy(
            src.at[pl.ds(j * part, part)], dst.at[0, pl.ds(j * part, part)],
            sem.at[2 + i * PARTS + j],
        )
        for i, (src, dst) in enumerate(((gate, out_gate), (up, out_up), (down, out_down)))
        for j in range(PARTS)
    ]
    for copy in copies:
        copy.start()
    for q in range(RING):
        cols = slice(q * QUARTER, (q + 1) * QUARTER)
        out_gain[:, cols] = stats[2 * q : 2 * q + 1, :QUARTER] / gain[:, cols]
        out_router[:, cols] = stats[2 * q + 1 : 2 * q + 2, :QUARTER] / gain[:, cols]
    low = lax.broadcasted_iota(jnp.int32, (2 * BLOCK, QUARTER), 0) < BLOCK
    half = jnp.where(lax.broadcasted_iota(jnp.int32, (2 * BLOCK, 1), 0) < BLOCK, 0.0, 1.0)
    load.wait()
    for q in range(RING):
        cols = slice(q * QUARTER, (q + 1) * QUARTER)
        patterns = []
        for ref in (nb, fresh):
            new_rows = ref[q, :, :QUARTER].astype(F32)
            turned = pltpu.roll(new_rows, BLOCK, 0)
            which = ref[q, :, QUARTER:].astype(F32)
            patterns.append((which[0:1, 0:1], jnp.where(low, new_rows, turned)))
            patterns.append((which[BLOCK : BLOCK + 1, 0:1], jnp.where(low, turned, new_rows)))
        for i in range(grad_out.shape[0] // 8):
            block = half + float(2 * i)
            value = grad_out[8 * i : 8 * i + 8, cols].astype(F32)
            for which, pattern in patterns:
                value = jnp.where(block == which, pattern, value)
            outcome[8 * i : 8 * i + 8, cols] = value.astype(BF16)
    store = pltpu.make_async_copy(outcome, out_inputs.at[0], sem.at[1])
    store.start()
    for copy in copies + [store]:
        copy.wait()


def finish(gate, up, down, grad_out, nb, fresh, stats, gain):
    tok_rows, model_dim = grad_out.shape
    ff = gate.shape[0]
    shape = jax.ShapeDtypeStruct
    vmem = pl.BlockSpec(memory_space=pltpu.VMEM)
    hbm = pl.BlockSpec(memory_space=pl.ANY)
    return pl.pallas_call(
        finish_kernel,
        out_shape=[shape((1, tok_rows, model_dim), BF16)]
        + [shape((1, ff, model_dim), F32)] * 3
        + [shape((1, model_dim), F32)] * 2,
        in_specs=[vmem] * 3 + [hbm] + [vmem] * 4,
        out_specs=[hbm] * 4 + [vmem] * 2,
        scratch_shapes=[pltpu.VMEM(grad_out.shape, BF16)] * 2
        + [pltpu.SemaphoreType.DMA((2 + 3 * PARTS,))],
        compiler_params=pltpu.CompilerParams(vmem_limit_bytes=8 * 1024 * 1024),
        name="finish",
    )(gate, up, down, grad_out, nb, fresh, stats, gain)


def on_device(saved, grad_out, route_blocks, route_dest, gain, w_router, w_gate, w_up, w_down):
    gate, up, down, nb, fresh, stats = communicate(
        route_blocks, route_dest, saved, grad_out, gain, w_router, w_gate, w_up, w_down
    )
    return tuple(finish(gate, up, down, grad_out, nb, fresh, stats, gain))


def solution(mesh):
    in_specs = (
        P("pipe", "ctx", None),
        P("ctx", None),
        P("pipe", "ctx", None),
        P("pipe", "ctx", None),
        P("pipe", None),
        P("pipe", None),
        P("pipe", "ctx", None),
        P("pipe", "ctx", None),
        P("pipe", "ctx", None),
    )
    out_specs = (
        P("pipe", "ctx", None),
        P("pipe", "ctx", None),
        P("pipe", "ctx", None),
        P("pipe", "ctx", None),
        P("pipe", None),
        P("pipe", None),
    )
    return jax.shard_map(
        on_device, mesh=mesh, in_specs=in_specs, out_specs=out_specs, check_vma=False
    )
```
